32 devices in a mesh: dp: 4 (over z), fsdp: 8 (over y, x, core).
Axes of the slice: x: 2, y: 2, z: 4, core: 2. Of those that a mesh axis runs over, the one named last changes fastest.
Arguments:
- tokens: bfloat16 [131072, 512], P(('dp', 'fsdp')), may hold values from -6 to 6
- cotangent: bfloat16 [131072, 512], P(('dp', 'fsdp')), may hold values from -6 to 6
- block_target: int32 [4096], P(('dp', 'fsdp')), may hold values from 0 to 1023, as said below
- sequence_lengths: int32 [32, 4], P(('dp', 'fsdp')), may hold values from 1 to 2048, 4096 in all within a row
- norm_gain: bfloat16 [512], P(('dp', 'fsdp')), may hold values from 0.5 to 1.5
- norm_shift: bfloat16 [512], P(('dp', 'fsdp')), may hold values from -3 to 3
- decay_real: bfloat16 [384], P(('dp', 'fsdp')), may hold values from -0.796875 to -0.19921875
- decay_rotation: bfloat16 [384], P(('dp', 'fsdp')), may hold values from -10 to 10
- log_timestep: bfloat16 [384], P(('dp', 'fsdp')), may hold values from -6.875 to -2.296875
- drive_matrix: bfloat16 [512, 768], P(('dp', 'fsdp')), may hold values from -1 to 1
- readout_matrix: bfloat16 [768, 512], P(('dp', 'fsdp')), may hold values from -0.3125 to 0.3125
- feedthrough: bfloat16 [512], P(('dp', 'fsdp')), may hold values from -3 to 3
- mixer_weight: bfloat16 [512, 1024], P(('dp', 'fsdp')), may hold values from -0.25 to 0.25
- mixer_bias: bfloat16 [1024], P(('dp', 'fsdp')), may hold values from -3 to 3
Outputs:
- layer_output: float32 [131072, 512], P(('dp', 'fsdp'))
- token_grad: float32 [131072, 512], P(('dp', 'fsdp'))
- gain_grad: float32 [512], P(('dp', 'fsdp'))
- shift_grad: float32 [512], P(('dp', 'fsdp'))
- real_grad: float32 [384], P(('dp', 'fsdp'))
- rotation_grad: float32 [384], P(('dp', 'fsdp'))
- timestep_grad: float32 [384], P(('dp', 'fsdp'))
- drive_grad: float32 [512, 768], P(('dp', 'fsdp'))
- readout_grad: float32 [768, 512], P(('dp', 'fsdp'))
- feedthrough_grad: float32 [512], P(('dp', 'fsdp'))
- weight_grad: float32 [512, 1024], P(('dp', 'fsdp'))
- bias_grad: float32 [1024], P(('dp', 'fsdp'))
The draws below stay inside these ranges and needn't reach their ends.
Inputs may be any that keep to these rules, and one draw needn't show every extreme that they name: Within each run of 1024 blocks (one group) the entries are a permutation of 0 to 1023, so every dealt device receives exactly 128 blocks; block b goes to dealt device block_target[b] // 128 of its group; one device sends 0, 16 or 32 of its blocks to any one device, and 32 to some device. `sequence_lengths`: each row sums to 4096.
All inputs are finite; a program needn't handle non-finite values.
Results may differ from the reference program's by a relative error of at most 0.019.
Values may be sent and summed in bfloat16 or wider, within the bound.
A program may use at most 320 MiB of HBM per device.

```python
import math
import jax
import jax.numpy as jnp
import numpy as np
from jax import lax

H = 512
P_SIZE = 384
TOK_DEV = 4096
BLK = 32
SEQ_DEV = 4
GROUPS = 4
GROUP_DEVS = 8
NB = 128
TOKENS = 131072
N_DP = 4
N_FSDP = 8


def group_targets(key):
    members = GROUP_DEVS
    portion = NB // members
    quarter = members // 4
    key_sign, key_rank, key_shuffle = jax.random.split(key, 3)
    shuffled = jax.random.permutation(key_sign, members)
    sign_pattern = jnp.where(shuffled < quarter, 1, jnp.where(shuffled < 2 * quarter, -1, 0)).astype(jnp.int32)
    positions = jnp.arange(members, dtype=jnp.int32)
    offsets = (positions[None, :] - positions[:, None]) % members
    counts = portion * (1 + sign_pattern[offsets])
    before = jnp.cumsum(counts, axis=0) - counts
    within = jnp.arange(2 * portion, dtype=jnp.int32)
    occupied = within[None, None, :] < counts[:, :, None]
    arrival_rank = before[:, :, None] + within[None, None, :]
    arrivals = jax.vmap(lambda subkey: jax.random.permutation(subkey, NB))(jax.random.split(key_rank, members)).astype(jnp.int32)
    target_device = jnp.broadcast_to(positions[None, :, None], arrival_rank.shape)
    placed = target_device * NB + arrivals[target_device, jnp.minimum(arrival_rank, NB - 1)]
    flat_occupied = occupied.reshape(members, -1)
    flat_placed = placed.reshape(members, -1)
    chosen = jnp.argsort(jnp.where(flat_occupied, 0, 1), axis=1, stable=True)[:, :NB]
    picked = jnp.take_along_axis(flat_placed, chosen, axis=1)
    shuffle = jax.vmap(lambda subkey: jax.random.permutation(subkey, NB))(jax.random.split(key_shuffle, members))
    return jnp.take_along_axis(picked, shuffle, axis=1).reshape(-1)


def draw_block_target(key, part):
    group_keys = jax.random.split(jax.random.fold_in(key, 7), GROUPS)
    return jax.vmap(group_targets)(group_keys).reshape(-1).astype(jnp.int32)


def shard_levels(key, extent, cuts, smallest, largest):
    def one(axis_at, shards_of):
        steps = jax.random.uniform(jax.random.fold_in(jax.random.fold_in(key, 6), axis_at), (shards_of,), jnp.float32, smallest / len(cuts), largest / len(cuts))
        return jnp.repeat(jnp.exp(steps), extent[axis_at] // shards_of).reshape((-1,) + (1,) * (len(extent) - axis_at - 1))

    loudness = one(*cuts[0])
    for cut in cuts[1:]:
        loudness = loudness * one(*cut)
    return loudness


def length_profile(number_of, total, most, skew):
    weights = [(1 << 20) // math.isqrt(standing ** skew) + 1 for standing in range(2, number_of + 1)]
    surplus, given = total - most - (number_of - 1), [1] * (number_of - 1)
    while surplus > 0:
        candidates = [i for i in range(number_of - 1) if given[i] < most]
        mass, remaining = sum([weights[i] for i in candidates]), surplus
        for i in candidates:
            addition = min(most - given[i], max(1, remaining * weights[i] // mass), surplus)
            given[i] = given[i] + addition
            surplus = surplus - addition
    return np.array([most] + given)


def ragged_sizes(key, count, total, limit, lean):
    if count == 2:
        one = jax.random.randint(key, (), max(1, total - limit), min(limit, total - 1) + 1)
        return jnp.stack([one, total - one])
    sizes = jnp.asarray(length_profile(count, total, limit, lean), jnp.int32)
    pairs = (count - 1) // 2
    giver, receiver = sizes[1:1 + 2 * pairs:2], sizes[2:2 + 2 * pairs:2]
    margin = jnp.minimum(giver - 1, limit - receiver)
    moved = jax.random.randint(jax.random.fold_in(key, 1), (pairs,), 0, 1 << 20) % (margin + 1)
    sizes = sizes.at[1:1 + 2 * pairs:2].set(giver - moved).at[2:2 + 2 * pairs:2].set(receiver + moved)
    return sizes[jax.random.permutation(jax.random.fold_in(key, 2), count)]


def centred(rng, extent, deviation, reach, cuts=(), kind=jnp.bfloat16):
    values = deviation * jax.random.normal(rng, extent, jnp.float32)
    if cuts:
        values = values * shard_levels(rng, extent, cuts, -0.22, 0.18)
    return jnp.clip(values, -reach, reach).astype(kind)


def setup_inputs(seed: int = 0) -> dict:
    streams_of = jax.random.split(jax.random.key(seed), 15)
    tokens = centred(streams_of[0], (TOKENS, H), 1.0, 6.0, ((0, 32),))
    cotangent = centred(streams_of[1], (TOKENS, H), 1.0, 6.0, ((0, 32),))
    block_target = draw_block_target(jax.random.fold_in(streams_of[14], 71), 0)
    sequence_lengths = jax.vmap(lambda own: ragged_sizes(own, SEQ_DEV, TOK_DEV, TOK_DEV // 2, 2))(jax.random.split(streams_of[3], (GROUPS * GROUP_DEVS))).reshape((GROUPS * GROUP_DEVS, SEQ_DEV)).astype(jnp.int32)
    norm_gain = jnp.clip(1.0 + 0.1 * jax.random.normal(streams_of[4], (H,), jnp.float32), 0.5, 1.5).astype(jnp.bfloat16)
    norm_shift = centred(streams_of[5], (H,), 0.5, 3.0, ((0, 32),))
    decay_real = jnp.clip(-0.796875 + 0.59765625 * jax.random.uniform(streams_of[6], (P_SIZE,), jnp.float32) ** shard_levels(streams_of[6], (P_SIZE,), ((0, 32),), -0.2, 0.2), -0.796875, -0.19921875).astype(jnp.bfloat16)
    decay_rotation = jnp.clip(jax.random.uniform(streams_of[7], (P_SIZE,), jnp.float32, -10.0, 10.0) * shard_levels(streams_of[7], (P_SIZE,), ((0, 32),), -0.4, 0.0), -10.0, 10.0).astype(jnp.bfloat16)
    log_timestep = jnp.clip(-6.875 + 4.578125 * jax.random.uniform(streams_of[8], (P_SIZE,), jnp.float32) ** shard_levels(streams_of[8], (P_SIZE,), ((0, 32),), -0.2, 0.2), -6.875, -2.296875).astype(jnp.bfloat16)
    drive_matrix = centred(streams_of[9], (H, 2 * P_SIZE), (H // 16) ** -0.5, 1.0, ((0, 32),))
    readout_matrix = centred(streams_of[10], (2 * P_SIZE, H), P_SIZE ** -0.5, 0.3125, ((0, 32),))
    feedthrough = centred(streams_of[11], (H,), 0.5, 3.0, ((0, 32),))
    mixer_weight = centred(streams_of[12], (H, 2 * H), H ** -0.5, 0.25, ((0, 32),))
    mixer_bias = centred(streams_of[13], (2 * H,), 0.5, 3.0, ((0, 32),))
    return {"tokens": tokens, "cotangent": cotangent, "block_target": block_target, "sequence_lengths": sequence_lengths, "norm_gain": norm_gain, "norm_shift": norm_shift, "decay_real": decay_real, "decay_rotation": decay_rotation, "log_timestep": log_timestep, "drive_matrix": drive_matrix, "readout_matrix": readout_matrix, "feedthrough": feedthrough, "mixer_weight": mixer_weight, "mixer_bias": mixer_bias}


@jax.custom_vjp
def low(v):
    return lax.optimization_barrier(v.astype(jnp.bfloat16)).astype(jnp.float32)

@jax.custom_vjp
def low_back(v):
    return v

def low_keep(v):
    return (low(v), None)

def low_pass(kept, grad):
    return (grad,)

def back_keep(v):
    return (v, None)

def back_low(kept, grad):
    return (low(grad),)
low.defvjp(low_keep, low_pass)
low_back.defvjp(back_keep, back_low)
EPSILON = 1e-05
HIGHEST = lax.Precision.HIGHEST

def combine(earlier, later):
    return (later[0] * earlier[0] - later[1] * earlier[1], later[0] * earlier[1] + later[1] * earlier[0], later[0] * earlier[2] - later[1] * earlier[3] + later[2], later[0] * earlier[3] + later[1] * earlier[2] + later[3])

def run_scan(keeping, factor_real, factor_quad, driven):
    states = factor_real.shape[0]
    rate_real = keeping[:, None] * factor_real[None, :]
    rate_quad = keeping[:, None] * factor_quad[None, :]
    swept = lax.associative_scan(combine, (rate_real, rate_quad, driven[:, :states], driven[:, states:]), axis=0)
    return jnp.concatenate([swept[2], -swept[3]], axis=-1)

def discretize(decay_real, decay_rotation, log_timestep, drive_matrix):
    states = decay_real.shape[0]
    timestep = jnp.exp(log_timestep)
    magnitude = jnp.exp(decay_real * timestep)
    turned = decay_rotation * timestep
    factor_real = magnitude * jnp.cos(turned)
    factor_quad = magnitude * jnp.sin(turned)
    modulus = decay_real * decay_real + decay_rotation * decay_rotation
    scale_real = ((factor_real - 1.0) * decay_real + factor_quad * decay_rotation) / modulus
    scale_quad = (factor_quad * decay_real - (factor_real - 1.0) * decay_rotation) / modulus
    drive_real = drive_matrix[:, :states]
    drive_quad = drive_matrix[:, states:]
    drive_bar = jnp.concatenate([scale_real * drive_real - scale_quad * drive_quad, scale_real * drive_quad + scale_quad * drive_real], axis=-1)
    return (factor_real, factor_quad, drive_bar)

def normalize(values, norm_gain, norm_shift):
    center = lax.optimization_barrier(jnp.mean(values, axis=-1, keepdims=True))
    spread = lax.optimization_barrier(jnp.mean((values - center) ** 2, axis=-1, keepdims=True))
    return (values - center) * lax.rsqrt(spread + EPSILON) * norm_gain + norm_shift

def reference(tokens, cotangent, block_target, sequence_lengths, norm_gain, norm_shift, decay_real, decay_rotation, log_timestep, drive_matrix, readout_matrix, feedthrough, mixer_weight, mixer_bias):
    devices = N_DP * N_FSDP
    group_blocks = TOK_DEV // BLK * N_FSDP
    total_blocks = block_target.shape[0]
    width = tokens.shape[1]
    group_index = jnp.arange(total_blocks, dtype=jnp.int32) // group_blocks
    dealt_index = (group_index * group_blocks + block_target).astype(jnp.int32)
    given_index = jnp.zeros((total_blocks,), jnp.int32).at[dealt_index].set(jnp.arange(total_blocks, dtype=jnp.int32))
    starts = jnp.cumsum(sequence_lengths, axis=1) - sequence_lengths
    row_ids = jnp.arange(TOK_DEV, dtype=jnp.int32)
    keeping = 1.0 - jnp.any(row_ids[None, :, None] == starts[:, None, :], axis=2).astype(jnp.float32)
    scan_block = jax.checkpoint(run_scan)

    def forward(rows, gain, shift, rate_real, rate_rotation, timestep_log, drive, readout, through, weight, bias):
        normed = low_back(low(normalize(rows, gain, shift)))
        factor_real, factor_quad, drive_bar = discretize(rate_real, rate_rotation, timestep_log, drive)
        drive_low = low(drive_bar)
        dealt = normed.reshape(total_blocks, BLK, width)[given_index].reshape(devices, TOK_DEV, width)
        driven = low_back(jnp.einsum('dth,hp->dtp', dealt, drive_low, precision=HIGHEST))
        scanned = lax.map(lambda pieces: scan_block(pieces[0], factor_real, factor_quad, pieces[1]), (keeping, driven))
        joined = low(scanned)
        mixed = low_back(jnp.einsum('dtp,ph->dth', joined, readout, precision=HIGHEST) + through * dealt)
        activated = low_back(low(jax.nn.gelu(mixed, approximate=False)))
        features = activated.reshape(total_blocks, BLK, width)[dealt_index].reshape(-1, width)
        hidden = low_back(jnp.dot(features, weight, precision=HIGHEST, preferred_element_type=jnp.float32) + bias)
        return rows + hidden[:, :width] * jax.nn.sigmoid(hidden[:, width:])
    inputs = (tokens.astype(jnp.float32), norm_gain.astype(jnp.float32), norm_shift.astype(jnp.float32), decay_real.astype(jnp.float32), decay_rotation.astype(jnp.float32), log_timestep.astype(jnp.float32), drive_matrix.astype(jnp.float32), readout_matrix.astype(jnp.float32), feedthrough.astype(jnp.float32), mixer_weight.astype(jnp.float32), mixer_bias.astype(jnp.float32))
    output, pullback = jax.vjp(forward, *inputs)
    grads = pullback(cotangent.astype(jnp.float32))
    return (output, grads[0], grads[1], grads[2], grads[3], grads[4], grads[5], grads[6], grads[7], grads[8], grads[9], grads[10])
```

```python
import functools
import itertools

import jax
import jax.numpy as jnp
from jax import lax
from jax.experimental import pallas as pl
from jax.experimental.pallas import tpu as pltpu
from jax.sharding import PartitionSpec as P

EPSILON = 1e-05
AXES = ("dp", "fsdp")
F32 = jnp.float32
BF16 = jnp.bfloat16
LANES = 128
SUB = 8
VMEM_LIMIT = 60 * 1024 * 1024


def dot(left, right):
    return jnp.dot(left, right, preferred_element_type=F32)


def contract_rows(left, right):
    return lax.dot_general(left, right, (((0,), (0,)), ((), ())), preferred_element_type=F32)


def contract_cols(left, right):
    return lax.dot_general(left, right, (((1,), (1,)), ((), ())), preferred_element_type=F32)


def lanes_to(mask, width):
    return jnp.concatenate([mask] * (width // LANES), axis=1)


def spread(vector, rows):
    return jnp.broadcast_to(vector, (rows, vector.shape[1]))


def erfc_abs(magnitude):
    t = 1.0 / (1.0 + 0.5 * magnitude)
    series = t * 0.17087277 - 0.82215223
    for term in (1.48851587, -1.13520398, 0.27886807, -0.18628806, 0.09678418, 0.37409196, 1.00002368):
        series = series * t + term
    return t * jnp.exp(series * t - 1.26551223 - magnitude * magnitude)


def gelu_parts(v):
    complement = 0.5 * erfc_abs(jnp.abs(v) * 0.7071067811865476)
    cdf = jnp.where(v < 0.0, complement, 1.0 - complement)
    density = 0.3989422804014327 * jnp.exp(-0.5 * v * v)
    return v * cdf, cdf + v * density


def permute_tile(perm, tile, span):
    return jnp.concatenate(
        [dot(perm, tile[i * span : (i + 1) * span]) for i in range(tile.shape[0] // span)], axis=0
    )


def norm_stats(rows):
    center = jnp.mean(rows, axis=-1, keepdims=True)
    moved = rows - center
    spread_of = jnp.mean(moved * moved, axis=-1, keepdims=True)
    return moved, lax.rsqrt(spread_of + EPSILON)


MESH = pl.DeviceIdType.MESH


class Grid:
    def __init__(self, sizes):
        self.dp, members = sizes
        self.bits = members.bit_length() - 1
        self.shape = (self.dp,) + (2,) * self.bits

    def here(self):
        row, column = lax.axis_index("dp"), lax.axis_index("fsdp")
        mine = [row] + [lax.rem(lax.div(column, 2**bit), 2) for bit in reversed(range(self.bits))]
        return row, column, mine

    def peers(self, dim):
        row, column, mine = self.here()
        if dim == 0:
            return [
                (away - 1, {"dp": lax.rem(row + away, self.dp)}, lax.rem(row + away, self.dp))
                for away in range(1, self.dp)
            ]
        step = 2 ** (self.bits - dim)
        return [(0, {"fsdp": column + step * (1 - 2 * mine[dim])}, 1 - mine[dim])]

    def orders(self, dims, last):
        return [tuple(dims[i:] + dims[:i]) + last for i in range(len(dims))]


def greet(grid):
    barrier = pltpu.get_barrier_semaphore()
    row, column, _ = grid.here()
    members = 2**grid.bits
    for away in range(1, grid.dp):
        pl.semaphore_signal(
            barrier, inc=1, device_id={"dp": lax.rem(row + away, grid.dp)}, device_id_type=MESH
        )
    for away in range(1, members):
        pl.semaphore_signal(
            barrier, inc=1, device_id={"fsdp": lax.rem(column + away, members)}, device_id_type=MESH
        )
    pl.semaphore_wait(barrier, grid.dp + members - 2)


def remote(source, target, send, recv, device):
    return pltpu.make_async_remote_copy(
        src_ref=source, dst_ref=target, send_sem=send, recv_sem=recv, device_id=device, device_id_type=MESH
    )


def gather_phase(grid, ref, axes, dim, done, send, recv, base):
    _, _, mine = grid.here()
    at = tuple(slice(None) if d in done else mine[d] for d in axes)
    return [
        pltpu.make_async_remote_copy(
            src_ref=ref.at[at], dst_ref=ref.at[at], send_sem=send.at[base + slot], recv_sem=recv.at[base + slot],
            device_id=device, device_id_type=MESH,
        )
        for slot, device, _ in grid.peers(dim)
    ]


def reduce_plan(grid, order):
    plan = []
    for phase, dim in enumerate(order):
        done = order[:phase]
        left = tuple(d for d in range(grid.bits + 1) if d not in done and d != dim)
        plan.append((dim, done, left))
    return plan


def lane_index(width):
    return lax.broadcasted_iota(jnp.int32, (1, width), 1).astype(F32)


def unpack(rows, row, count, width):
    lanes = lane_index(width)
    owner = jnp.floor((lanes + 0.5) * (1.0 / count))
    inner = lanes - count * owner
    taken = lax.broadcasted_iota(jnp.int32, (LANES, width), 0).astype(F32) == inner
    spread_out = dot(rows.astype(BF16), jnp.where(taken, 1.0, 0.0).astype(BF16))
    index = lax.broadcasted_iota(jnp.int32, (rows.shape[0], width), 0).astype(F32)
    return jnp.sum(jnp.where(index == owner * SUB + row, spread_out, 0.0), axis=0, keepdims=True)


def rates_of(real, rotation, step_log):
    timestep = jnp.exp(step_log)
    magnitude = jnp.exp(real * timestep)
    turned = rotation * timestep
    factor_re = magnitude * jnp.cos(turned)
    factor_im = magnitude * jnp.sin(turned)
    modulus = real * real + rotation * rotation
    scale_re = ((factor_re - 1.0) * real + factor_im * rotation) / modulus
    scale_im = (factor_im * real - (factor_re - 1.0) * rotation) / modulus
    return timestep, factor_re, factor_im, modulus, scale_re, scale_im


def cross_blocks(members, reverse, pieces, place, own_place, broken, flow_re, flow_im, dealt, carries):
    states = flow_re.shape[1]
    total = place.shape[1]
    steps = total // members
    rows = lax.broadcasted_iota(jnp.int32, (total, total), 0).astype(F32)
    chosen = jnp.where(rows == place[...], 1.0, 0.0).astype(BF16)
    dealt[...] = dot(chosen, pieces[...].reshape(total, 2 * states))
    rate_re = spread(flow_re, members)
    rate_im = spread(-flow_im if reverse else flow_im, members)
    marks = [broken[s] for s in range(broken.shape[0])]

    def step(i, state):
        re, im = state
        p = steps - 1 - i if reverse else i
        at = pl.multiple_of(p * members, members)
        here = dealt[pl.ds(at, members), :]
        met = marks[0] == p
        for mark in marks[1:]:
            met = met | (mark == p)
        mask = lanes_to(jnp.where(met, 0.0, 1.0), states)
        dealt[pl.ds(at, members), :] = jnp.concatenate([re, im], axis=1)
        return (
            mask * (rate_re * re - rate_im * im) + here[:, :states],
            mask * (rate_re * im + rate_im * re) + here[:, states:],
        )

    zero = jnp.zeros((members, states), F32)
    lax.fori_loop(0, steps, step, (zero, zero), unroll=4)
    own = own_place.shape[0]
    columns = lax.broadcasted_iota(jnp.int32, (own, total), 1).astype(F32)
    taken = jnp.where(columns == lanes_to(own_place[...], total), 1.0, 0.0).astype(BF16)
    high = dealt[...].astype(BF16)
    low = (dealt[...] - high.astype(F32)).astype(BF16)
    carries[...] = dot(taken, high) + dot(taken, low)


def front_kernel(
    grid, block_rows, counts, tokens, gain_s, shift_s, through_s, bias_s, real_s, rotation_s, step_s, target_s,
    lengths_s, drive_s, readout_s, mixer_s, perm,
    dealt, driven, keep, carries, drive, drive_raw, readout_w, mixer_w, vectors, rates, place, own_place, broken,
    xhat, table, drive_w, bits, pieces, dealt_ends, send, recv, local, push_send, push_recv,
):
    i = pl.program_id(0)
    tiles = (pl.num_programs(0) - 1) // 2
    row, column, mine = grid.here()
    members = 2**grid.bits
    blocks = target_s.shape[0]
    tile = tokens.shape[0]
    width = tokens.shape[1]
    both = drive.shape[1]
    states = both // 2
    span = SUB * block_rows
    chains = tile // span
    tile_blocks = tile // block_rows
    axes = tuple(range(grid.bits + 1))
    wholes = (table, drive_w, readout_w, mixer_w)
    dims = list(range(grid.bits))
    orders = grid.orders(dims, (grid.bits,))
    orders = [orders[0], orders[0], orders[1 % len(orders)], orders[2 % len(orders)]]
    slots = grid.dp - 1 + grid.bits
    phases = grid.bits + 1

    def phase_copies(k, phase):
        order = orders[k]
        base = k * slots + sum(len(grid.peers(d)) for d in order[:phase])
        return gather_phase(grid, wholes[k], axes, order[phase], order[:phase], send, recv, base)

    def advance(ks, phase):
        for k in ks:
            if phase:
                for copy in phase_copies(k, phase - 1):
                    copy.wait()
            if phase < phases:
                for copy in phase_copies(k, phase):
                    copy.start()

    @pl.when(i == 0)
    def _():
        copies = [
            pltpu.make_async_copy(shard, ref.at[tuple(mine)], local.at[k])
            for k, (shard, ref) in enumerate(zip((drive_s, readout_s, mixer_s), wholes[1:]))
        ]
        for copy in copies:
            copy.start()
        held = [gain_s, shift_s, through_s, bias_s, real_s, rotation_s, step_s, target_s]
        own = table.at[tuple(mine)]
        own[...] = jnp.zeros_like(own)
        for k, ref in enumerate(held):
            own[k : k + 1, : ref.shape[0]] = ref[...].astype(F32).reshape(1, ref.shape[0])
        sequences = lengths_s.shape[1]
        own[4:5, LANES // 2 : LANES // 2 + sequences] = lengths_s[...].astype(F32)
        greet(grid)
        for copy in copies:
            copy.wait()
        advance((0, 1, 2, 3), 0)

    for phase in range(1, phases):
        @pl.when(i == min(2 * phase, tiles))
        def _():
            advance((0, 1), phase)

        @pl.when(i == min(4 * phase - 1, 2 * tiles - 2))
        def _():
            advance((2, 3), phase)

    @pl.when(i < tiles)
    def _():
        moved, rstd = norm_stats(tokens[...].astype(F32))
        xhat[pl.ds(pl.multiple_of(i * tile, tile), tile), :] = moved * rstd

    @pl.when(i == tiles)
    def _():
        advance((0, 1), phases)
        rows = table[...].reshape(-1, LANES)
        vectors[...] = jnp.zeros_like(vectors)
        for k, size in enumerate((width, width, width, 2 * width)):
            vectors[k : k + 1, :size] = unpack(rows, k, counts[k], size)
        real, rotation, step_log = [unpack(rows, k, counts[k], states) for k in (4, 5, 6)]
        _, factor_re, factor_im, _, scale_re, scale_im = rates_of(real, rotation, step_log)
        flow_re, flow_im = factor_re, factor_im
        power = 1
        while power < block_rows:
            flow_re, flow_im = flow_re * flow_re - flow_im * flow_im, 2.0 * flow_re * flow_im
            power *= 2
        for k, value in enumerate((factor_re, factor_im, flow_re, flow_im, real, rotation, step_log)):
            rates[k : k + 1, :] = value
        drive_raw[...] = drive_w[...].reshape(width, both)
        raw = drive_raw[...].astype(F32)
        drive[:, :states] = (scale_re * raw[:, :states] - scale_im * raw[:, states:]).astype(BF16)
        drive[:, states:] = (scale_re * raw[:, states:] + scale_im * raw[:, :states]).astype(BF16)
        group = table[row].reshape(members * SUB, LANES)
        for m in range(members):
            q = group[m * SUB + 7 : m * SUB + 8, :blocks]
            d = jnp.floor(q * (1.0 / blocks))
            place[:, m * blocks : (m + 1) * blocks] = (q - d * blocks) * members + d
        lengths = jnp.concatenate([group[m * SUB + 4 : m * SUB + 5, :] for m in range(members)], axis=0)
        sequences = lengths_s.shape[1]
        q = table[tuple(mine) + (slice(7, 8), slice(None))]
        diagonal = lax.broadcasted_iota(jnp.int32, (blocks, LANES), 0) == lax.broadcasted_iota(
            jnp.int32, (blocks, LANES), 1
        )
        q = jnp.sum(jnp.where(diagonal, jnp.broadcast_to(q, (blocks, LANES)), 0.0), axis=1, keepdims=True)
        q = jnp.broadcast_to(q, (blocks, LANES))
        d = jnp.floor(q * (1.0 / blocks))
        p = q - d * blocks
        own_place[...] = p * members + d
        start = jnp.zeros((members, LANES), F32)
        marks = jnp.zeros((blocks, LANES), jnp.int32)
        for s in range(sequences):
            broken[s] = jnp.floor(start * (1.0 / block_rows)).astype(jnp.int32)
            mark = jnp.zeros((blocks, LANES), F32)
            for m in range(members):
                mark = jnp.where(d == float(m), jnp.broadcast_to(start[m : m + 1, :], (blocks, LANES)), mark)
            mark = mark - p * block_rows
            inside = (mark >= 0.0) & (mark < block_rows)
            shift = jnp.where(inside, mark, 0.0).astype(jnp.int32)
            marks = marks | jnp.where(inside, lax.shift_left(jnp.ones_like(shift), shift), 0)
            column_of = lengths[:, LANES // 2 + s : LANES // 2 + s + 1]
            start = start + jnp.broadcast_to(column_of, (members, LANES))
        bits[...] = marks

    def pushes(j):
        at = (column, pl.ds(pl.multiple_of(j * tile_blocks, tile_blocks), tile_blocks))
        return push_to(at)

    def push_to(at):
        far = [
            remote(
                pieces.at[at], pieces.at[at], push_send.at[away // 2], push_recv.at[away // 2],
                {"fsdp": lax.rem(column + away, members)},
            )
            for away in range(2, members, 2)
        ]
        near = remote(pieces.at[at], pieces.at[at], push_send.at[0], push_recv.at[0], {"fsdp": sibling})
        return far + [near]

    sibling = column + 1 - 2 * mine[-1]

    @pl.when((i >= tiles) & (i < 2 * tiles))
    def _():
        j = i - tiles
        gain = vectors[0:1, :width]
        shift = vectors[1:2, :width]
        normed = xhat[pl.ds(pl.multiple_of(j * tile, tile), tile), :] * gain + shift
        dealt[...] = permute_tile(perm[...], normed.astype(BF16), span).astype(BF16)
        driven[...] = dot(dealt[...], drive[...])
        rate_re = spread(rates[0:1, :], SUB)
        rate_im = spread(rates[1:2, :], SUB)
        first = pl.multiple_of(j * tile_blocks, tile_blocks)
        mark = bits[pl.ds(first, tile_blocks), :]
        state = [(jnp.zeros((SUB, states), F32), jnp.zeros((SUB, states), F32)) for _ in range(chains)]
        for t in range(block_rows):
            single = 1 << t if t < 31 else -(1 << 31)
            for c in range(chains):
                at = c * span + t * SUB
                narrow = jnp.where((mark[c * SUB : (c + 1) * SUB] & single) == 0, 1.0, 0.0)
                keep[at : at + SUB, :] = narrow
                mask = lanes_to(narrow, states)
                re, im = state[c]
                now_re = mask * (rate_re * re - rate_im * im) + driven[at : at + SUB, :states]
                now_im = mask * (rate_re * im + rate_im * re) + driven[at : at + SUB, states:]
                state[c] = (now_re, now_im)
        ends = jnp.concatenate([jnp.concatenate(state[c], axis=1) for c in range(chains)], axis=0)
        pieces[column, pl.ds(first, tile_blocks), :] = ends.astype(BF16)
        for copy in pushes(j):
            copy.start()

    @pl.when(i == 2 * tiles)
    def _():
        onward = []
        for k, copy in enumerate(push_to((column,))[:-1]):
            copy.wait()
            from_there = lax.rem(column + members - 2 * (k + 1), members)
            slot = members // 2 + k
            onward.append(
                remote(
                    pieces.at[from_there], pieces.at[from_there], push_send.at[slot], push_recv.at[slot],
                    {"fsdp": sibling},
                )
            )
            onward[-1].start()
        push_to((column,))[-1].wait()
        for copy in onward:
            copy.wait()
        cross_blocks(
            members, False, pieces, place, own_place, broken, rates[2:3, :], rates[3:4, :], dealt_ends, carries
        )
        advance((2, 3), phases)


def main_kernel(
    grid, block_rows, cotangent, dealt, driven, carry, keep, rates, readout, vectors, mixer, perm, back, place,
    own_place, broken,
    gated_low, mixed_low, joined, joined_grad, weight_grad, bias_grad, through_grad, readout_grad, coming,
    pieces, dealt_heads, push_send, push_recv,
):
    i = pl.program_id(0)
    tiles = pl.num_programs(0) - 1
    _, column, _ = grid.here()
    members = 2**grid.bits
    span = SUB * block_rows
    tile, width = cotangent.shape
    states = rates.shape[1]
    chains = tile // span
    tile_blocks = tile // block_rows

    def push_to(at):
        return [
            remote(
                pieces.at[at], pieces.at[at], push_send.at[away - 1], push_recv.at[away - 1],
                {"fsdp": lax.rem(column + away, members)},
            )
            for away in range(1, members)
        ]

    @pl.when(i == 0)
    def _():
        weight_grad[...] = jnp.zeros_like(weight_grad)
        bias_grad[...] = jnp.zeros_like(bias_grad)
        through_grad[...] = jnp.zeros_like(through_grad)
        readout_grad[...] = jnp.zeros_like(readout_grad)
        greet(grid)

    @pl.when(i < tiles)
    def _():
        through = vectors[2:3, :width]
        bias = vectors[3:4, : 2 * width]
        rate_re = spread(rates[0:1, :], SUB)
        rate_im = spread(rates[1:2, :], SUB)
        state = [
            (carry[c * SUB : (c + 1) * SUB, :states], carry[c * SUB : (c + 1) * SUB, states:])
            for c in range(chains)
        ]
        for t in range(0, block_rows, 2):
            for c in range(chains):
                held = []
                for step in (t, t + 1):
                    at = c * span + step * SUB
                    mask = lanes_to(keep[at : at + SUB, :], states)
                    re, im = state[c]
                    now_re = mask * (rate_re * re - rate_im * im) + driven[at : at + SUB, :states]
                    now_im = mask * (rate_re * im + rate_im * re) + driven[at : at + SUB, states:]
                    state[c] = (now_re, now_im)
                    held.append(state[c])
                at = c * span + t * SUB
                joined[at : at + 2 * SUB, :states] = jnp.concatenate([held[0][0], held[1][0]], axis=0).astype(BF16)
                joined[at : at + 2 * SUB, states:] = (-jnp.concatenate([held[0][1], held[1][1]], axis=0)).astype(BF16)

        dealt_f32 = dealt[...].astype(F32)
        mixed = dot(joined[...], readout[...]) + through * dealt_f32
        activated, slope = gelu_parts(mixed)
        features = permute_tile(back[...], activated.astype(BF16), span).astype(BF16)
        hidden = dot(features, mixer[...]) + bias
        value = hidden[:, :width]
        sig = 1.0 / (1.0 + jnp.exp(-hidden[:, width:]))
        gated_low[...] = (value * sig).astype(BF16)
        cot_sig = cotangent[...].astype(F32) * sig
        hidden_low = jnp.concatenate(
            [cot_sig.astype(BF16), (cot_sig * value * (1.0 - sig)).astype(BF16)], axis=1
        )
        weight_grad[...] += contract_rows(features, hidden_low)
        bias_grad[...] += jnp.sum(hidden_low.astype(F32), axis=0, keepdims=True)
        feature_grad = contract_cols(hidden_low, mixer[...]).astype(BF16)
        mixed_grad = (permute_tile(perm[...], feature_grad, span) * slope).astype(BF16)
        mixed_low[...] = mixed_grad
        through_grad[...] += jnp.sum(mixed_grad.astype(F32) * dealt_f32, axis=0, keepdims=True)
        readout_grad[...] += contract_rows(joined[...], mixed_grad)
        joined_grad[...] = contract_cols(mixed_grad, readout[...])

        going = [(jnp.zeros((SUB, states), F32), jnp.zeros((SUB, states), F32)) for _ in range(chains)]
        for t in reversed(range(block_rows)):
            for c in range(chains):
                at = c * span + t * SUB
                mask = lanes_to(keep[at : at + SUB, :], states)
                re = joined_grad[at : at + SUB, :states] + going[c][0]
                im = going[c][1] - joined_grad[at : at + SUB, states:]
                going[c] = (mask * (rate_re * re + rate_im * im), mask * (rate_re * im - rate_im * re))
        heads = jnp.concatenate([jnp.concatenate(going[c], axis=1) for c in range(chains)], axis=0)
        at = (column, pl.ds(pl.multiple_of(i * tile_blocks, tile_blocks), tile_blocks))
        pieces[at + (slice(None),)] = heads.astype(BF16)
        for copy in push_to(at):
            copy.start()

    @pl.when(i == tiles)
    def _():
        for copy in push_to((column,)):
            copy.wait()
        cross_blocks(
            members, True, pieces, place, own_place, broken, rates[2:3, :], rates[3:4, :], dealt_heads, coming
        )


def last_kernel(
    grid, block_rows, orders, dealt, joined, joined_grad, carry, coming, keep, mixed_low, tokens, rates, vectors, drive,
    drive_raw, back, readout_grad, weight_grad, bias_grad, through_grad,
    given_low, drive_sum, readout_sum, weight_sum, vector_sum,
    driven_all, drive_grad, drive_parts, decay_cot, gain_grad, shift_grad, *rest,
):
    i = pl.program_id(0)
    tiles = (pl.num_programs(0) - 1) // 2
    row, column, mine = grid.here()
    members = 2**grid.bits
    core = grid.bits
    phases = grid.bits + 1
    span = SUB * block_rows
    tile, width = tokens.shape
    both = joined.shape[1]
    states = both // 2
    chains = tile // span
    rest = list(rest)
    parts = (readout_grad, weight_grad, drive_parts)
    outs = (readout_sum, weight_sum, drive_sum)
    count = len(parts)
    accs = [rest.pop(0) for _ in range(count)]
    stages = [[rest.pop(0) for _ in range(phases)] for _ in range(count)]
    landed = [[rest.pop(0) for _ in range(phases)] for _ in range(count)]
    vector_stage, across, along, send, recv, vector_send, vector_recv = rest
    plans = [reduce_plan(grid, order) for order in orders]
    slots = grid.dp - 1 + grid.bits
    every = tuple(range(grid.bits + 1))
    kept = every[:-1]

    def combos(left):
        return list(itertools.product(*[range(grid.shape[d]) for d in left]))

    def at(dim, index, left, combo, dims):
        chosen = dict(zip(left, combo))
        chosen[dim] = index
        return tuple(chosen[d] if d in chosen else mine[d] for d in dims)

    def hops(k, phase):
        dim = plans[k][phase][0]
        base = k * slots + sum(len(grid.peers(d)) for d in orders[k][:phase])
        return [
            (
                remote(
                    stages[k][phase].at[slot], landed[k][phase].at[slot], send.at[base + slot], recv.at[base + slot],
                    device,
                ),
                slot,
                index,
            )
            for slot, device, index in grid.peers(dim)
        ]

    def begin(k, phase):
        dim, _, left = plans[k][phase]
        for copy, slot, index in hops(k, phase):
            for combo in combos(left):
                if dim == core:
                    piece = parts[k][at(dim, index, left, combo, every)]
                else:
                    piece = accs[k][at(dim, index, left, combo, kept)]
                stages[k][phase][(slot,) + combo] = piece.astype(BF16)
            copy.start()

    def finish(k, phase):
        dim, _, left = plans[k][phase]
        copies = hops(k, phase)
        for copy, _, _ in copies:
            copy.wait()
        for combo in combos(left):
            if dim == core:
                piece = parts[k][at(dim, mine[dim], left, combo, every)]
            else:
                piece = accs[k][at(dim, mine[dim], left, combo, kept)]
            for _, slot, _ in copies:
                piece = piece + landed[k][phase][(slot,) + combo].astype(F32)
            accs[k][at(dim, mine[dim], left, combo, kept)] = piece

    def advance(ks, phase):
        for k in ks:
            if phase:
                finish(k, phase - 1)
            if phase < phases:
                begin(k, phase)
            else:
                outs[k][...] = accs[k][tuple(mine[:-1])]

    rate_re = spread(rates[0:1, :], SUB)
    rate_im = spread(rates[1:2, :], SUB)

    @pl.when(i == 0)
    def _():
        drive_grad[...] = jnp.zeros_like(drive_grad)
        decay_cot[...] = jnp.zeros_like(decay_cot)
        gain_grad[...] = jnp.zeros_like(gain_grad)
        shift_grad[...] = jnp.zeros_like(shift_grad)
        greet(grid)
        advance((0, 1), 0)

    for phase in range(1, phases + 1):
        @pl.when(i == min(2 * phase, 2 * tiles - 1))
        def _():
            advance((0, 1), phase)

    @pl.when(i < tiles)
    def _():
        driven_low = driven_all.at[pl.ds(pl.multiple_of(i * tile, tile), tile)]
        going = [
            (coming[c * SUB : (c + 1) * SUB, :states], coming[c * SUB : (c + 1) * SUB, states:])
            for c in range(chains)
        ]
        total = [(jnp.zeros((SUB, states), F32), jnp.zeros((SUB, states), F32)) for _ in range(chains)]
        for t in reversed(range(0, block_rows, 2)):
            for c in range(chains):
                pair = c * span + t * SUB
                here_re = joined[pair : pair + SUB, :states].astype(F32)
                here_im = -joined[pair : pair + SUB, states:].astype(F32)
                if t == 0:
                    past_re = carry[c * SUB : (c + 1) * SUB, :states]
                    past_im = carry[c * SUB : (c + 1) * SUB, states:]
                else:
                    past_re = joined[pair - SUB : pair, :states].astype(F32)
                    past_im = -joined[pair - SUB : pair, states:].astype(F32)
                held = {}
                for step, (prev_re, prev_im) in ((t + 1, (here_re, here_im)), (t, (past_re, past_im))):
                    where = c * span + step * SUB
                    mask = lanes_to(keep[where : where + SUB, :], states)
                    re = joined_grad[where : where + SUB, :states] + going[c][0]
                    im = going[c][1] - joined_grad[where : where + SUB, states:]
                    held[step] = (re, im)
                    on_re = mask * (rate_re * re + rate_im * im)
                    on_im = mask * (rate_re * im - rate_im * re)
                    going[c] = (on_re, on_im)
                    total[c] = (
                        total[c][0] + (on_re * prev_re + on_im * prev_im),
                        total[c][1] + (on_im * prev_re - on_re * prev_im),
                    )
                driven_low[pair : pair + 2 * SUB, :states] = jnp.concatenate(
                    [held[t][0], held[t + 1][0]], axis=0
                ).astype(BF16)
                driven_low[pair : pair + 2 * SUB, states:] = jnp.concatenate(
                    [held[t][1], held[t + 1][1]], axis=0
                ).astype(BF16)
        for c in range(chains):
            decay_cot[...] += jnp.concatenate(total[c], axis=1)
        drive_grad[...] += contract_rows(dealt[...], driven_low[...])

    @pl.when(i == tiles)
    def _():
        shard = drive_parts.shape[-2]
        for s, place in enumerate(itertools.product(*[range(size) for size in grid.shape])):
            drive_parts[place] = drive_grad[s * shard : (s + 1) * shard, :]
        advance((2,), 0)

    for phase in range(1, phases):
        @pl.when(i == min(tiles + 2 * phase, 2 * tiles))
        def _():
            advance((2,), phase)

    @pl.when((i >= tiles) & (i < 2 * tiles))
    def _():
        j = i - tiles
        driven_low = driven_all[pl.ds(pl.multiple_of(j * tile, tile), tile), :]
        normed_grad = vectors[2:3, :width] * mixed_low[...].astype(F32) + contract_cols(driven_low, drive[...])
        given = permute_tile(back[...], normed_grad.astype(BF16), span)
        given_low[...] = given.astype(BF16)
        moved, rstd = norm_stats(tokens[...].astype(F32))
        gain_grad[...] += jnp.sum(given * (moved * rstd), axis=0, keepdims=True)
        shift_grad[...] += jnp.sum(given, axis=0, keepdims=True)

    @pl.when(i == 2 * tiles)
    def _():
        cot = jnp.sum(decay_cot[...], axis=0, keepdims=True)
        factor_re, factor_im = rates[0:1, :], rates[1:2, :]
        size = factor_re * factor_re + factor_im * factor_im
        vector_stage[...] = jnp.zeros_like(vector_stage)
        vector_stage[0:1, :width] = gain_grad[...]
        vector_stage[1:2, :width] = shift_grad[...]
        vector_stage[2:3, :width] = through_grad[...]
        vector_stage[3:4, :] = bias_grad[:, :both]
        vector_stage[4:5, : 2 * width - both] = bias_grad[:, both:]
        vector_stage[5:6, :states] = (cot[:, :states] * factor_re - cot[:, states:] * factor_im) / size
        vector_stage[5:6, states:] = (cot[:, :states] * factor_im + cot[:, states:] * factor_re) / size
        d_re, d_im = drive_grad[:, :states], drive_grad[:, states:]
        b_re, b_im = drive_raw[:, :states].astype(F32), drive_raw[:, states:].astype(F32)
        vector_stage[6:7, :states] = jnp.sum(d_re * b_re + d_im * b_im, axis=0, keepdims=True)
        vector_stage[6:7, states:] = jnp.sum(d_im * b_re - d_re * b_im, axis=0, keepdims=True)

        copies = [
            remote(
                vector_stage, across.at[away - 1], vector_send.at[away - 1], vector_recv.at[away - 1],
                {"fsdp": lax.rem(column + away, members)},
            )
            for away in range(1, members)
        ]
        for copy in copies:
            copy.start()
        for copy in copies:
            copy.wait()
        total = vector_stage[...]
        for k in range(members - 1):
            total = total + across[k]
        vector_sum[...] = total
        copies = [
            remote(
                vector_sum, along.at[away - 1], vector_send.at[members - 2 + away], vector_recv.at[members - 2 + away],
                {"dp": lax.rem(row + away, grid.dp)},
            )
            for away in range(1, grid.dp)
        ]
        for copy in copies:
            copy.start()
        advance((2,), phases)
        for copy in copies:
            copy.wait()
        total = vector_sum[...]
        for k in range(grid.dp - 1):
            total = total + along[k]
        vector_sum[...] = total


def tail_kernel(
    grid, tokens, cotangent, given_low, gated_low, vectors, rates, drive_sum, readout_sum, weight_sum, vector_sum,
    out, token_grad, gain_grad, shift_grad, real_grad, rotation_grad, timestep_grad, drive_grad, readout_grad,
    through_grad, weight_grad, bias_grad,
):
    width = tokens.shape[1]
    both = vector_sum.shape[1]
    states = both // 2
    rows = tokens[...].astype(F32)
    out[...] = rows + gated_low[...].astype(F32)
    moved, rstd = norm_stats(rows)
    xhat = moved * rstd
    scaled = given_low[...].astype(F32) * vectors[0:1, :width]
    inner = jnp.mean(scaled * xhat, axis=-1, keepdims=True)
    token_grad[...] = cotangent[...].astype(F32) + rstd * (
        scaled - jnp.mean(scaled, axis=-1, keepdims=True) - xhat * inner
    )

    @pl.when(pl.program_id(0) == 0)
    def _():
        row, column, _ = grid.here()
        me = row * 2**grid.bits + column
        real, rotation, step_log = [rates[k : k + 1, :] for k in (4, 5, 6)]
        timestep, factor_re, factor_im, modulus, scale_re, scale_im = rates_of(real, rotation, step_log)
        d_re, d_im = drive_sum[:, :states], drive_sum[:, states:]
        drive_grad[:, :states] = scale_re * d_re + scale_im * d_im
        drive_grad[:, states:] = scale_re * d_im - scale_im * d_re
        readout_grad[...] = readout_sum[...]
        weight_grad[...] = weight_sum[...]
        s_re, s_im = vector_sum[6:7, :states], vector_sum[6:7, states:]
        total_re = vector_sum[5:6, :states] + (s_re * real - s_im * rotation) / modulus
        total_im = vector_sum[5:6, states:] + (s_re * rotation + s_im * real) / modulus
        ratio_re = (scale_re * real + scale_im * rotation) / modulus
        ratio_im = (scale_im * real - scale_re * rotation) / modulus
        lambda_re = timestep * (total_re * factor_re + total_im * factor_im) - (s_re * ratio_re + s_im * ratio_im)
        lambda_im = timestep * (total_im * factor_re - total_re * factor_im) - (s_im * ratio_re - s_re * ratio_im)
        turn_re = real * factor_re - rotation * factor_im
        turn_im = real * factor_im + rotation * factor_re
        step_grad = timestep * (total_re * turn_re + total_im * turn_im)

        def own(vector, target):
            length, size = vector.shape[1], target.shape[0]
            wide = jnp.broadcast_to(vector, (SUB, length))
            rolled = pltpu.roll(wide, lax.rem(length - me * size, length), 1)
            target[...] = rolled[0:1, :size].reshape(size)

        own(vector_sum[0:1, :width], gain_grad)
        own(vector_sum[1:2, :width], shift_grad)
        own(vector_sum[2:3, :width], through_grad)
        own(jnp.concatenate([vector_sum[3:4, :], vector_sum[4:5, : 2 * width - both]], axis=1), bias_grad)
        own(lambda_re, real_grad)
        own(lambda_im, rotation_grad)
        own(step_grad, timestep_grad)


def whole(shape):
    return pl.BlockSpec(shape, lambda i: (0,) * len(shape), pipeline_mode=pl.Buffered(1))


def total_of(shape):
    return pl.BlockSpec(shape, lambda i: (0,) * len(shape))


def tiled(rows, columns):
    return pl.BlockSpec((rows, columns), lambda i: (i, 0))


def params(cid=None):
    if cid is None:
        return pltpu.CompilerParams(dimension_semantics=("arbitrary",), vmem_limit_bytes=VMEM_LIMIT)
    return pltpu.CompilerParams(
        dimension_semantics=("arbitrary",), vmem_limit_bytes=VMEM_LIMIT, collective_id=cid, has_side_effects=True
    )


def body(
    tokens, cotangent, block_target, sequence_lengths, norm_gain, norm_shift, decay_real, decay_rotation,
    log_timestep, drive_matrix, readout_matrix, feedthrough, mixer_weight, mixer_bias,
):
    members = lax.axis_size("fsdp")
    grid = Grid((lax.axis_size("dp"), members))
    blocks = block_target.shape[0]
    rows, width = tokens.shape
    both = drive_matrix.shape[1]
    states = both // 2
    block_rows = rows // blocks
    span = SUB * block_rows
    tile = 2 * span
    tiles = rows // tile
    tile_blocks = tile // block_rows
    total = blocks * members
    sequences = sequence_lengths.shape[1]
    shape = jax.ShapeDtypeStruct
    anywhere = pl.BlockSpec(memory_space=pl.ANY)
    regular = pltpu.SemaphoreType.DMA

    order = jnp.arange(span, dtype=jnp.int32)
    source = (order % SUB) * block_rows + order // SUB
    perm = (source[:, None] == order[None]).astype(BF16)
    back = (order[:, None] == source[None]).astype(BF16)

    def early(rows_of, columns):
        return pl.BlockSpec((rows_of, columns), lambda i: (jnp.minimum(i, tiles - 1), 0))

    def late(rows_of, columns):
        return pl.BlockSpec((rows_of, columns), lambda i: (jnp.clip(i - tiles, 0, tiles - 1), 0))

    def flat(size):
        return pl.BlockSpec((size,), lambda i: (0,))

    small = (norm_gain, norm_shift, feedthrough, mixer_bias, decay_real, decay_rotation, log_timestep, block_target)
    counts = tuple(v.shape[0] for v in small)
    shards = (drive_matrix, readout_matrix, mixer_weight)
    slots = grid.dp - 1 + grid.bits
    dealt, driven, keep, carry, drive, drive_raw, readout, mixer, vectors, rates, place, own_place, broken = pl.pallas_call(
        functools.partial(front_kernel, grid, block_rows, counts),
        grid=(2 * tiles + 1,),
        in_specs=[early(tile, width)]
        + [flat(size) for size in counts]
        + [whole((1, sequences)), anywhere, anywhere, anywhere, whole((span, span))],
        out_specs=[
            late(tile, width), late(tile, both), late(tile, LANES), total_of((blocks, both)), total_of((width, both)),
            total_of((width, both)), anywhere, anywhere, total_of((SUB, 2 * width)), total_of((SUB, states)),
            total_of((1, total)), total_of((blocks, LANES)), total_of((sequences, members, LANES)),
        ],
        out_shape=[
            shape((rows, width), BF16), shape((rows, both), F32), shape((rows, LANES), F32), shape((blocks, both), F32),
            shape((width, both), BF16), shape((width, both), BF16),
            shape(grid.shape + readout_matrix.shape, BF16), shape(grid.shape + mixer_weight.shape, BF16),
            shape((SUB, 2 * width), F32), shape((SUB, states), F32), shape((1, total), F32),
            shape((blocks, LANES), F32), shape((sequences, members, LANES), jnp.int32),
        ],
        scratch_shapes=[
            pltpu.VMEM((rows, width), F32),
            pltpu.VMEM(grid.shape + (SUB, LANES), F32),
            pltpu.VMEM(grid.shape + drive_matrix.shape, BF16),
            pltpu.VMEM((blocks, LANES), jnp.int32),
            pltpu.VMEM((members, blocks, both), BF16),
            pltpu.VMEM((total, both), F32),
            regular((4 * slots,)), regular((4 * slots,)), regular((len(shards),)), regular((members,)), regular((members,)),
        ],
        compiler_params=params(0),
        name="front",
    )(tokens, *small, sequence_lengths, *shards, perm)
    readout = readout.reshape(both, width)
    mixer = mixer.reshape(width, 2 * width)

    gated_low, mixed_low, joined, joined_grad, weight_grad, bias_grad, through_grad, readout_grad, coming = pl.pallas_call(
        functools.partial(main_kernel, grid, block_rows),
        grid=(tiles + 1,),
        in_specs=[
            early(tile, width), early(tile, width), early(tile, both), early(tile_blocks, both),
            early(tile, LANES), whole((SUB, states)), whole((both, width)), whole((SUB, 2 * width)),
            whole((width, 2 * width)), whole((span, span)), whole((span, span)), whole((1, total)),
            whole((blocks, LANES)), whole((sequences, members, LANES)),
        ],
        out_specs=[
            early(tile, width), early(tile, width), early(tile, both), early(tile, both),
            total_of((width, 2 * width)), total_of((1, 2 * width)), total_of((1, width)), total_of((both, width)),
            total_of((blocks, both)),
        ],
        out_shape=[
            shape((rows, width), BF16), shape((rows, width), BF16), shape((rows, both), BF16),
            shape((rows, both), F32), shape((width, 2 * width), F32), shape((1, 2 * width), F32),
            shape((1, width), F32), shape((both, width), F32), shape((blocks, both), F32),
        ],
        scratch_shapes=[
            pltpu.VMEM((members, blocks, both), BF16), pltpu.VMEM((total, both), F32), regular((members - 1,)),
            regular((members - 1,)),
        ],
        compiler_params=params(1),
        name="main",
    )(cotangent, dealt, driven, carry, keep, rates, readout, vectors, mixer, perm, back, place, own_place, broken)

    dims = list(range(grid.bits))
    turns = grid.orders(dims, ())
    orders = [(grid.bits,) + turns[k % len(turns)] for k in range(3)]
    weights = (readout_matrix, mixer_weight, drive_matrix)
    buffers = []
    for turn, weight in zip(orders, weights):
        for dim, _, left in reduce_plan(grid, turn):
            fan = grid.dp - 1 if dim == 0 else 1
            buffers.append(pltpu.VMEM((fan,) + tuple(grid.shape[d] for d in left) + weight.shape, BF16))
    given_low, drive_sum, readout_sum, weight_sum, vector_sum = pl.pallas_call(
        functools.partial(last_kernel, grid, block_rows, orders),
        grid=(2 * tiles + 1,),
        in_specs=[
            early(tile, width), early(tile, both), early(tile, both), early(tile_blocks, both), early(tile_blocks, both),
            early(tile, LANES), late(tile, width), late(tile, width), whole((SUB, states)), whole((SUB, 2 * width)),
            whole((width, both)), whole((width, both)), whole((span, span)), whole(grid.shape + readout_matrix.shape),
            whole(grid.shape + mixer_weight.shape), whole((1, 2 * width)), whole((1, width)),
        ],
        out_specs=[
            late(tile, width), total_of(drive_matrix.shape), total_of(readout_matrix.shape),
            total_of(mixer_weight.shape), total_of((SUB, both)),
        ],
        out_shape=[
            shape((rows, width), BF16), shape(drive_matrix.shape, F32), shape(readout_matrix.shape, F32),
            shape(mixer_weight.shape, F32), shape((SUB, both), F32),
        ],
        scratch_shapes=[
            pltpu.VMEM((rows, both), BF16), pltpu.VMEM((width, both), F32),
            pltpu.VMEM(grid.shape + drive_matrix.shape, F32), pltpu.VMEM((SUB, both), F32),
            pltpu.VMEM((1, width), F32), pltpu.VMEM((1, width), F32),
        ]
        + [pltpu.VMEM(grid.shape[:-1] + weight.shape, F32) for weight in weights]
        + buffers
        + buffers
        + [
            pltpu.VMEM((SUB, both), F32), pltpu.VMEM((members - 1, SUB, both), F32),
            pltpu.VMEM((grid.dp - 1, SUB, both), F32), regular((3 * slots,)), regular((3 * slots,)),
            regular((members + grid.dp - 2,)), regular((members + grid.dp - 2,)),
        ],
        compiler_params=params(2),
        name="last",
    )(
        dealt, joined, joined_grad, carry, coming, keep, mixed_low, tokens, rates, vectors, drive, drive_raw, back,
        readout_grad.reshape(grid.shape + readout_matrix.shape), weight_grad.reshape(grid.shape + mixer_weight.shape),
        bias_grad, through_grad,
    )

    vector_sizes = [v.shape[0] for v in (norm_gain, norm_shift, decay_real, decay_rotation, log_timestep)]
    outs = pl.pallas_call(
        functools.partial(tail_kernel, grid),
        grid=(tiles,),
        in_specs=[tiled(tile, width)] * 4
        + [
            whole((SUB, 2 * width)), whole((SUB, states)), whole(drive_matrix.shape), whole(readout_matrix.shape),
            whole(mixer_weight.shape), whole((SUB, both)),
        ],
        out_specs=[tiled(tile, width)] * 2
        + [flat(size) for size in vector_sizes]
        + [
            total_of(drive_matrix.shape), total_of(readout_matrix.shape), flat(feedthrough.shape[0]),
            total_of(mixer_weight.shape), flat(mixer_bias.shape[0]),
        ],
        out_shape=[shape((rows, width), F32)] * 2
        + [shape((size,), F32) for size in vector_sizes]
        + [
            shape(drive_matrix.shape, F32), shape(readout_matrix.shape, F32), shape(feedthrough.shape, F32),
            shape(mixer_weight.shape, F32), shape(mixer_bias.shape, F32),
        ],
        compiler_params=params(),
        name="tail",
    )(tokens, cotangent, given_low, gated_low, vectors, rates, drive_sum, readout_sum, weight_sum, vector_sum)
    return tuple(outs)


def solution(mesh):
    rows = P(AXES, None)
    flat = P(AXES)
    return jax.shard_map(
        body,
        mesh=mesh,
        in_specs=(rows, rows, flat, rows, flat, flat, flat, flat, flat, rows, rows, flat, rows, flat),
        out_specs=(rows, rows, flat, flat, flat, flat, flat, rows, rows, flat, rows, flat),
        check_vma=False,
    )
```

```python
import functools
import itertools

import jax
import jax.numpy as jnp
import numpy as np
from jax import lax
from jax.experimental import pallas as pl
from jax.experimental.pallas import tpu as pltpu
from jax.sharding import PartitionSpec as P

EPSILON = 1e-05
AXES = ("dp", "fsdp")
F32 = jnp.float32
BF16 = jnp.bfloat16
LANES = 128
SUB = 8
VMEM_LIMIT = 60 * 1024 * 1024


def dot(left, right):
    return jnp.dot(left, right, preferred_element_type=F32)


def contract_rows(left, right):
    return lax.dot_general(left, right, (((0,), (0,)), ((), ())), preferred_element_type=F32)


def contract_cols(left, right):
    return lax.dot_general(left, right, (((1,), (1,)), ((), ())), preferred_element_type=F32)


def lanes_to(mask, width):
    return jnp.concatenate([mask] * (width // LANES), axis=1)


def spread(vector, rows):
    return jnp.broadcast_to(vector, (rows, vector.shape[1]))


def gelu_parts(v):
    cdf = 0.5 + 0.5 * lax.erf(v * 0.7071067811865476)
    density = 0.3989422804014327 * jnp.exp(-0.5 * v * v)
    return v * cdf, cdf + v * density


def permute_tile(perm, tile, span):
    return jnp.concatenate(
        [dot(perm, tile[i * span : (i + 1) * span]) for i in range(tile.shape[0] // span)], axis=0
    )


def norm_stats(rows):
    center = jnp.mean(rows, axis=-1, keepdims=True)
    moved = rows - center
    spread_of = jnp.mean(moved * moved, axis=-1, keepdims=True)
    return moved, lax.rsqrt(spread_of + EPSILON)


MESH = pl.DeviceIdType.MESH


class Grid:
    def __init__(self, dp, members):
        self.dp, self.members = dp, members
        self.shape = (dp, members // 2, 2)
        self.slots = dp - 1 + members // 2 - 1 + 1

    def here(self):
        row, column = lax.axis_index("dp"), lax.axis_index("fsdp")
        return row, column, (row, lax.div(column, 2), lax.rem(column, 2))

    def fan(self, dim):
        return self.shape[dim] - 1

    def peers(self, dim):
        row, column, mine = self.here()
        found = []
        for away in range(1, self.shape[dim]):
            index = lax.rem(mine[dim] + away, self.shape[dim])
            if dim == 0:
                device = {"dp": index}
            elif dim == 1:
                device = {"fsdp": 2 * index + mine[2]}
            else:
                device = {"fsdp": 2 * mine[1] + index}
            found.append((away - 1, device, index))
        return found


def announce(grid):
    barrier = pltpu.get_barrier_semaphore()
    row, column, _ = grid.here()
    for away in range(1, grid.dp):
        pl.semaphore_signal(
            barrier, inc=1, device_id={"dp": lax.rem(row + away, grid.dp)}, device_id_type=MESH
        )
    for away in range(1, grid.members):
        pl.semaphore_signal(
            barrier, inc=1, device_id={"fsdp": lax.rem(column + away, grid.members)}, device_id_type=MESH
        )


def meet(grid):
    pl.semaphore_wait(pltpu.get_barrier_semaphore(), grid.dp + grid.members - 2)


def remote(source, target, send, recv, device):
    return pltpu.make_async_remote_copy(
        src_ref=source, dst_ref=target, send_sem=send, recv_sem=recv, device_id=device, device_id_type=MESH
    )


def gather_phase(grid, ref, axes, dim, done, send, recv, base):
    _, _, mine = grid.here()
    at = tuple(slice(None) if d in done else mine[d] for d in axes)
    return [
        pltpu.make_async_remote_copy(
            src_ref=ref.at[at], dst_ref=ref.at[at], send_sem=send.at[base + slot], recv_sem=recv.at[base + slot],
            device_id=device, device_id_type=MESH,
        )
        for slot, device, _ in grid.peers(dim)
    ]


def reduce_plan(grid, order):
    plan = []
    for phase, dim in enumerate(order):
        done = order[:phase]
        left = tuple(d for d in range(len(grid.shape)) if d not in done and d != dim)
        plan.append((dim, done, left))
    return plan


def lane_index(width):
    return lax.broadcasted_iota(jnp.int32, (1, width), 1).astype(F32)


def unpack(rows, row, count, width):
    lanes = lane_index(width)
    owner = jnp.floor((lanes + 0.5) * (1.0 / count))
    inner = lanes - count * owner
    taken = lax.broadcasted_iota(jnp.int32, (LANES, width), 0).astype(F32) == inner
    spread_out = dot(rows.astype(BF16), jnp.where(taken, 1.0, 0.0).astype(BF16))
    index = lax.broadcasted_iota(jnp.int32, (rows.shape[0], width), 0).astype(F32)
    return jnp.sum(jnp.where(index == owner * SUB + row, spread_out, 0.0), axis=0, keepdims=True)


def rates_of(real, rotation, step_log):
    timestep = jnp.exp(step_log)
    magnitude = jnp.exp(real * timestep)
    turned = rotation * timestep
    factor_re = magnitude * jnp.cos(turned)
    factor_im = magnitude * jnp.sin(turned)
    modulus = real * real + rotation * rotation
    scale_re = ((factor_re - 1.0) * real + factor_im * rotation) / modulus
    scale_im = (factor_im * real - (factor_re - 1.0) * rotation) / modulus
    return timestep, factor_re, factor_im, modulus, scale_re, scale_im


def cross_blocks(members, reverse, pieces, place, own_place, broken, flow_re, flow_im, dealt, carries):
    states = flow_re.shape[1]
    total = place.shape[1]
    steps = total // members
    rows = lax.broadcasted_iota(jnp.int32, (total, total), 0).astype(F32)
    chosen = jnp.where(rows == place[...], 1.0, 0.0).astype(BF16)
    dealt[...] = dot(chosen, pieces[...].reshape(total, 2 * states))
    rate_re = spread(flow_re, members)
    rate_im = spread(-flow_im if reverse else flow_im, members)
    marks = [broken[s] for s in range(broken.shape[0])]

    def step(i, state):
        re, im = state
        p = steps - 1 - i if reverse else i
        at = pl.multiple_of(p * members, members)
        here = dealt[pl.ds(at, members), :]
        met = marks[0] == p
        for mark in marks[1:]:
            met = met | (mark == p)
        mask = lanes_to(jnp.where(met, 0.0, 1.0), states)
        dealt[pl.ds(at, members), :] = jnp.concatenate([re, im], axis=1)
        return (
            mask * (rate_re * re - rate_im * im) + here[:, :states],
            mask * (rate_re * im + rate_im * re) + here[:, states:],
        )

    zero = jnp.zeros((members, states), F32)
    lax.fori_loop(0, steps, step, (zero, zero), unroll=4)
    own = own_place.shape[0]
    columns = lax.broadcasted_iota(jnp.int32, (own, total), 1).astype(F32)
    taken = jnp.where(columns == lanes_to(own_place[...], total), 1.0, 0.0).astype(BF16)
    high = dealt[...].astype(BF16)
    low = (dealt[...] - high.astype(F32)).astype(BF16)
    carries[...] = dot(taken, high) + dot(taken, low)


def front_kernel(
    grid, block_rows, counts, tile, tokens, gain_s, shift_s, through_s, bias_s, real_s, rotation_s, step_s, target_s,
    lengths_s, drive_s, readout_s, mixer_s, perm,
    dealt, driven, keep, carries, drive, drive_raw, readout_w, mixer_w, vectors, rates, place, own_place, broken,
    rows_in, normed, xhat, table, drive_w, bits, pieces, dealt_ends, send, recv, local, push_send, push_recv,
):
    i = pl.program_id(0)
    tiles = pl.num_programs(0) - 2
    row, column, mine = grid.here()
    members = grid.members
    blocks = target_s.shape[0]
    width = tokens.shape[1]
    both = drive.shape[1]
    states = both // 2
    span = SUB * block_rows
    chains = tile // span
    tile_blocks = tile // block_rows
    axes = tuple(range(len(grid.shape)))
    wholes = (table, drive_w, readout_w, mixer_w)
    orders = ((0, 1, 2), (0, 1, 2), (1, 0, 2), (0, 1, 2))
    phases = 3

    def phase_copies(k, phase):
        order = orders[k]
        base = k * grid.slots + sum(grid.fan(d) for d in order[:phase])
        return gather_phase(grid, wholes[k], axes, order[phase], order[:phase], send, recv, base)

    def advance(ks, phase):
        for k in ks:
            if phase:
                for copy in phase_copies(k, phase - 1):
                    copy.wait()
            if phase < phases:
                for copy in phase_copies(k, phase):
                    copy.start()

    @pl.when(i == 0)
    def _():
        copies = [
            pltpu.make_async_copy(shard, ref.at[tuple(mine)], local.at[k])
            for k, (shard, ref) in enumerate(zip((drive_s, readout_s, mixer_s), wholes[1:]))
        ]
        for copy in copies:
            copy.start()
        held = [gain_s, shift_s, through_s, bias_s, real_s, rotation_s, step_s, target_s]
        own = table.at[tuple(mine)]
        own[...] = jnp.zeros_like(own)
        for k, ref in enumerate(held):
            own[k : k + 1, : ref.shape[0]] = ref[...].astype(F32).reshape(1, ref.shape[0])
        sequences = lengths_s.shape[1]
        own[4:5, LANES // 2 : LANES // 2 + sequences] = lengths_s[...].astype(F32)
        announce(grid)
        chunks = [
            pltpu.make_async_copy(
                tokens.at[pl.ds(j * tile, tile)], rows_in.at[pl.ds(j * tile, tile)], local.at[len(copies) + j]
            )
            for j in range(tiles)
        ]
        for copy in chunks:
            copy.start()
        for copy in copies:
            copy.wait()
        meet(grid)
        advance((0, 1), 0)

        def stats(j, _):
            at = pl.ds(pl.multiple_of(j * tile, tile), tile)
            moved, rstd = norm_stats(rows_in[at, :].astype(F32))
            xhat[at, :] = moved * rstd
            return 0

        for copy in chunks[: tiles // 2]:
            copy.wait()
        lax.fori_loop(0, tiles // 2, stats, 0)
        advance((0, 1), 1)
        advance((2, 3), 0)
        for copy in chunks[tiles // 2 :]:
            copy.wait()
        lax.fori_loop(tiles // 2, tiles, stats, 0)
        advance((0,), 2)
        advance((0,), 3)
        rows = table[...].reshape(-1, LANES)
        vectors[...] = jnp.zeros_like(vectors)
        for k, size in enumerate((width, width, width, 2 * width)):
            vectors[k : k + 1, :size] = unpack(rows, k, counts[k], size)
        real, rotation, step_log = [unpack(rows, k, counts[k], states) for k in (4, 5, 6)]
        _, factor_re, factor_im, _, scale_re, scale_im = rates_of(real, rotation, step_log)
        flow_re, flow_im = factor_re, factor_im
        power = 1
        while power < block_rows:
            flow_re, flow_im = flow_re * flow_re - flow_im * flow_im, 2.0 * flow_re * flow_im
            power *= 2
        for k, value in enumerate((factor_re, factor_im, flow_re, flow_im, real, rotation, step_log)):
            rates[k : k + 1, :] = value
        group = table[row].reshape(members * SUB, LANES)
        for m in range(members):
            q = group[m * SUB + 7 : m * SUB + 8, :blocks]
            d = jnp.floor(q * (1.0 / blocks))
            place[:, m * blocks : (m + 1) * blocks] = (q - d * blocks) * members + d
        lengths = jnp.concatenate([group[m * SUB + 4 : m * SUB + 5, :] for m in range(members)], axis=0)
        sequences = lengths_s.shape[1]
        q = table[tuple(mine) + (slice(7, 8), slice(None))]
        diagonal = lax.broadcasted_iota(jnp.int32, (blocks, LANES), 0) == lax.broadcasted_iota(
            jnp.int32, (blocks, LANES), 1
        )
        q = jnp.sum(jnp.where(diagonal, jnp.broadcast_to(q, (blocks, LANES)), 0.0), axis=1, keepdims=True)
        q = jnp.broadcast_to(q, (blocks, LANES))
        d = jnp.floor(q * (1.0 / blocks))
        p = q - d * blocks
        own_place[...] = p * members + d
        start = jnp.zeros((members, LANES), F32)
        marks = jnp.zeros((blocks, LANES), jnp.int32)
        for s in range(sequences):
            broken[s] = jnp.floor(start * (1.0 / block_rows)).astype(jnp.int32)
            mark = jnp.zeros((blocks, LANES), F32)
            for m in range(members):
                mark = jnp.where(d == float(m), jnp.broadcast_to(start[m : m + 1, :], (blocks, LANES)), mark)
            mark = mark - p * block_rows
            inside = (mark >= 0.0) & (mark < block_rows)
            shift = jnp.where(inside, mark, 0.0).astype(jnp.int32)
            marks = marks | jnp.where(inside, lax.shift_left(jnp.ones_like(shift), shift), 0)
            column_of = lengths[:, LANES // 2 + s : LANES // 2 + s + 1]
            start = start + jnp.broadcast_to(column_of, (members, LANES))
        bits[...] = marks
        gain = vectors[0:1, :width]
        shift_by = vectors[1:2, :width]

        def settle(j, _):
            at = pl.ds(pl.multiple_of(j * tile, tile), tile)
            rounded = (xhat[at, :] * gain + shift_by).astype(BF16)
            normed[at, :] = permute_tile(perm[...], rounded, span).astype(BF16)
            return 0

        lax.fori_loop(0, tiles // 2, settle, 0)
        advance((1,), 2)
        lax.fori_loop(tiles // 2, tiles, settle, 0)
        advance((1,), 3)
        drive_raw[...] = drive_w[...].reshape(width, both)
        raw = drive_raw[...].astype(F32)
        drive[:, :states] = (scale_re * raw[:, :states] - scale_im * raw[:, states:]).astype(BF16)
        drive[:, states:] = (scale_re * raw[:, states:] + scale_im * raw[:, :states]).astype(BF16)

    @pl.when(i == 1)
    def _():
        advance((2, 3), 1)

    @pl.when(i == tiles // 2 + 1)
    def _():
        advance((2, 3), 2)

    def push_far(at):
        return [
            remote(pieces.at[at], pieces.at[at], push_send.at[slot], push_recv.at[slot], device)
            for slot, device, _ in grid.peers(1)
        ]

    def push_near(at, slot):
        device = grid.peers(2)[0][1]
        return remote(pieces.at[at], pieces.at[at], push_send.at[slot], push_recv.at[slot], device)

    far = grid.fan(1)

    @pl.when((i >= 1) & (i <= tiles))
    def _():
        j = i - 1
        dealt[...] = normed[pl.ds(pl.multiple_of(j * tile, tile), tile), :]
        driven[...] = dot(dealt[...], drive[...])
        rate_re = spread(rates[0:1, :], SUB)
        rate_im = spread(rates[1:2, :], SUB)
        first = pl.multiple_of(j * tile_blocks, tile_blocks)
        mark = bits[pl.ds(first, tile_blocks), :]
        state = [(jnp.zeros((SUB, states), F32), jnp.zeros((SUB, states), F32)) for _ in range(chains)]
        for t in range(block_rows):
            single = 1 << t if t < 31 else -(1 << 31)
            for c in range(chains):
                at = c * span + t * SUB
                narrow = jnp.where((mark[c * SUB : (c + 1) * SUB] & single) == 0, 1.0, 0.0)
                keep[at : at + SUB, :] = narrow
                mask = lanes_to(narrow, states)
                re, im = state[c]
                now_re = mask * (rate_re * re - rate_im * im) + driven[at : at + SUB, :states]
                now_im = mask * (rate_re * im + rate_im * re) + driven[at : at + SUB, states:]
                state[c] = (now_re, now_im)
        ends = jnp.concatenate([jnp.concatenate(state[c], axis=1) for c in range(chains)], axis=0)
        pieces[column, pl.ds(first, tile_blocks), :] = ends.astype(BF16)
        at = (column, pl.ds(first, tile_blocks))
        for copy in push_far(at) + [push_near(at, far)]:
            copy.start()

    @pl.when(i == tiles + 1)
    def _():
        onward = []
        for k, copy in enumerate(push_far((column,))):
            copy.wait()
            there = 2 * lax.rem(mine[1] + grid.shape[1] - 1 - k, grid.shape[1]) + mine[2]
            onward.append(push_near((there,), far + 1 + k))
            onward[-1].start()
        push_near((column,), far).wait()
        for copy in onward:
            copy.wait()
        cross_blocks(
            members, False, pieces, place, own_place, broken, rates[2:3, :], rates[3:4, :], dealt_ends, carries
        )
        advance((2, 3), phases)


def main_kernel(
    grid, block_rows, cotangent, dealt, driven, carry, keep, rates, readout, vectors, mixer, perm, back, place,
    own_place, broken,
    gated_low, mixed_low, joined, joined_grad, weight_grad, bias_grad, through_grad, readout_grad, mixed_sum, coming,
    pieces, dealt_heads, push_send, push_recv,
):
    i = pl.program_id(0)
    tiles = pl.num_programs(0) - 1
    _, column, _ = grid.here()
    members = grid.members
    span = SUB * block_rows
    tile, width = cotangent.shape
    states = rates.shape[1]
    chains = tile // span
    tile_blocks = tile // block_rows

    def push_to(at):
        return [
            remote(
                pieces.at[at], pieces.at[at], push_send.at[away - 1], push_recv.at[away - 1],
                {"fsdp": lax.rem(column + away, members)},
            )
            for away in range(1, members)
        ]

    @pl.when(i == 0)
    def _():
        weight_grad[...] = jnp.zeros_like(weight_grad)
        bias_grad[...] = jnp.zeros_like(bias_grad)
        through_grad[...] = jnp.zeros_like(through_grad)
        readout_grad[...] = jnp.zeros_like(readout_grad)
        mixed_sum[...] = jnp.zeros_like(mixed_sum)
        announce(grid)

    @pl.when(i < tiles)
    def _():
        through = vectors[2:3, :width]
        bias = vectors[3:4, : 2 * width]
        rate_re = spread(rates[0:1, :], SUB)
        rate_im = spread(rates[1:2, :], SUB)
        state = [
            (carry[c * SUB : (c + 1) * SUB, :states], carry[c * SUB : (c + 1) * SUB, states:])
            for c in range(chains)
        ]
        for t in range(0, block_rows, 2):
            for c in range(chains):
                held = []
                for step in (t, t + 1):
                    at = c * span + step * SUB
                    mask = lanes_to(keep[at : at + SUB, :], states)
                    re, im = state[c]
                    now_re = mask * (rate_re * re - rate_im * im) + driven[at : at + SUB, :states]
                    now_im = mask * (rate_re * im + rate_im * re) + driven[at : at + SUB, states:]
                    state[c] = (now_re, now_im)
                    held.append(state[c])
                at = c * span + t * SUB
                joined[at : at + 2 * SUB, :states] = jnp.concatenate([held[0][0], held[1][0]], axis=0).astype(BF16)
                joined[at : at + 2 * SUB, states:] = (-jnp.concatenate([held[0][1], held[1][1]], axis=0)).astype(BF16)

        dealt_f32 = dealt[...].astype(F32)
        mixed = dot(joined[...], readout[...]) + through * dealt_f32
        activated, slope = gelu_parts(mixed)
        features = permute_tile(back[...], activated.astype(BF16), span).astype(BF16)
        hidden = dot(features, mixer[...]) + bias
        value = hidden[:, :width]
        sig = 1.0 / (1.0 + jnp.exp(-hidden[:, width:]))
        gated_low[...] = (value * sig).astype(BF16)
        cot_sig = cotangent[...].astype(F32) * sig
        hidden_low = jnp.concatenate(
            [cot_sig.astype(BF16), (cot_sig * value * (1.0 - sig)).astype(BF16)], axis=1
        )
        weight_grad[...] += contract_rows(features, hidden_low)
        bias_grad[...] += jnp.sum(hidden_low.astype(F32), axis=0, keepdims=True)
        feature_grad = contract_cols(hidden_low, mixer[...]).astype(BF16)
        mixed_grad = (permute_tile(perm[...], feature_grad, span) * slope).astype(BF16)
        mixed_low[...] = mixed_grad
        mixed_f32 = mixed_grad.astype(F32)
        through_grad[...] += jnp.sum(mixed_f32 * dealt_f32, axis=0, keepdims=True)
        mixed_sum[...] += jnp.sum(mixed_f32, axis=0, keepdims=True)
        readout_grad[...] += contract_rows(joined[...], mixed_grad)
        joined_grad[...] = contract_cols(mixed_grad, readout[...])

        going = [(jnp.zeros((SUB, states), F32), jnp.zeros((SUB, states), F32)) for _ in range(chains)]
        for t in reversed(range(block_rows)):
            for c in range(chains):
                at = c * span + t * SUB
                mask = lanes_to(keep[at : at + SUB, :], states)
                re = joined_grad[at : at + SUB, :states] + going[c][0]
                im = going[c][1] - joined_grad[at : at + SUB, states:]
                going[c] = (mask * (rate_re * re + rate_im * im), mask * (rate_re * im - rate_im * re))
        heads = jnp.concatenate([jnp.concatenate(going[c], axis=1) for c in range(chains)], axis=0)
        at = (column, pl.ds(pl.multiple_of(i * tile_blocks, tile_blocks), tile_blocks))
        pieces[at + (slice(None),)] = heads.astype(BF16)

        @pl.when(i == 0)
        def _():
            meet(grid)

        for copy in push_to(at):
            copy.start()

    @pl.when(i == tiles)
    def _():
        for copy in push_to((column,)):
            copy.wait()
        cross_blocks(
            members, True, pieces, place, own_place, broken, rates[2:3, :], rates[3:4, :], dealt_heads, coming
        )


def split(values):
    high = values.astype(BF16)
    rest = values - high.astype(F32)
    middle = rest.astype(BF16)
    return high, middle, (rest - middle.astype(F32)).astype(BF16)


def row_times(row, matrix):
    wide = [jnp.broadcast_to(piece.astype(F32), (SUB, row.shape[1])).astype(BF16) for piece in split(row)]
    return sum(contract_cols(piece, matrix) for piece in wide)[0:1]


def row_sums(matrix):
    ones = jnp.ones((SUB, matrix.shape[1]), BF16)
    return sum(contract_cols(ones, piece) for piece in split(matrix))[0:1]


def last_kernel(
    grid, block_rows, orders, dealt, joined, joined_grad, carry, coming, keep, mixed_low, tokens, rates, vectors, drive,
    drive_raw, back, readout_grad, weight_grad, bias_grad, through_grad, mixed_sum,
    token_part, drive_sum, readout_sum, weight_sum, vector_sum,
    driven_all, drive_grad, drive_parts, decay_cot, driven_sum, *rest,
):
    i = pl.program_id(0)
    tiles = (pl.num_programs(0) - 1) // 2
    row, column, mine = grid.here()
    members = grid.members
    core = 2
    phases = 3
    span = SUB * block_rows
    tile, width = tokens.shape
    both = joined.shape[1]
    states = both // 2
    chains = tile // span
    rest = list(rest)
    parts = (readout_grad, weight_grad, drive_parts)
    outs = (readout_sum, weight_sum, drive_sum)
    count = len(parts)
    accs = [rest.pop(0) for _ in range(count)]
    stages = [[rest.pop(0) for _ in range(phases)] for _ in range(count)]
    landed = [[rest.pop(0) for _ in range(phases)] for _ in range(count)]
    vector_stage, across, along, send, recv, vector_send, vector_recv = rest
    plans = [reduce_plan(grid, order) for order in orders]
    every = (0, 1, 2)
    kept = every[:-1]

    def combos(left):
        return list(itertools.product(*[range(grid.shape[d]) for d in left]))

    def at(dim, index, left, combo, dims):
        chosen = dict(zip(left, combo))
        chosen[dim] = index
        return tuple(chosen[d] if d in chosen else mine[d] for d in dims)

    def hops(k, phase):
        dim = plans[k][phase][0]
        base = k * grid.slots + sum(grid.fan(d) for d in orders[k][:phase])
        return [
            (
                remote(
                    stages[k][phase].at[slot], landed[k][phase].at[slot], send.at[base + slot], recv.at[base + slot],
                    device,
                ),
                slot,
                index,
            )
            for slot, device, index in grid.peers(dim)
        ]

    def begin(k, phase):
        dim, _, left = plans[k][phase]
        for copy, slot, index in hops(k, phase):
            for combo in combos(left):
                if dim == core:
                    piece = parts[k][at(dim, index, left, combo, every)]
                else:
                    piece = accs[k][at(dim, index, left, combo, kept)]
                stages[k][phase][(slot,) + combo] = piece.astype(BF16)
            copy.start()

    def finish(k, phase):
        dim, _, left = plans[k][phase]
        copies = hops(k, phase)
        for copy, _, _ in copies:
            copy.wait()
        for combo in combos(left):
            if dim == core:
                piece = parts[k][at(dim, mine[dim], left, combo, every)]
            else:
                piece = accs[k][at(dim, mine[dim], left, combo, kept)]
            for _, slot, _ in copies:
                piece = piece + landed[k][phase][(slot,) + combo].astype(F32)
            accs[k][at(dim, mine[dim], left, combo, kept)] = piece

    def advance(ks, phase):
        for k in ks:
            if phase:
                finish(k, phase - 1)
            if phase < phases:
                begin(k, phase)
            else:
                outs[k][...] = accs[k][mine[:-1]]

    rate_re = spread(rates[0:1, :], SUB)
    rate_im = spread(rates[1:2, :], SUB)

    def vector_across():
        return [
            remote(
                vector_stage, across.at[away - 1], vector_send.at[away - 1], vector_recv.at[away - 1],
                {"fsdp": lax.rem(column + away, members)},
            )
            for away in range(1, members)
        ]

    def vector_along():
        return [
            remote(
                vector_sum, along.at[slot], vector_send.at[members - 1 + slot], vector_recv.at[members - 1 + slot], device
            )
            for slot, device, _ in grid.peers(0)
        ]

    @pl.when(i == 0)
    def _():
        drive_grad[...] = jnp.zeros_like(drive_grad)
        decay_cot[...] = jnp.zeros_like(decay_cot)
        driven_sum[...] = jnp.zeros_like(driven_sum)
        announce(grid)

    @pl.when(i == 1)
    def _():
        meet(grid)
        advance((0, 1), 0)

    @pl.when(i == 3)
    def _():
        advance((0, 1), 1)

    @pl.when(i == tiles - 1)
    def _():
        advance((0,), 2)

    @pl.when(i == tiles + 2)
    def _():
        advance((1,), 2)

    @pl.when(i == 2 * tiles - 1)
    def _():
        advance((0, 1), 3)

    @pl.when(i < tiles)
    def _():
        driven_low = driven_all.at[pl.ds(pl.multiple_of(i * tile, tile), tile)]
        going = [
            (coming[c * SUB : (c + 1) * SUB, :states], coming[c * SUB : (c + 1) * SUB, states:])
            for c in range(chains)
        ]
        total = [(jnp.zeros((SUB, states), F32), jnp.zeros((SUB, states), F32)) for _ in range(chains)]
        sums = list(total)
        for t in reversed(range(0, block_rows, 2)):
            for c in range(chains):
                pair = c * span + t * SUB
                here_re = joined[pair : pair + SUB, :states].astype(F32)
                here_im = -joined[pair : pair + SUB, states:].astype(F32)
                if t == 0:
                    past_re = carry[c * SUB : (c + 1) * SUB, :states]
                    past_im = carry[c * SUB : (c + 1) * SUB, states:]
                else:
                    past_re = joined[pair - SUB : pair, :states].astype(F32)
                    past_im = -joined[pair - SUB : pair, states:].astype(F32)
                held = {}
                for step, (prev_re, prev_im) in ((t + 1, (here_re, here_im)), (t, (past_re, past_im))):
                    where = c * span + step * SUB
                    mask = lanes_to(keep[where : where + SUB, :], states)
                    re = joined_grad[where : where + SUB, :states] + going[c][0]
                    im = going[c][1] - joined_grad[where : where + SUB, states:]
                    held[step] = (re, im)
                    sums[c] = (sums[c][0] + re, sums[c][1] + im)
                    on_re = mask * (rate_re * re + rate_im * im)
                    on_im = mask * (rate_re * im - rate_im * re)
                    going[c] = (on_re, on_im)
                    total[c] = (
                        total[c][0] + (on_re * prev_re + on_im * prev_im),
                        total[c][1] + (on_im * prev_re - on_re * prev_im),
                    )
                driven_low[pair : pair + 2 * SUB, :states] = jnp.concatenate(
                    [held[t][0], held[t + 1][0]], axis=0
                ).astype(BF16)
                driven_low[pair : pair + 2 * SUB, states:] = jnp.concatenate(
                    [held[t][1], held[t + 1][1]], axis=0
                ).astype(BF16)
        for c in range(chains):
            decay_cot[...] += jnp.concatenate(total[c], axis=1)
            driven_sum[...] += jnp.concatenate(sums[c], axis=1)
        drive_grad[...] += contract_rows(dealt[...], driven_low[...])

    @pl.when(i == tiles)
    def _():
        shard = drive_parts.shape[-2]
        for s, place in enumerate(itertools.product(*[range(size) for size in grid.shape])):
            drive_parts[place] = drive_grad[s * shard : (s + 1) * shard, :]
        advance((2,), 0)
        cot = jnp.sum(decay_cot[...], axis=0, keepdims=True)
        factor_re, factor_im = rates[0:1, :], rates[1:2, :]
        size = factor_re * factor_re + factor_im * factor_im
        vector_stage[...] = jnp.zeros_like(vector_stage)
        through = vectors[2:3, :width]
        summed = jnp.sum(driven_sum[...], axis=0, keepdims=True)
        shift_sum = through * mixed_sum[...] + row_times(summed, drive[...])
        crossed = row_sums(drive[...].astype(F32) * drive_grad[...]) + through * through_grad[...]
        vector_stage[0:1, :width] = (crossed - vectors[1:2, :width] * shift_sum) / vectors[0:1, :width]
        vector_stage[1:2, :width] = shift_sum
        vector_stage[2:3, :width] = through_grad[...]
        vector_stage[3:4, :] = bias_grad[:, :both]
        vector_stage[4:5, : 2 * width - both] = bias_grad[:, both:]
        vector_stage[5:6, :states] = (cot[:, :states] * factor_re - cot[:, states:] * factor_im) / size
        vector_stage[5:6, states:] = (cot[:, :states] * factor_im + cot[:, states:] * factor_re) / size
        d_re, d_im = drive_grad[:, :states], drive_grad[:, states:]
        b_re, b_im = drive_raw[:, :states].astype(F32), drive_raw[:, states:].astype(F32)
        vector_stage[6:7, :states] = jnp.sum(d_re * b_re + d_im * b_im, axis=0, keepdims=True)
        vector_stage[6:7, states:] = jnp.sum(d_im * b_re - d_re * b_im, axis=0, keepdims=True)

        for copy in vector_across():
            copy.start()

    @pl.when(i == tiles + 1)
    def _():
        advance((2,), 1)

    @pl.when(i == tiles + 3)
    def _():
        for copy in vector_across():
            copy.wait()
        total = vector_stage[...]
        for k in range(members - 1):
            total = total + across[k]
        vector_sum[...] = total
        for copy in vector_along():
            copy.start()

    @pl.when(i == tiles + 5)
    def _():
        advance((2,), 2)

    @pl.when(i == 2 * tiles)
    def _():
        for copy in vector_along():
            copy.wait()
        total = vector_sum[...]
        for k in range(grid.dp - 1):
            total = total + along[k]
        vector_sum[...] = total
        advance((2,), 3)

    @pl.when((i >= tiles) & (i < 2 * tiles))
    def _():
        j = i - tiles
        driven_low = driven_all[pl.ds(pl.multiple_of(j * tile, tile), tile), :]
        normed_grad = vectors[2:3, :width] * mixed_low[...].astype(F32) + contract_cols(driven_low, drive[...])
        given = permute_tile(back[...], normed_grad.astype(BF16), span)
        moved, rstd = norm_stats(tokens[...].astype(F32))
        xhat = moved * rstd
        scaled = given * vectors[0:1, :width]
        inner = jnp.mean(scaled * xhat, axis=-1, keepdims=True)
        token_part[...] = (
            rstd * (scaled - jnp.mean(scaled, axis=-1, keepdims=True) - xhat * inner)
        ).astype(BF16)


def tail_kernel(
    grid, tokens, cotangent, token_part, gated_low, rates, drive_sum, readout_sum, weight_sum, vector_sum,
    out, token_grad, gain_grad, shift_grad, real_grad, rotation_grad, timestep_grad, drive_grad, readout_grad,
    through_grad, weight_grad, bias_grad,
):
    width = tokens.shape[1]
    both = vector_sum.shape[1]
    states = both // 2
    out[...] = tokens[...].astype(F32) + gated_low[...].astype(F32)
    token_grad[...] = cotangent[...].astype(F32) + token_part[...].astype(F32)

    @pl.when(pl.program_id(0) == 0)
    def _():
        row, column, _ = grid.here()
        me = row * grid.members + column
        real, rotation, step_log = [rates[k : k + 1, :] for k in (4, 5, 6)]
        timestep, factor_re, factor_im, modulus, scale_re, scale_im = rates_of(real, rotation, step_log)
        d_re, d_im = drive_sum[:, :states], drive_sum[:, states:]
        drive_grad[:, :states] = scale_re * d_re + scale_im * d_im
        drive_grad[:, states:] = scale_re * d_im - scale_im * d_re
        readout_grad[...] = readout_sum[...]
        weight_grad[...] = weight_sum[...]
        s_re, s_im = vector_sum[6:7, :states], vector_sum[6:7, states:]
        total_re = vector_sum[5:6, :states] + (s_re * real - s_im * rotation) / modulus
        total_im = vector_sum[5:6, states:] + (s_re * rotation + s_im * real) / modulus
        ratio_re = (scale_re * real + scale_im * rotation) / modulus
        ratio_im = (scale_im * real - scale_re * rotation) / modulus
        lambda_re = timestep * (total_re * factor_re + total_im * factor_im) - (s_re * ratio_re + s_im * ratio_im)
        lambda_im = timestep * (total_im * factor_re - total_re * factor_im) - (s_im * ratio_re - s_re * ratio_im)
        turn_re = real * factor_re - rotation * factor_im
        turn_im = real * factor_im + rotation * factor_re
        step_grad = timestep * (total_re * turn_re + total_im * turn_im)

        def own(vector, target):
            length, size = vector.shape[1], target.shape[0]
            wide = jnp.broadcast_to(vector, (SUB, length))
            rolled = pltpu.roll(wide, lax.rem(length - me * size, length), 1)
            target[...] = rolled[0:1, :size].reshape(size)

        own(vector_sum[0:1, :width], gain_grad)
        own(vector_sum[1:2, :width], shift_grad)
        own(vector_sum[2:3, :width], through_grad)
        own(jnp.concatenate([vector_sum[3:4, :], vector_sum[4:5, : 2 * width - both]], axis=1), bias_grad)
        own(lambda_re, real_grad)
        own(lambda_im, rotation_grad)
        own(step_grad, timestep_grad)


def whole(shape):
    return pl.BlockSpec(shape, lambda i: (0,) * len(shape), pipeline_mode=pl.Buffered(1))


def total_of(shape):
    return pl.BlockSpec(shape, lambda i: (0,) * len(shape))


def tiled(rows, columns):
    return pl.BlockSpec((rows, columns), lambda i: (i, 0))


def params(cid=None):
    if cid is None:
        return pltpu.CompilerParams(dimension_semantics=("arbitrary",), vmem_limit_bytes=VMEM_LIMIT)
    return pltpu.CompilerParams(
        dimension_semantics=("arbitrary",), vmem_limit_bytes=VMEM_LIMIT, collective_id=cid, has_side_effects=True
    )


def body(
    tokens, cotangent, block_target, sequence_lengths, norm_gain, norm_shift, decay_real, decay_rotation,
    log_timestep, drive_matrix, readout_matrix, feedthrough, mixer_weight, mixer_bias,
):
    members = lax.axis_size("fsdp")
    grid = Grid(lax.axis_size("dp"), members)
    blocks = block_target.shape[0]
    rows, width = tokens.shape
    both = drive_matrix.shape[1]
    states = both // 2
    block_rows = rows // blocks
    span = SUB * block_rows
    tile = 2 * span
    tiles = rows // tile
    tile_blocks = tile // block_rows
    total = blocks * members
    sequences = sequence_lengths.shape[1]
    shape = jax.ShapeDtypeStruct
    anywhere = pl.BlockSpec(memory_space=pl.ANY)
    regular = pltpu.SemaphoreType.DMA

    order = np.arange(span)
    source = (order % SUB) * block_rows + order // SUB
    perm = jnp.asarray(source[:, None] == order[None], BF16)
    back = jnp.asarray(order[:, None] == source[None], BF16)

    def early(rows_of, columns):
        return pl.BlockSpec((rows_of, columns), lambda i: (jnp.minimum(i, tiles - 1), 0))

    def late(rows_of, columns):
        return pl.BlockSpec((rows_of, columns), lambda i: (jnp.clip(i - tiles, 0, tiles - 1), 0))

    def flat(size):
        return pl.BlockSpec((size,), lambda i: (0,))

    small = (norm_gain, norm_shift, feedthrough, mixer_bias, decay_real, decay_rotation, log_timestep, block_target)
    counts = tuple(v.shape[0] for v in small)
    shards = (drive_matrix, readout_matrix, mixer_weight)
    slots = grid.slots

    def shifted(rows_of, columns):
        return pl.BlockSpec((rows_of, columns), lambda i: (jnp.clip(i - 1, 0, tiles - 1), 0))

    dealt, driven, keep, carry, drive, drive_raw, readout, mixer, vectors, rates, place, own_place, broken = pl.pallas_call(
        functools.partial(front_kernel, grid, block_rows, counts, tile),
        grid=(tiles + 2,),
        in_specs=[anywhere]
        + [flat(size) for size in counts]
        + [whole((1, sequences)), anywhere, anywhere, anywhere, whole((span, span))],
        out_specs=[
            shifted(tile, width), shifted(tile, both), shifted(tile, LANES), total_of((blocks, both)),
            total_of((width, both)),
            total_of((width, both)), anywhere, anywhere, total_of((SUB, 2 * width)), total_of((SUB, states)),
            total_of((1, total)), total_of((blocks, LANES)), total_of((sequences, members, LANES)),
        ],
        out_shape=[
            shape((rows, width), BF16), shape((rows, both), F32), shape((rows, LANES), F32), shape((blocks, both), F32),
            shape((width, both), BF16), shape((width, both), BF16),
            shape(grid.shape + readout_matrix.shape, BF16), shape(grid.shape + mixer_weight.shape, BF16),
            shape((SUB, 2 * width), F32), shape((SUB, states), F32), shape((1, total), F32),
            shape((blocks, LANES), F32), shape((sequences, members, LANES), jnp.int32),
        ],
        scratch_shapes=[
            pltpu.VMEM((rows, width), BF16),
            pltpu.VMEM((rows, width), BF16),
            pltpu.VMEM((rows, width), F32),
            pltpu.VMEM(grid.shape + (SUB, LANES), F32),
            pltpu.VMEM(grid.shape + drive_matrix.shape, BF16),
            pltpu.VMEM((blocks, LANES), jnp.int32),
            pltpu.VMEM((members, blocks, both), BF16),
            pltpu.VMEM((total, both), F32),
            regular((4 * slots,)), regular((4 * slots,)), regular((len(shards) + tiles,)), regular((members,)),
            regular((members,)),
        ],
        compiler_params=params(0),
        name="front",
    )(tokens, *small, sequence_lengths, *shards, perm)
    readout = readout.reshape(both, width)
    mixer = mixer.reshape(width, 2 * width)

    gated_low, mixed_low, joined, joined_grad, weight_grad, bias_grad, through_grad, readout_grad, mixed_sum, coming = pl.pallas_call(
        functools.partial(main_kernel, grid, block_rows),
        grid=(tiles + 1,),
        in_specs=[
            early(tile, width), early(tile, width), early(tile, both), early(tile_blocks, both),
            early(tile, LANES), whole((SUB, states)), whole((both, width)), whole((SUB, 2 * width)),
            whole((width, 2 * width)), whole((span, span)), whole((span, span)), whole((1, total)),
            whole((blocks, LANES)), whole((sequences, members, LANES)),
        ],
        out_specs=[
            early(tile, width), early(tile, width), early(tile, both), early(tile, both),
            total_of((width, 2 * width)), total_of((1, 2 * width)), total_of((1, width)), total_of((both, width)),
            total_of((1, width)), total_of((blocks, both)),
        ],
        out_shape=[
            shape((rows, width), BF16), shape((rows, width), BF16), shape((rows, both), BF16),
            shape((rows, both), F32), shape((width, 2 * width), F32), shape((1, 2 * width), F32),
            shape((1, width), F32), shape((both, width), F32), shape((1, width), F32), shape((blocks, both), F32),
        ],
        scratch_shapes=[
            pltpu.VMEM((members, blocks, both), BF16), pltpu.VMEM((total, both), F32), regular((members - 1,)),
            regular((members - 1,)),
        ],
        compiler_params=params(1),
        name="main",
    )(cotangent, dealt, driven, carry, keep, rates, readout, vectors, mixer, perm, back, place, own_place, broken)

    orders = ((2, 0, 1), (2, 1, 0), (2, 1, 0))
    weights = (readout_matrix, mixer_weight, drive_matrix)
    buffers = []
    for turn, weight in zip(orders, weights):
        for dim, _, left in reduce_plan(grid, turn):
            buffers.append(pltpu.VMEM((grid.fan(dim),) + tuple(grid.shape[d] for d in left) + weight.shape, BF16))
    token_part, drive_sum, readout_sum, weight_sum, vector_sum = pl.pallas_call(
        functools.partial(last_kernel, grid, block_rows, orders),
        grid=(2 * tiles + 1,),
        in_specs=[
            early(tile, width), early(tile, both), early(tile, both), early(tile_blocks, both), early(tile_blocks, both),
            early(tile, LANES), late(tile, width), late(tile, width), whole((SUB, states)), whole((SUB, 2 * width)),
            whole((width, both)), whole((width, both)), whole((span, span)), whole(grid.shape + readout_matrix.shape),
            whole(grid.shape + mixer_weight.shape), whole((1, 2 * width)), whole((1, width)), whole((1, width)),
        ],
        out_specs=[
            late(tile, width), total_of(drive_matrix.shape), total_of(readout_matrix.shape),
            total_of(mixer_weight.shape), total_of((SUB, both)),
        ],
        out_shape=[
            shape((rows, width), BF16), shape(drive_matrix.shape, F32), shape(readout_matrix.shape, F32),
            shape(mixer_weight.shape, F32), shape((SUB, both), F32),
        ],
        scratch_shapes=[
            pltpu.VMEM((rows, both), BF16), pltpu.VMEM((width, both), F32),
            pltpu.VMEM(grid.shape + drive_matrix.shape, F32), pltpu.VMEM((SUB, both), F32),
            pltpu.VMEM((SUB, both), F32),
        ]
        + [pltpu.VMEM(grid.shape[:-1] + weight.shape, F32) for weight in weights]
        + buffers
        + buffers
        + [
            pltpu.VMEM((SUB, both), F32), pltpu.VMEM((members - 1, SUB, both), F32),
            pltpu.VMEM((grid.dp - 1, SUB, both), F32), regular((3 * slots,)), regular((3 * slots,)),
            regular((members + grid.dp - 2,)), regular((members + grid.dp - 2,)),
        ],
        compiler_params=params(2),
        name="last",
    )(
        dealt, joined, joined_grad, carry, coming, keep, mixed_low, tokens, rates, vectors, drive, drive_raw, back,
        readout_grad.reshape(grid.shape + readout_matrix.shape), weight_grad.reshape(grid.shape + mixer_weight.shape),
        bias_grad, through_grad, mixed_sum,
    )

    vector_sizes = [v.shape[0] for v in (norm_gain, norm_shift, decay_real, decay_rotation, log_timestep)]
    slab = 2 * tile
    outs = pl.pallas_call(
        functools.partial(tail_kernel, grid),
        grid=(rows // slab,),
        in_specs=[tiled(slab, width)] * 4
        + [
            whole((SUB, states)), whole(drive_matrix.shape), whole(readout_matrix.shape),
            whole(mixer_weight.shape), whole((SUB, both)),
        ],
        out_specs=[tiled(slab, width)] * 2
        + [flat(size) for size in vector_sizes]
        + [
            total_of(drive_matrix.shape), total_of(readout_matrix.shape), flat(feedthrough.shape[0]),
            total_of(mixer_weight.shape), flat(mixer_bias.shape[0]),
        ],
        out_shape=[shape((rows, width), F32)] * 2
        + [shape((size,), F32) for size in vector_sizes]
        + [
            shape(drive_matrix.shape, F32), shape(readout_matrix.shape, F32), shape(feedthrough.shape, F32),
            shape(mixer_weight.shape, F32), shape(mixer_bias.shape, F32),
        ],
        compiler_params=params(),
        name="tail",
    )(tokens, cotangent, token_part, gated_low, rates, drive_sum, readout_sum, weight_sum, vector_sum)
    return tuple(outs)


def solution(mesh):
    rows = P(AXES, None)
    flat = P(AXES)
    return jax.shard_map(
        body,
        mesh=mesh,
        in_specs=(rows, rows, flat, rows, flat, flat, flat, flat, flat, rows, rows, flat, rows, flat),
        out_specs=(rows, rows, flat, flat, flat, flat, flat, rows, rows, flat, rows, flat),
        check_vma=False,
    )
```

```python
import functools
import itertools

import jax
import jax.numpy as jnp
import numpy as np
from jax import lax
from jax.experimental import pallas as pl
from jax.experimental.pallas import tpu as pltpu
from jax.sharding import PartitionSpec as P

EPSILON = 1e-05
AXES = ("dp", "fsdp")
F32 = jnp.float32
BF16 = jnp.bfloat16
LANES = 128
SUB = 8
VMEM_LIMIT = 63 * 1024 * 1024


def dot(left, right):
    return jnp.dot(left, right, preferred_element_type=F32)


def contract_rows(left, right):
    return lax.dot_general(left, right, (((0,), (0,)), ((), ())), preferred_element_type=F32)


def contract_cols(left, right):
    return lax.dot_general(left, right, (((1,), (1,)), ((), ())), preferred_element_type=F32)


def lanes_to(mask, width):
    return jnp.concatenate([mask] * (width // LANES), axis=1)


def spread(vector, rows):
    return jnp.broadcast_to(vector, (rows, vector.shape[1]))


def gelu_parts(v):
    cdf = 0.5 + 0.5 * lax.erf(v * 0.7071067811865476)
    density = 0.3989422804014327 * jnp.exp(-0.5 * v * v)
    return v * cdf, cdf + v * density


def permute_tile(perm, tile, span):
    return jnp.concatenate(
        [dot(perm, tile[i * span : (i + 1) * span]) for i in range(tile.shape[0] // span)], axis=0
    )


def norm_stats(rows):
    center = jnp.mean(rows, axis=-1, keepdims=True)
    moved = rows - center
    spread_of = jnp.mean(moved * moved, axis=-1, keepdims=True)
    return moved, lax.rsqrt(spread_of + EPSILON)


MESH = pl.DeviceIdType.MESH


class Grid:
    def __init__(self, dp, members):
        self.dp, self.members = dp, members
        self.shape = (dp, members // 2, 2)
        self.slots = dp - 1 + members // 2 - 1 + 1

    def here(self):
        row, column = lax.axis_index("dp"), lax.axis_index("fsdp")
        return row, column, (row, lax.div(column, 2), lax.rem(column, 2))

    def fan(self, dim):
        return self.shape[dim] - 1

    def peers(self, dim):
        row, column, mine = self.here()
        found = []
        for away in range(1, self.shape[dim]):
            index = lax.rem(mine[dim] + away, self.shape[dim])
            if dim == 0:
                device = {"dp": index}
            elif dim == 1:
                device = {"fsdp": 2 * index + mine[2]}
            else:
                device = {"fsdp": 2 * mine[1] + index}
            found.append((away - 1, device, index))
        return found


def others(grid, everyone):
    row, column, _ = grid.here()
    found = []
    for down in range(grid.dp):
        for away in range(grid.members):
            if (down or away) and (everyone or not (down and away)):
                found.append({"dp": lax.rem(row + down, grid.dp), "fsdp": lax.rem(column + away, grid.members)})
    return found


def announce(grid, everyone=False):
    barrier = pltpu.get_barrier_semaphore()
    for device in others(grid, everyone):
        pl.semaphore_signal(barrier, inc=1, device_id=device, device_id_type=MESH)


def meet(grid, everyone=False):
    count = grid.dp * grid.members - 1 if everyone else grid.dp + grid.members - 2
    pl.semaphore_wait(pltpu.get_barrier_semaphore(), count)


def remote(source, target, send, recv, device):
    return pltpu.make_async_remote_copy(
        src_ref=source, dst_ref=target, send_sem=send, recv_sem=recv, device_id=device, device_id_type=MESH
    )


def gather_phase(grid, ref, cut, axes, dim, done, send, recv, base):
    _, _, mine = grid.here()
    at = tuple(slice(None) if d in done else mine[d] for d in axes)
    if cut is not None:
        at = at + (slice(None), cut)
    return [
        pltpu.make_async_remote_copy(
            src_ref=ref.at[at], dst_ref=ref.at[at], send_sem=send.at[base + slot], recv_sem=recv.at[base + slot],
            device_id=device, device_id_type=MESH,
        )
        for slot, device, _ in grid.peers(dim)
    ]


def reduce_plan(grid, order):
    plan = []
    for phase, dim in enumerate(order):
        done = order[:phase]
        left = tuple(d for d in range(len(grid.shape)) if d not in done and d != dim)
        plan.append((dim, done, left))
    return plan


def lane_index(width):
    return lax.broadcasted_iota(jnp.int32, (1, width), 1).astype(F32)


def unpack(rows, row, count, width):
    lanes = lane_index(width)
    owner = jnp.floor((lanes + 0.5) * (1.0 / count))
    inner = lanes - count * owner
    taken = lax.broadcasted_iota(jnp.int32, (LANES, width), 0).astype(F32) == inner
    spread_out = dot(rows.astype(BF16), jnp.where(taken, 1.0, 0.0).astype(BF16))
    index = lax.broadcasted_iota(jnp.int32, (rows.shape[0], width), 0).astype(F32)
    return jnp.sum(jnp.where(index == owner * SUB + row, spread_out, 0.0), axis=0, keepdims=True)


def rates_of(real, rotation, step_log):
    timestep = jnp.exp(step_log)
    magnitude = jnp.exp(real * timestep)
    turned = rotation * timestep
    factor_re = magnitude * jnp.cos(turned)
    factor_im = magnitude * jnp.sin(turned)
    modulus = real * real + rotation * rotation
    scale_re = ((factor_re - 1.0) * real + factor_im * rotation) / modulus
    scale_im = (factor_im * real - (factor_re - 1.0) * rotation) / modulus
    return timestep, factor_re, factor_im, modulus, scale_re, scale_im


def cross_blocks(members, reverse, arrive, pieces, place, own_place, broken, flow_re, flow_im, chosen, dealt, carries):
    states = flow_re.shape[1]
    total = place.shape[1]
    steps = total // members
    chunk = chosen.shape[0]

    def choose(at):
        rows = lax.broadcasted_iota(jnp.int32, (chunk, total), 0).astype(F32) + float(at)
        return jnp.where(rows == place[...], 1.0, 0.0).astype(BF16)

    chosen[...] = choose(0)
    arrive()
    for at in range(0, total, chunk):
        if at:
            chosen[...] = choose(at)
        dealt[at : at + chunk, :] = dot(chosen[...], pieces[...].reshape(total, 2 * states))
    rate_re = spread(flow_re, members)
    rate_im = spread(-flow_im if reverse else flow_im, members)
    marks = [broken[s] for s in range(broken.shape[0])]

    def step(i, state):
        re, im = state
        p = steps - 1 - i if reverse else i
        at = pl.multiple_of(p * members, members)
        here = dealt[pl.ds(at, members), :]
        met = marks[0] == p
        for mark in marks[1:]:
            met = met | (mark == p)
        mask = lanes_to(jnp.where(met, 0.0, 1.0), states)
        dealt[pl.ds(at, members), :] = jnp.concatenate([re, im], axis=1)
        return (
            mask * (rate_re * re - rate_im * im) + here[:, :states],
            mask * (rate_re * im + rate_im * re) + here[:, states:],
        )

    zero = jnp.zeros((members, states), F32)
    lax.fori_loop(0, steps, step, (zero, zero), unroll=4)
    own = own_place.shape[0]
    step_rows = min(total, 1024)
    found = jnp.zeros((own, 2 * states), F32)
    for at in range(0, total, step_rows):
        columns = lax.broadcasted_iota(jnp.int32, (own, step_rows), 1).astype(F32) + float(at)
        taken = jnp.where(columns == lanes_to(own_place[...], step_rows), 1.0, 0.0).astype(BF16)
        entering = dealt[at : at + step_rows, :]
        high = entering.astype(BF16)
        low = (entering - high.astype(F32)).astype(BF16)
        found = found + (dot(taken, high) + dot(taken, low))
    carries[...] = found


def front_kernel(
    grid, block_rows, counts, tile, tokens, cotangent, gain_s, shift_s, through_s, bias_s, real_s, rotation_s, step_s, target_s,
    lengths_s, drive_s, readout_s, mixer_s, perm,
    dealt, rows_p, cot_p, driven, keep, carries, drive, drive_raw, readout_w, mixer_w, vectors, rates, place, own_place, broken,
    rows_in, normed, xhat, table, drive_w, bits, pieces, chosen, dealt_ends, send, recv, local, push_send, push_recv,
    table_send, table_recv,
):
    i = pl.program_id(0)
    tiles = pl.num_programs(0) - 2
    row, column, mine = grid.here()
    members = grid.members
    blocks = target_s.shape[0]
    width = tokens.shape[1]
    both = drive.shape[1]
    states = both // 2
    span = SUB * block_rows
    chains = tile // span
    tile_blocks = tile // block_rows
    axes = tuple(range(len(grid.shape)))
    half = mixer_w.shape[-1] // 2
    wholes = (drive_w, readout_w, mixer_w, mixer_w)
    cuts = (None, None, pl.ds(0, half), pl.ds(half, half))
    orders = ((0, 1, 2), (1, 0, 2), (1, 0, 2), (0, 1, 2))
    phases = 3

    def phase_copies(k, phase):
        order = orders[k]
        base = k * grid.slots + sum(grid.fan(d) for d in order[:phase])
        return gather_phase(grid, wholes[k], cuts[k], axes, order[phase], order[:phase], send, recv, base)

    def table_copies():
        return [
            remote(table.at[mine], table.at[mine], table_send.at[k], table_recv.at[k], device)
            for k, device in enumerate(others(grid, True))
        ]

    def advance(ks, phase):
        for k in ks:
            if phase:
                for copy in phase_copies(k, phase - 1):
                    copy.wait()
            if phase < phases:
                for copy in phase_copies(k, phase):
                    copy.start()

    @pl.when(i == 0)
    def _():
        copies = [
            pltpu.make_async_copy(shard, ref.at[tuple(mine)], local.at[k])
            for k, (shard, ref) in enumerate(zip((drive_s, readout_s, mixer_s), wholes))
        ]
        for copy in copies:
            copy.start()
        held = [gain_s, shift_s, through_s, bias_s, real_s, rotation_s, step_s, target_s]
        own = table.at[tuple(mine)]
        own[...] = jnp.zeros_like(own)
        for k, ref in enumerate(held):
            own[k : k + 1, : ref.shape[0]] = ref[...].astype(F32).reshape(1, ref.shape[0])
        sequences = lengths_s.shape[1]
        own[4:5, LANES // 2 : LANES // 2 + sequences] = lengths_s[...].astype(F32)
        announce(grid, True)
        chunks = [
            pltpu.make_async_copy(
                tokens.at[pl.ds(j * tile, tile)], rows_in.at[pl.ds(j * tile, tile)], local.at[len(copies) + j]
            )
            for j in range(tiles)
        ]
        for copy in chunks:
            copy.start()
        for copy in copies:
            copy.wait()
        meet(grid, True)
        advance((0,), 0)
        for copy in table_copies():
            copy.start()
        advance((1, 2), 0)

        def stats(j, _):
            at = pl.ds(pl.multiple_of(j * tile, tile), tile)
            turned = permute_tile(perm[...], rows_in[at, :], span)
            rows_in[at, :] = turned.astype(BF16)
            moved, rstd = norm_stats(turned)
            xhat[at, :] = moved * rstd
            return 0

        for copy in chunks[: tiles // 2]:
            copy.wait()
        lax.fori_loop(0, tiles // 2, stats, 0)
        advance((0,), 1)
        advance((3,), 0)
        advance((1, 2), 1)
        for copy in chunks[tiles // 2 :]:
            copy.wait()
        lax.fori_loop(tiles // 2, tiles, stats, 0)
        for copy in table_copies():
            copy.wait()
        rows = table[...].reshape(-1, LANES)
        vectors[...] = jnp.zeros_like(vectors)
        for k, size in enumerate((width, width, width, 2 * width)):
            vectors[k : k + 1, :size] = unpack(rows, k, counts[k], size)
        real, rotation, step_log = [unpack(rows, k, counts[k], states) for k in (4, 5, 6)]
        _, factor_re, factor_im, _, scale_re, scale_im = rates_of(real, rotation, step_log)
        flow_re, flow_im = factor_re, factor_im
        power = 1
        while power < block_rows:
            flow_re, flow_im = flow_re * flow_re - flow_im * flow_im, 2.0 * flow_re * flow_im
            power *= 2
        for k, value in enumerate((factor_re, factor_im, flow_re, flow_im, real, rotation, step_log)):
            rates[k : k + 1, :] = value
        group = table[row].reshape(members * SUB, LANES)
        for m in range(members):
            q = group[m * SUB + 7 : m * SUB + 8, :blocks]
            d = jnp.floor(q * (1.0 / blocks))
            place[:, m * blocks : (m + 1) * blocks] = (q - d * blocks) * members + d
        lengths = jnp.concatenate([group[m * SUB + 4 : m * SUB + 5, :] for m in range(members)], axis=0)
        sequences = lengths_s.shape[1]
        q = table[tuple(mine) + (slice(7, 8), slice(None))]
        diagonal = lax.broadcasted_iota(jnp.int32, (blocks, LANES), 0) == lax.broadcasted_iota(
            jnp.int32, (blocks, LANES), 1
        )
        q = jnp.sum(jnp.where(diagonal, jnp.broadcast_to(q, (blocks, LANES)), 0.0), axis=1, keepdims=True)
        q = jnp.broadcast_to(q, (blocks, LANES))
        d = jnp.floor(q * (1.0 / blocks))
        p = q - d * blocks
        own_place[...] = p * members + d
        start = jnp.zeros((members, LANES), F32)
        marks = jnp.zeros((blocks, LANES), jnp.int32)
        for s in range(sequences):
            broken[s] = jnp.floor(start * (1.0 / block_rows)).astype(jnp.int32)
            mark = jnp.zeros((blocks, LANES), F32)
            for m in range(members):
                mark = jnp.where(d == float(m), jnp.broadcast_to(start[m : m + 1, :], (blocks, LANES)), mark)
            mark = mark - p * block_rows
            inside = (mark >= 0.0) & (mark < block_rows)
            shift = jnp.where(inside, mark, 0.0).astype(jnp.int32)
            marks = marks | jnp.where(inside, lax.shift_left(jnp.ones_like(shift), shift), 0)
            column_of = lengths[:, LANES // 2 + s : LANES // 2 + s + 1]
            start = start + jnp.broadcast_to(column_of, (members, LANES))
        bits[...] = marks
        gain = vectors[0:1, :width]
        shift_by = vectors[1:2, :width]

        def settle(j, _):
            at = pl.ds(pl.multiple_of(j * tile, tile), tile)
            normed[at, :] = (xhat[at, :] * gain + shift_by).astype(BF16)
            return 0

        advance((0,), 2)
        lax.fori_loop(0, tiles, settle, 0)
        advance((0,), 3)
        advance((3,), 1)
        drive_raw[...] = drive_w[...].reshape(width, both)
        raw = drive_raw[...].astype(F32)
        drive[:, :states] = (scale_re * raw[:, :states] - scale_im * raw[:, states:]).astype(BF16)
        drive[:, states:] = (scale_re * raw[:, states:] + scale_im * raw[:, :states]).astype(BF16)

    def push_far(at):
        return [
            remote(pieces.at[at], pieces.at[at], push_send.at[slot], push_recv.at[slot], device)
            for slot, device, _ in grid.peers(1)
        ]

    def push_near(at, slot):
        device = grid.peers(2)[0][1]
        return remote(pieces.at[at], pieces.at[at], push_send.at[slot], push_recv.at[slot], device)

    far = grid.fan(1)

    @pl.when((i >= 1) & (i <= tiles))
    def _():
        j = i - 1
        dealt[...] = normed[pl.ds(pl.multiple_of(j * tile, tile), tile), :]
        rows_p[...] = rows_in[pl.ds(pl.multiple_of(j * tile, tile), tile), :]
        cot_p[...] = permute_tile(perm[...], cotangent[...], span).astype(BF16)
        driven[...] = dot(dealt[...], drive[...])
        rate_re = spread(rates[0:1, :], SUB)
        rate_im = spread(rates[1:2, :], SUB)
        first = pl.multiple_of(j * tile_blocks, tile_blocks)
        mark = bits[pl.ds(first, tile_blocks), :]
        state = [(jnp.zeros((SUB, states), F32), jnp.zeros((SUB, states), F32)) for _ in range(chains)]
        for t in range(block_rows):
            single = 1 << t if t < 31 else -(1 << 31)
            for c in range(chains):
                at = c * span + t * SUB
                narrow = jnp.where((mark[c * SUB : (c + 1) * SUB] & single) == 0, 1.0, 0.0)
                keep[at : at + SUB, :] = narrow
                mask = lanes_to(narrow, states)
                re, im = state[c]
                now_re = mask * (rate_re * re - rate_im * im) + driven[at : at + SUB, :states]
                now_im = mask * (rate_re * im + rate_im * re) + driven[at : at + SUB, states:]
                state[c] = (now_re, now_im)
        ends = jnp.concatenate([jnp.concatenate(state[c], axis=1) for c in range(chains)], axis=0)
        pieces[column, pl.ds(first, tile_blocks), :] = ends.astype(BF16)
        at = (column, pl.ds(first, tile_blocks))
        for copy in push_far(at) + [push_near(at, far)]:
            copy.start()

    @pl.when(i == tiles + 1)
    def _():
        def arrive():
            onward = []
            for k, copy in enumerate(push_far((column,))):
                copy.wait()
                there = 2 * lax.rem(mine[1] + grid.shape[1] - 1 - k, grid.shape[1]) + mine[2]
                onward.append(push_near((there,), far + 1 + k))
                onward[-1].start()
            advance((1, 2, 3), 2)
            push_near((column,), far).wait()
            for copy in onward:
                copy.wait()

        cross_blocks(
            members, False, arrive, pieces, place, own_place, broken, rates[2:3, :], rates[3:4, :], chosen, dealt_ends,
            carries,
        )
        advance((1, 2, 3), phases)


def split(values):
    high = values.astype(BF16)
    rest = values - high.astype(F32)
    middle = rest.astype(BF16)
    return high, middle, (rest - middle.astype(F32)).astype(BF16)


def row_times(row, matrix):
    wide = [jnp.broadcast_to(piece.astype(F32), (SUB, row.shape[1])).astype(BF16) for piece in split(row)]
    return sum(contract_cols(piece, matrix) for piece in wide)[0:1]


def row_sums(matrix):
    ones = jnp.ones((SUB, matrix.shape[1]), BF16)
    return sum(contract_cols(ones, piece) for piece in split(matrix))[0:1]


def back_kernel(
    grid, block_rows, orders, cotangent, dealt, driven, carry, keep, rows_p, rates, readout, vectors, mixer, place,
    own_place, broken, drive, drive_raw,
    gated_low, token_part, drive_sum, readout_sum, weight_sum, vector_sum,
    joined_all, joined_grad_all, mixed_all, coming, weight_grad, bias_grad, through_grad, readout_grad, mixed_sum,
    drive_grad, decay_cot, driven_sum, pieces, chosen, dealt_heads, push_send, push_recv, *rest,
):
    i = pl.program_id(0)
    tiles = (pl.num_programs(0) - 2) // 3
    row, column, mine = grid.here()
    members = grid.members
    core = 2
    phases = 3
    span = SUB * block_rows
    tile, width = cotangent.shape
    both = joined_all.shape[1]
    states = both // 2
    chains = tile // span
    tile_blocks = tile // block_rows
    rest = list(rest)
    parts = (readout_grad, weight_grad, drive_grad)
    outs = (readout_sum, weight_sum, drive_sum)
    count = len(parts)
    accs = [rest.pop(0) for _ in range(count)]
    stages = [[rest.pop(0) for _ in range(phases)] for _ in range(count)]
    landed = [[rest.pop(0) for _ in range(phases)] for _ in range(count)]
    vector_stage, across, along, send, recv, vector_send, vector_recv = rest
    plans = [reduce_plan(grid, order) for order in orders]
    every = (0, 1, 2)
    kept = every[:-1]
    first_a = tiles + 1
    first_b = 2 * tiles + 1

    def push_to(at):
        return [
            remote(
                pieces.at[at], pieces.at[at], push_send.at[away - 1], push_recv.at[away - 1],
                {"fsdp": lax.rem(column + away, members)},
            )
            for away in range(1, members)
        ]

    def combos(left):
        return list(itertools.product(*[range(grid.shape[d]) for d in left]))

    def at_of(dim, index, left, combo, dims):
        chosen_of = dict(zip(left, combo))
        chosen_of[dim] = index
        return tuple(chosen_of[d] if d in chosen_of else mine[d] for d in dims)

    def piece_of(k, dim, index, left, combo):
        if dim != core:
            return accs[k][at_of(dim, index, left, combo, kept)]
        size = outs[k].shape[0]
        down, half, low = at_of(dim, index, left, combo, every)
        start = ((down * grid.shape[1] + half) * 2 + low) * size
        if size % SUB == 0:
            return parts[k][pl.ds(pl.multiple_of(start, size), size), :]
        low_row = jnp.minimum(lax.div(start, SUB) * SUB, parts[k].shape[0] - 2 * SUB)
        window = parts[k][pl.ds(pl.multiple_of(low_row, SUB), 2 * SUB), :]
        return pltpu.roll(window, lax.rem(2 * SUB - (start - low_row), 2 * SUB), 0)[:size]

    def hops(k, phase):
        dim = plans[k][phase][0]
        base = k * grid.slots + sum(grid.fan(d) for d in orders[k][:phase])
        return [
            (
                remote(
                    stages[k][phase].at[slot], landed[k][phase].at[slot], send.at[base + slot], recv.at[base + slot],
                    device,
                ),
                slot,
                index,
            )
            for slot, device, index in grid.peers(dim)
        ]

    def begin(k, phase):
        dim, _, left = plans[k][phase]
        for copy, slot, index in hops(k, phase):
            for combo in combos(left):
                stages[k][phase][(slot,) + combo] = piece_of(k, dim, index, left, combo).astype(BF16)
            copy.start()

    def finish(k, phase):
        dim, _, left = plans[k][phase]
        copies = hops(k, phase)
        for copy, _, _ in copies:
            copy.wait()
        for combo in combos(left):
            piece = piece_of(k, dim, mine[dim], left, combo)
            for _, slot, _ in copies:
                piece = piece + landed[k][phase][(slot,) + combo].astype(F32)
            accs[k][at_of(dim, mine[dim], left, combo, kept)] = piece

    def advance(ks, phase):
        for k in ks:
            if phase:
                finish(k, phase - 1)
            if phase < phases:
                begin(k, phase)
            else:
                outs[k][...] = accs[k][mine[:-1]]

    def vector_across():
        return [
            remote(
                vector_stage, across.at[away - 1], vector_send.at[away - 1], vector_recv.at[away - 1],
                {"fsdp": lax.rem(column + away, members)},
            )
            for away in range(1, members)
        ]

    def vector_along():
        return [
            remote(
                vector_sum, along.at[slot], vector_send.at[members - 1 + slot], vector_recv.at[members - 1 + slot], device
            )
            for slot, device, _ in grid.peers(0)
        ]

    rate_re = spread(rates[0:1, :], SUB)
    rate_im = spread(rates[1:2, :], SUB)

    @pl.when(i == 0)
    def _():
        for total in (
            weight_grad, bias_grad, through_grad, readout_grad, mixed_sum, drive_grad, decay_cot, driven_sum
        ):
            total[...] = jnp.zeros_like(total)
        announce(grid)

    @pl.when(i < tiles)
    def _():
        through = vectors[2:3, :width]
        bias = vectors[3:4, : 2 * width]
        here = pl.ds(pl.multiple_of(i * tile, tile), tile)
        joined = joined_all.at[here]
        joined_grad = joined_grad_all.at[here]
        state = [
            (carry[c * SUB : (c + 1) * SUB, :states], carry[c * SUB : (c + 1) * SUB, states:])
            for c in range(chains)
        ]
        for t in range(0, block_rows, 2):
            for c in range(chains):
                held = []
                for step in (t, t + 1):
                    at = c * span + step * SUB
                    mask = lanes_to(keep[at : at + SUB, :], states)
                    re, im = state[c]
                    now_re = mask * (rate_re * re - rate_im * im) + driven[at : at + SUB, :states]
                    now_im = mask * (rate_re * im + rate_im * re) + driven[at : at + SUB, states:]
                    state[c] = (now_re, now_im)
                    held.append(state[c])
                at = c * span + t * SUB
                joined[at : at + 2 * SUB, :states] = jnp.concatenate([held[0][0], held[1][0]], axis=0).astype(BF16)
                joined[at : at + 2 * SUB, states:] = (-jnp.concatenate([held[0][1], held[1][1]], axis=0)).astype(BF16)

        dealt_f32 = dealt[...].astype(F32)
        mixed = dot(joined[...], readout[...]) + through * dealt_f32
        activated, slope = gelu_parts(mixed)
        features = activated.astype(BF16)
        hidden = dot(features, mixer[...]) + bias
        value = hidden[:, :width]
        sig = 0.5 + 0.5 * jnp.tanh(0.5 * hidden[:, width:])
        gated_low[...] = (value * sig).astype(BF16)
        cot_sig = cotangent[...].astype(F32) * sig
        hidden_low = jnp.concatenate(
            [cot_sig.astype(BF16), (cot_sig * value * (1.0 - sig)).astype(BF16)], axis=1
        )
        weight_grad[...] += contract_rows(features, hidden_low)
        bias_grad[...] += jnp.sum(hidden_low.astype(F32), axis=0, keepdims=True)
        feature_grad = contract_cols(hidden_low, mixer[...]).astype(BF16)
        mixed_grad = (feature_grad.astype(F32) * slope).astype(BF16)
        mixed_all[here, :] = mixed_grad
        mixed_f32 = mixed_grad.astype(F32)
        through_grad[...] += jnp.sum(mixed_f32 * dealt_f32, axis=0, keepdims=True)
        mixed_sum[...] += jnp.sum(mixed_f32, axis=0, keepdims=True)
        readout_grad[...] += contract_rows(joined[...], mixed_grad)
        joined_grad[...] = contract_cols(mixed_grad, readout[...])

        going = [(jnp.zeros((SUB, states), F32), jnp.zeros((SUB, states), F32)) for _ in range(chains)]
        for t in reversed(range(block_rows)):
            for c in range(chains):
                at = c * span + t * SUB
                mask = lanes_to(keep[at : at + SUB, :], states)
                re = joined_grad[at : at + SUB, :states] + going[c][0]
                im = going[c][1] - joined_grad[at : at + SUB, states:]
                going[c] = (mask * (rate_re * re + rate_im * im), mask * (rate_re * im - rate_im * re))
        heads = jnp.concatenate([jnp.concatenate(going[c], axis=1) for c in range(chains)], axis=0)
        at = (column, pl.ds(pl.multiple_of(i * tile_blocks, tile_blocks), tile_blocks))
        pieces[at + (slice(None),)] = heads.astype(BF16)

        @pl.when(i == 0)
        def _():
            meet(grid)

        for copy in push_to(at):
            copy.start()

    @pl.when(i == tiles)
    def _():
        def arrive():
            advance((0, 1), 0)
            for copy in push_to((column,)):
                copy.wait()

        cross_blocks(
            members, True, arrive, pieces, place, own_place, broken, rates[2:3, :], rates[3:4, :], chosen, dealt_heads,
            coming,
        )
        advance((0, 1), 1)

    @pl.when(i == first_a + tiles // 2)
    def _():
        advance((1,), 2)

    @pl.when(i == first_a + tiles - 2)
    def _():
        advance((0,), 2)

    @pl.when(i == first_b)
    def _():
        advance((1,), 3)

    @pl.when(i == first_b + 2)
    def _():
        advance((0,), 3)

    @pl.when((i >= first_a) & (i < first_b))
    def _():
        j = first_b - 1 - i
        here = pl.ds(pl.multiple_of(j * tile, tile), tile)
        joined = joined_all.at[here]
        driven_low = joined
        joined_grad = joined_grad_all.at[here]
        entering = coming[pl.ds(pl.multiple_of(j * tile_blocks, tile_blocks), tile_blocks), :]
        going = [
            (entering[c * SUB : (c + 1) * SUB, :states], entering[c * SUB : (c + 1) * SUB, states:])
            for c in range(chains)
        ]
        total = [(jnp.zeros((SUB, states), F32), jnp.zeros((SUB, states), F32)) for _ in range(chains)]
        sums = list(total)
        for t in reversed(range(0, block_rows, 2)):
            for c in range(chains):
                pair = c * span + t * SUB
                here_re = joined[pair : pair + SUB, :states].astype(F32)
                here_im = -joined[pair : pair + SUB, states:].astype(F32)
                if t == 0:
                    past_re = carry[c * SUB : (c + 1) * SUB, :states]
                    past_im = carry[c * SUB : (c + 1) * SUB, states:]
                else:
                    past_re = joined[pair - SUB : pair, :states].astype(F32)
                    past_im = -joined[pair - SUB : pair, states:].astype(F32)
                held = {}
                for step, (prev_re, prev_im) in ((t + 1, (here_re, here_im)), (t, (past_re, past_im))):
                    where = c * span + step * SUB
                    mask = lanes_to(keep[where : where + SUB, :], states)
                    re = joined_grad[where : where + SUB, :states] + going[c][0]
                    im = going[c][1] - joined_grad[where : where + SUB, states:]
                    held[step] = (re, im)
                    sums[c] = (sums[c][0] + re, sums[c][1] + im)
                    on_re = mask * (rate_re * re + rate_im * im)
                    on_im = mask * (rate_re * im - rate_im * re)
                    going[c] = (on_re, on_im)
                    total[c] = (
                        total[c][0] + (on_re * prev_re + on_im * prev_im),
                        total[c][1] + (on_im * prev_re - on_re * prev_im),
                    )
                driven_low[pair : pair + 2 * SUB, :states] = jnp.concatenate(
                    [held[t][0], held[t + 1][0]], axis=0
                ).astype(BF16)
                driven_low[pair : pair + 2 * SUB, states:] = jnp.concatenate(
                    [held[t][1], held[t + 1][1]], axis=0
                ).astype(BF16)
        for c in range(chains):
            decay_cot[...] += jnp.concatenate(total[c], axis=1)
            driven_sum[...] += jnp.concatenate(sums[c], axis=1)
        drive_grad[...] += contract_rows(dealt[...], driven_low[...])

    @pl.when(i == first_b)
    def _():
        advance((2,), 0)
        cot = jnp.sum(decay_cot[...], axis=0, keepdims=True)
        factor_re, factor_im = rates[0:1, :], rates[1:2, :]
        size = factor_re * factor_re + factor_im * factor_im
        vector_stage[...] = jnp.zeros_like(vector_stage)
        through = vectors[2:3, :width]
        summed = jnp.sum(driven_sum[...], axis=0, keepdims=True)
        shift_sum = through * mixed_sum[...] + row_times(summed, drive[...])
        crossed = row_sums(drive[...].astype(F32) * drive_grad[...]) + through * through_grad[...]
        vector_stage[0:1, :width] = (crossed - vectors[1:2, :width] * shift_sum) / vectors[0:1, :width]
        vector_stage[1:2, :width] = shift_sum
        vector_stage[2:3, :width] = through_grad[...]
        vector_stage[3:4, :] = bias_grad[:, :both]
        vector_stage[4:5, : 2 * width - both] = bias_grad[:, both:]
        vector_stage[5:6, :states] = (cot[:, :states] * factor_re - cot[:, states:] * factor_im) / size
        vector_stage[5:6, states:] = (cot[:, :states] * factor_im + cot[:, states:] * factor_re) / size
        d_re, d_im = drive_grad[:, :states], drive_grad[:, states:]
        b_re, b_im = drive_raw[:, :states].astype(F32), drive_raw[:, states:].astype(F32)
        vector_stage[6:7, :states] = jnp.sum(d_re * b_re + d_im * b_im, axis=0, keepdims=True)
        vector_stage[6:7, states:] = jnp.sum(d_im * b_re - d_re * b_im, axis=0, keepdims=True)

        for copy in vector_across():
            copy.start()

    @pl.when(i == first_b + 1)
    def _():
        advance((2,), 1)

    @pl.when(i == first_b + 3)
    def _():
        for copy in vector_across():
            copy.wait()
        total = vector_stage[...]
        for k in range(members - 1):
            total = total + across[k]
        vector_sum[...] = total
        for copy in vector_along():
            copy.start()

    @pl.when(i == first_b + tiles - 2)
    def _():
        advance((2,), 2)

    @pl.when(i == first_b + tiles)
    def _():
        for copy in vector_along():
            copy.wait()
        total = vector_sum[...]
        for k in range(grid.dp - 1):
            total = total + along[k]
        vector_sum[...] = total
        advance((2,), 3)

    @pl.when((i >= first_b) & (i < first_b + tiles))
    def _():
        j = i - first_b
        here = pl.ds(pl.multiple_of(j * tile, tile), tile)
        driven_low = joined_all[here, :]
        normed_grad = vectors[2:3, :width] * mixed_all[here, :].astype(F32) + contract_cols(driven_low, drive[...])
        given = normed_grad.astype(BF16).astype(F32)
        moved, rstd = norm_stats(rows_p[...].astype(F32))
        xhat = moved * rstd
        scaled = given * vectors[0:1, :width]
        inner = jnp.mean(scaled * xhat, axis=-1, keepdims=True)
        token_part[...] = (
            rstd * (scaled - jnp.mean(scaled, axis=-1, keepdims=True) - xhat * inner)
        ).astype(BF16)


def tail_kernel(
    grid, span, tokens, cotangent, token_part, gated_low, back, rates, drive_sum, readout_sum, weight_sum, vector_sum,
    out, token_grad, gain_grad, shift_grad, real_grad, rotation_grad, timestep_grad, drive_grad, readout_grad,
    through_grad, weight_grad, bias_grad,
):
    width = tokens.shape[1]
    both = vector_sum.shape[1]
    states = both // 2
    out[...] = tokens[...].astype(F32) + permute_tile(back[...], gated_low[...], span)
    token_grad[...] = cotangent[...].astype(F32) + permute_tile(back[...], token_part[...], span)

    @pl.when(pl.program_id(0) == 0)
    def _():
        row, column, _ = grid.here()
        me = row * grid.members + column
        real, rotation, step_log = [rates[k : k + 1, :] for k in (4, 5, 6)]
        timestep, factor_re, factor_im, modulus, scale_re, scale_im = rates_of(real, rotation, step_log)
        d_re, d_im = drive_sum[:, :states], drive_sum[:, states:]
        drive_grad[:, :states] = scale_re * d_re + scale_im * d_im
        drive_grad[:, states:] = scale_re * d_im - scale_im * d_re
        readout_grad[...] = readout_sum[...]
        weight_grad[...] = weight_sum[...]
        s_re, s_im = vector_sum[6:7, :states], vector_sum[6:7, states:]
        total_re = vector_sum[5:6, :states] + (s_re * real - s_im * rotation) / modulus
        total_im = vector_sum[5:6, states:] + (s_re * rotation + s_im * real) / modulus
        ratio_re = (scale_re * real + scale_im * rotation) / modulus
        ratio_im = (scale_im * real - scale_re * rotation) / modulus
        lambda_re = timestep * (total_re * factor_re + total_im * factor_im) - (s_re * ratio_re + s_im * ratio_im)
        lambda_im = timestep * (total_im * factor_re - total_re * factor_im) - (s_im * ratio_re - s_re * ratio_im)
        turn_re = real * factor_re - rotation * factor_im
        turn_im = real * factor_im + rotation * factor_re
        step_grad = timestep * (total_re * turn_re + total_im * turn_im)

        def own(vector, target):
            length, size = vector.shape[1], target.shape[0]
            wide = jnp.broadcast_to(vector, (SUB, length))
            rolled = pltpu.roll(wide, lax.rem(length - me * size, length), 1)
            target[...] = rolled[0:1, :size].reshape(size)

        own(vector_sum[0:1, :width], gain_grad)
        own(vector_sum[1:2, :width], shift_grad)
        own(vector_sum[2:3, :width], through_grad)
        own(jnp.concatenate([vector_sum[3:4, :], vector_sum[4:5, : 2 * width - both]], axis=1), bias_grad)
        own(lambda_re, real_grad)
        own(lambda_im, rotation_grad)
        own(step_grad, timestep_grad)


def whole(shape):
    return pl.BlockSpec(shape, lambda i: (0,) * len(shape), pipeline_mode=pl.Buffered(1))


def total_of(shape):
    return pl.BlockSpec(shape, lambda i: (0,) * len(shape))


def tiled(rows, columns):
    return pl.BlockSpec((rows, columns), lambda i: (i, 0))


def params(cid=None):
    if cid is None:
        return pltpu.CompilerParams(dimension_semantics=("arbitrary",), vmem_limit_bytes=VMEM_LIMIT)
    return pltpu.CompilerParams(
        dimension_semantics=("arbitrary",), vmem_limit_bytes=VMEM_LIMIT, collective_id=cid, has_side_effects=True
    )


def body(
    tokens, cotangent, block_target, sequence_lengths, norm_gain, norm_shift, decay_real, decay_rotation,
    log_timestep, drive_matrix, readout_matrix, feedthrough, mixer_weight, mixer_bias,
):
    members = lax.axis_size("fsdp")
    grid = Grid(lax.axis_size("dp"), members)
    blocks = block_target.shape[0]
    rows, width = tokens.shape
    both = drive_matrix.shape[1]
    states = both // 2
    block_rows = rows // blocks
    span = SUB * block_rows
    tile = 2 * span if members <= SUB else span
    tiles = rows // tile
    tile_blocks = tile // block_rows
    total = blocks * members
    chunk = min(total, 2**30 // total**2)
    sequences = sequence_lengths.shape[1]
    shape = jax.ShapeDtypeStruct
    anywhere = pl.BlockSpec(memory_space=pl.ANY)
    regular = pltpu.SemaphoreType.DMA

    order = np.arange(span)
    source = (order % SUB) * block_rows + order // SUB
    perm = jnp.asarray(source[:, None] == order[None], BF16)
    back = jnp.asarray(order[:, None] == source[None], BF16)

    def flat(size):
        return pl.BlockSpec((size,), lambda i: (0,))

    small = (norm_gain, norm_shift, feedthrough, mixer_bias, decay_real, decay_rotation, log_timestep, block_target)
    counts = tuple(v.shape[0] for v in small)
    shards = (drive_matrix, readout_matrix, mixer_weight)
    slots = grid.slots

    def shifted(rows_of, columns):
        return pl.BlockSpec((rows_of, columns), lambda i: (jnp.clip(i - 1, 0, tiles - 1), 0))

    dealt, rows_p, cot_p, driven, keep, carry, drive, drive_raw, readout, mixer, vectors, rates, place, own_place, broken = pl.pallas_call(
        functools.partial(front_kernel, grid, block_rows, counts, tile),
        grid=(tiles + 2,),
        in_specs=[anywhere, shifted(tile, width)]
        + [flat(size) for size in counts]
        + [whole((1, sequences)), anywhere, anywhere, anywhere, whole((span, span))],
        out_specs=[
            shifted(tile, width), shifted(tile, width), shifted(tile, width), shifted(tile, both), shifted(tile, LANES),
            total_of((blocks, both)),
            total_of((width, both)),
            total_of((width, both)), anywhere, anywhere, total_of((SUB, 2 * width)), total_of((SUB, states)),
            total_of((1, total)), total_of((blocks, LANES)), total_of((sequences, members, LANES)),
        ],
        out_shape=[
            shape((rows, width), BF16), shape((rows, width), BF16), shape((rows, width), BF16),
            shape((rows, both), F32), shape((rows, LANES), F32), shape((blocks, both), F32),
            shape((width, both), BF16), shape((width, both), BF16),
            shape(grid.shape + readout_matrix.shape, BF16), shape(grid.shape + mixer_weight.shape, BF16),
            shape((SUB, 2 * width), F32), shape((SUB, states), F32), shape((1, total), F32),
            shape((blocks, LANES), F32), shape((sequences, members, LANES), jnp.int32),
        ],
        scratch_shapes=[
            pltpu.VMEM((rows, width), BF16),
            pltpu.VMEM((rows, width), BF16),
            pltpu.VMEM((rows, width), F32),
            pltpu.VMEM(grid.shape + (SUB, LANES), F32),
            pltpu.VMEM(grid.shape + drive_matrix.shape, BF16),
            pltpu.VMEM((blocks, LANES), jnp.int32),
            pltpu.VMEM((members, blocks, both), BF16),
            pltpu.VMEM((chunk, total), BF16),
            pltpu.VMEM((total, both), F32),
            regular((4 * slots,)), regular((4 * slots,)), regular((len(shards) + tiles,)), regular((members,)),
            regular((members,)), regular((grid.dp * members - 1,)), regular((grid.dp * members - 1,)),
        ],
        compiler_params=params(0),
        name="front",
    )(tokens, cotangent, *small, sequence_lengths, *shards, perm)
    readout = readout.reshape(both, width)
    mixer = mixer.reshape(width, 2 * width)

    def first(rows_of, columns):
        return pl.BlockSpec((rows_of, columns), lambda i: (jnp.minimum(i, tiles - 1), 0))

    def twice(rows_of, columns):
        def index(i):
            return (jnp.where(i <= tiles, jnp.minimum(i, tiles - 1), jnp.maximum(2 * tiles - i, 0)), 0)

        return pl.BlockSpec((rows_of, columns), index)

    def final(rows_of, columns):
        return pl.BlockSpec((rows_of, columns), lambda i: (jnp.clip(i - 2 * tiles - 1, 0, tiles - 1), 0))

    orders = ((2, 0, 1), (2, 1, 0), (2, 1, 0))
    weights = (readout_matrix, mixer_weight, drive_matrix)
    buffers = []
    for turn, weight in zip(orders, weights):
        for dim, _, left in reduce_plan(grid, turn):
            buffers.append(pltpu.VMEM((grid.fan(dim),) + tuple(grid.shape[d] for d in left) + weight.shape, BF16))
    gated_low, token_part, drive_sum, readout_sum, weight_sum, vector_sum = pl.pallas_call(
        functools.partial(back_kernel, grid, block_rows, orders),
        grid=(3 * tiles + 2,),
        in_specs=[
            first(tile, width), twice(tile, width), first(tile, both), twice(tile_blocks, both), twice(tile, LANES),
            final(tile, width), whole((SUB, states)), whole((both, width)), whole((SUB, 2 * width)),
            whole((width, 2 * width)), whole((1, total)), whole((blocks, LANES)), whole((sequences, members, LANES)),
            whole((width, both)), whole((width, both)),
        ],
        out_specs=[
            first(tile, width), final(tile, width), total_of(drive_matrix.shape), total_of(readout_matrix.shape),
            total_of(mixer_weight.shape), total_of((SUB, both)),
        ],
        out_shape=[
            shape((rows, width), BF16), shape((rows, width), BF16), shape(drive_matrix.shape, F32),
            shape(readout_matrix.shape, F32), shape(mixer_weight.shape, F32), shape((SUB, both), F32),
        ],
        scratch_shapes=[
            pltpu.VMEM((rows, both), BF16), pltpu.VMEM((rows, both), F32), pltpu.VMEM((rows, width), BF16),
            pltpu.VMEM((blocks, both), F32), pltpu.VMEM((width, 2 * width), F32), pltpu.VMEM((1, 2 * width), F32),
            pltpu.VMEM((1, width), F32), pltpu.VMEM((both, width), F32), pltpu.VMEM((1, width), F32),
            pltpu.VMEM((width, both), F32), pltpu.VMEM((SUB, both), F32), pltpu.VMEM((SUB, both), F32),
            pltpu.VMEM((members, blocks, both), BF16), pltpu.VMEM((chunk, total), BF16), pltpu.VMEM((total, both), F32),
            regular((members - 1,)), regular((members - 1,)),
        ]
        + [pltpu.VMEM(grid.shape[:-1] + weight.shape, F32) for weight in weights]
        + buffers
        + buffers
        + [
            pltpu.VMEM((SUB, both), F32), pltpu.VMEM((members - 1, SUB, both), F32),
            pltpu.VMEM((grid.dp - 1, SUB, both), F32), regular((3 * slots,)), regular((3 * slots,)),
            regular((members + grid.dp - 2,)), regular((members + grid.dp - 2,)),
        ],
        compiler_params=params(1),
        name="back",
    )(
        cot_p, dealt, driven, carry, keep, rows_p, rates, readout, vectors, mixer, place, own_place, broken, drive,
        drive_raw,
    )

    vector_sizes = [v.shape[0] for v in (norm_gain, norm_shift, decay_real, decay_rotation, log_timestep)]
    slab = 2 * tile
    outs = pl.pallas_call(
        functools.partial(tail_kernel, grid, span),
        grid=(rows // slab,),
        in_specs=[tiled(slab, width)] * 4
        + [
            whole((span, span)), whole((SUB, states)), whole(drive_matrix.shape), whole(readout_matrix.shape),
            whole(mixer_weight.shape), whole((SUB, both)),
        ],
        out_specs=[tiled(slab, width)] * 2
        + [flat(size) for size in vector_sizes]
        + [
            total_of(drive_matrix.shape), total_of(readout_matrix.shape), flat(feedthrough.shape[0]),
            total_of(mixer_weight.shape), flat(mixer_bias.shape[0]),
        ],
        out_shape=[shape((rows, width), F32)] * 2
        + [shape((size,), F32) for size in vector_sizes]
        + [
            shape(drive_matrix.shape, F32), shape(readout_matrix.shape, F32), shape(feedthrough.shape, F32),
            shape(mixer_weight.shape, F32), shape(mixer_bias.shape, F32),
        ],
        compiler_params=params(),
        name="tail",
    )(tokens, cotangent, token_part, gated_low, back, rates, drive_sum, readout_sum, weight_sum, vector_sum)
    return tuple(outs)


def solution(mesh):
    rows = P(AXES, None)
    flat = P(AXES)
    return jax.shard_map(
        body,
        mesh=mesh,
        in_specs=(rows, rows, flat, rows, flat, flat, flat, flat, flat, rows, rows, flat, rows, flat),
        out_specs=(rows, rows, flat, flat, flat, flat, flat, rows, rows, flat, rows, flat),
        check_vma=False,
    )
```

```python
import functools
import itertools

import jax
import jax.numpy as jnp
import numpy as np
from jax import lax
from jax.experimental import pallas as pl
from jax.experimental.pallas import tpu as pltpu
from jax.sharding import PartitionSpec as P

EPSILON = 1e-05
AXES = ("dp", "fsdp")
F32 = jnp.float32
BF16 = jnp.bfloat16
LANES = 128
SUB = 8
VMEM_LIMIT = 65400 * 1024


def dot(left, right):
    return jnp.dot(left, right, preferred_element_type=F32)


def contract_rows(left, right):
    return lax.dot_general(left, right, (((0,), (0,)), ((), ())), preferred_element_type=F32)


def contract_cols(left, right):
    return lax.dot_general(left, right, (((1,), (1,)), ((), ())), preferred_element_type=F32)


def lanes_to(mask, width):
    return jnp.concatenate([mask] * (width // LANES), axis=1)


def spread(vector, rows):
    return jnp.broadcast_to(vector, (rows, vector.shape[1]))


def gelu_parts(v):
    cdf = 0.5 + 0.5 * lax.erf(v * 0.7071067811865476)
    density = 0.3989422804014327 * jnp.exp(-0.5 * v * v)
    return v * cdf, cdf + v * density


def permute_tile(perm, tile, span):
    return jnp.concatenate(
        [dot(perm, tile[i * span : (i + 1) * span]) for i in range(tile.shape[0] // span)], axis=0
    )


def norm_stats(rows):
    center = jnp.mean(rows, axis=-1, keepdims=True)
    moved = rows - center
    spread_of = jnp.mean(moved * moved, axis=-1, keepdims=True)
    return moved, lax.rsqrt(spread_of + EPSILON)


MESH = pl.DeviceIdType.MESH


class Grid:
    def __init__(self, dp, members):
        self.dp, self.members = dp, members
        self.shape = (dp, members // 2, 2)
        self.slots = dp - 1 + members // 2 - 1 + 1

    def here(self):
        row, column = lax.axis_index("dp"), lax.axis_index("fsdp")
        return row, column, (row, lax.div(column, 2), lax.rem(column, 2))

    def fan(self, dim):
        return self.shape[dim] - 1

    def peers(self, dim):
        row, column, mine = self.here()
        found = []
        for away in range(1, self.shape[dim]):
            index = lax.rem(mine[dim] + away, self.shape[dim])
            if dim == 0:
                device = {"dp": index}
            elif dim == 1:
                device = {"fsdp": 2 * index + mine[2]}
            else:
                device = {"fsdp": 2 * mine[1] + index}
            found.append((away - 1, device, index))
        return found


def others(grid, everyone):
    row, column, _ = grid.here()
    found = []
    for down in range(grid.dp):
        for away in range(grid.members):
            if (down or away) and (everyone or not (down and away)):
                found.append({"dp": lax.rem(row + down, grid.dp), "fsdp": lax.rem(column + away, grid.members)})
    return found


def announce(grid, everyone=False):
    barrier = pltpu.get_barrier_semaphore()
    for device in others(grid, everyone):
        pl.semaphore_signal(barrier, inc=1, device_id=device, device_id_type=MESH)


def meet(grid, everyone=False):
    count = grid.dp * grid.members - 1 if everyone else grid.dp + grid.members - 2
    pl.semaphore_wait(pltpu.get_barrier_semaphore(), count)


def remote(source, target, send, recv, device):
    return pltpu.make_async_remote_copy(
        src_ref=source, dst_ref=target, send_sem=send, recv_sem=recv, device_id=device, device_id_type=MESH
    )


def gather_phase(grid, ref, cut, axes, dim, done, send, recv, base):
    _, _, mine = grid.here()
    at = tuple(slice(None) if d in done else mine[d] for d in axes)
    if cut is not None:
        at = at + (slice(None), cut)
    return [
        pltpu.make_async_remote_copy(
            src_ref=ref.at[at], dst_ref=ref.at[at], send_sem=send.at[base + slot], recv_sem=recv.at[base + slot],
            device_id=device, device_id_type=MESH,
        )
        for slot, device, _ in grid.peers(dim)
    ]


def reduce_plan(grid, order):
    plan = []
    for phase, dim in enumerate(order):
        done = order[:phase]
        left = tuple(d for d in range(len(grid.shape)) if d not in done and d != dim)
        plan.append((dim, done, left))
    return plan


def lane_index(width):
    return lax.broadcasted_iota(jnp.int32, (1, width), 1).astype(F32)


def unpack(rows, row, count, width):
    lanes = lane_index(width)
    owner = jnp.floor((lanes + 0.5) * (1.0 / count))
    inner = lanes - count * owner
    taken = lax.broadcasted_iota(jnp.int32, (LANES, width), 0).astype(F32) == inner
    spread_out = dot(rows.astype(BF16), jnp.where(taken, 1.0, 0.0).astype(BF16))
    index = lax.broadcasted_iota(jnp.int32, (rows.shape[0], width), 0).astype(F32)
    return jnp.sum(jnp.where(index == owner * SUB + row, spread_out, 0.0), axis=0, keepdims=True)


def rates_of(real, rotation, step_log):
    timestep = jnp.exp(step_log)
    magnitude = jnp.exp(real * timestep)
    turned = rotation * timestep
    factor_re = magnitude * jnp.cos(turned)
    factor_im = magnitude * jnp.sin(turned)
    modulus = real * real + rotation * rotation
    scale_re = ((factor_re - 1.0) * real + factor_im * rotation) / modulus
    scale_im = (factor_im * real - (factor_re - 1.0) * rotation) / modulus
    return timestep, factor_re, factor_im, modulus, scale_re, scale_im


def encode(values, inverse):
    scaled = values * inverse
    most = jnp.maximum(jnp.max(jnp.abs(scaled), axis=1, keepdims=True), 1e-30)
    power = jnp.broadcast_to(jnp.ceil(jnp.log2(most)), (values.shape[0], LANES))
    steps = jnp.round(scaled * lanes_to(32000.0 * jnp.exp2(-power), values.shape[1]))
    return jnp.concatenate([steps, power], axis=1).astype(jnp.int32).astype(jnp.int16)


def cross_blocks(members, reverse, arrive, pieces, norm, place, own_place, broken, flow_re, flow_im, chosen, dealt, carries):
    states = flow_re.shape[1]
    total = place.shape[1]
    steps = total // members
    blocks = steps
    chunk = chosen.shape[0]

    def choose(at):
        rows = lax.broadcasted_iota(jnp.int32, (chunk, total), 0).astype(F32) + float(at)
        return jnp.where(rows == place[...], 1.0, 0.0).astype(BF16)

    chosen[...] = choose(0)
    arrive()
    for at in range(0, total, chunk):
        if at:
            chosen[...] = choose(at)
        moved, power = 0.0, 0.0
        for first in range(0, members, 4):
            held = pieces[first : first + 4].reshape(4 * blocks, -1).astype(jnp.int32)
            picked = chosen[:, first * blocks : (first + 4) * blocks]
            ints = held[:, : 2 * states]
            high = (ints & -256).astype(F32).astype(BF16)
            low = (ints & 255).astype(F32).astype(BF16)
            moved = moved + (dot(picked, high) + dot(picked, low))
            power = power + dot(picked, held[:, 2 * states :].astype(F32).astype(BF16))
        moved = moved * (lanes_to(jnp.exp2(power) * (1.0 / 32000.0), 2 * states) * norm)
        dealt[at : at + chunk, :] = moved.astype(dealt.dtype)
    rate_re = spread(flow_re, members)
    rate_im = spread(-flow_im if reverse else flow_im, members)
    marks = [broken[s] for s in range(broken.shape[0])]

    def step(i, state):
        re, im = state
        p = steps - 1 - i if reverse else i
        at = pl.multiple_of(p * members, members)
        here = dealt[pl.ds(at, members), :].astype(F32)
        met = marks[0] == p
        for mark in marks[1:]:
            met = met | (mark == p)
        mask = lanes_to(jnp.where(met, 0.0, 1.0), states)
        dealt[pl.ds(at, members), :] = jnp.concatenate([re, im], axis=1).astype(dealt.dtype)
        return (
            mask * (rate_re * re - rate_im * im) + here[:, :states],
            mask * (rate_re * im + rate_im * re) + here[:, states:],
        )

    zero = jnp.zeros((members, states), F32)
    lax.fori_loop(0, steps, step, (zero, zero), unroll=4)
    own = own_place.shape[0]
    step_rows = min(total, 1024)
    found = jnp.zeros((own, 2 * states), F32)
    for at in range(0, total, step_rows):
        columns = lax.broadcasted_iota(jnp.int32, (own, step_rows), 1).astype(F32) + float(at)
        taken = jnp.where(columns == lanes_to(own_place[...], step_rows), 1.0, 0.0).astype(BF16)
        entering = dealt[at : at + step_rows, :].astype(F32)
        high = entering.astype(BF16)
        low = (entering - high.astype(F32)).astype(BF16)
        found = found + (dot(taken, high) + dot(taken, low))
    carries[...] = found


def split(values):
    high = values.astype(BF16)
    rest = values - high.astype(F32)
    middle = rest.astype(BF16)
    return high, middle, (rest - middle.astype(F32)).astype(BF16)


def row_times(row, matrix):
    wide = [jnp.broadcast_to(piece.astype(F32), (SUB, row.shape[1])).astype(BF16) for piece in split(row)]
    return sum(contract_cols(piece, matrix) for piece in wide)[0:1]


def row_sums(matrix):
    ones = jnp.ones((SUB, matrix.shape[1]), BF16)
    return sum(contract_cols(ones, piece) for piece in split(matrix))[0:1]


def layer_kernel(
    grid, block_rows, counts, tile, orders, tokens, cotangent, gain_s, shift_s, through_s, bias_s, real_s, rotation_s,
    step_s, target_s, lengths_s, drive_s, readout_s, mixer_s, perm,
    gated_low, token_part, drive_sum, readout_sum, weight_sum, vector_sum, rates,
    rows_in, normed, mixed_all, big, joined_all, table, drive_w, readout_w, mixer_w, drive, readout, mixer,
    vectors, place, own_place, broken, bits, carry, coming, pieces_ends, pieces, chosen, dealt_x, weight_grad,
    bias_grad, through_grad, readout_grad, mixed_sum, drive_grad, decay_cot, driven_sum, send_w, recv_w, local,
    ends_send, ends_recv, table_send, table_recv, push_send, push_recv, *rest,
):
    i = pl.program_id(0)
    tiles = (pl.num_programs(0) - 2) // 3
    row, column, mine = grid.here()
    members = grid.members
    core = 2
    phases = 3
    span = SUB * block_rows
    width = rows_in.shape[1]
    both = joined_all.shape[1]
    states = both // 2
    blocks = target_s.shape[0]
    chains = tile // span
    tile_blocks = tile // block_rows
    axes = (0, 1, 2)
    half = mixer_w.shape[-1] // 2
    wholes = (drive_w, readout_w, mixer_w, mixer_w)
    cuts = (None, None, pl.ds(0, half), pl.ds(half, half))
    ways = ((0, 1, 2), (1, 0, 2), (1, 0, 2), (0, 1, 2))

    def phase_copies(k, phase):
        order = ways[k]
        base = k * grid.slots + sum(grid.fan(d) for d in order[:phase])
        return gather_phase(grid, wholes[k], cuts[k], axes, order[phase], order[:phase], send_w, recv_w, base)

    def table_copies():
        return [
            remote(table.at[mine], table.at[mine], table_send.at[k], table_recv.at[k], device)
            for k, device in enumerate(others(grid, True))
        ]

    def gather_on(ks, phase):
        for k in ks:
            if phase:
                for copy in phase_copies(k, phase - 1):
                    copy.wait()
            if phase < phases:
                for copy in phase_copies(k, phase):
                    copy.start()

    def push_far(at):
        return [
            remote(pieces_ends.at[at], pieces_ends.at[at], ends_send.at[slot], ends_recv.at[slot], device)
            for slot, device, _ in grid.peers(1)
        ]

    def push_near(at, slot):
        device = grid.peers(2)[0][1]
        return remote(pieces_ends.at[at], pieces_ends.at[at], ends_send.at[slot], ends_recv.at[slot], device)

    far = grid.fan(1)

    def tile_at(j):
        return pl.ds(pl.multiple_of(j * tile, tile), tile)

    def mask_of(marks, c, t):
        single = 1 << t if t < 31 else -(1 << 31)
        return lanes_to(jnp.where((marks[c * SUB : (c + 1) * SUB] & single) == 0, 1.0, 0.0), states)

    def marks_of(j):
        return bits[pl.ds(pl.multiple_of(j * tile_blocks, tile_blocks), tile_blocks), :]

    def of_blocks(ref, j):
        return ref[pl.ds(pl.multiple_of(j * tile_blocks, tile_blocks), tile_blocks), :]

    def note_norm(k, squares):
        norm = jnp.sqrt(squares[:, :states] + squares[:, states:])
        norm = jnp.maximum(jnp.concatenate([norm, norm], axis=1), 1e-20)
        vectors[k : k + 1, :both] = norm
        vectors[k + 1 : k + 2, :both] = 1.0 / norm

    def flatten(source, target):
        size = source.shape[-2]
        for k, where in enumerate(itertools.product(*[range(n) for n in grid.shape])):
            target[k * size : (k + 1) * size, :] = source[where]

    rest = list(rest)
    parts = (readout_grad, weight_grad, drive_grad)
    outs = (readout_sum, weight_sum, drive_sum)
    count = len(parts)
    aligned = [out.shape[0] % SUB == 0 for out in outs]
    accs = [None if whole_rows else rest.pop(0) for whole_rows in aligned]
    stages = [[rest.pop(0) for _ in range(phases)] for _ in range(count)]
    landed = [[rest.pop(0) for _ in range(phases)] for _ in range(count)]
    vector_stage, across, along, send, recv, vector_send, vector_recv = rest
    plans = [reduce_plan(grid, order) for order in orders]
    every = (0, 1, 2)
    kept = every[:-1]
    first_a = tiles + 1
    first_b = 2 * tiles + 1

    def push_to(at):
        return [
            remote(
                pieces.at[at], pieces.at[at], push_send.at[away - 1], push_recv.at[away - 1],
                {"fsdp": lax.rem(column + away, members)},
            )
            for away in range(1, members)
        ]

    def combos(left):
        return list(itertools.product(*[range(grid.shape[d]) for d in left]))

    def at_of(dim, index, left, combo, dims):
        chosen_of = dict(zip(left, combo))
        chosen_of[dim] = index
        return tuple(chosen_of[d] if d in chosen_of else mine[d] for d in dims)

    def rows_of(k, where):
        size = outs[k].shape[0]
        down, half_of, low = where
        return pl.ds(pl.multiple_of(((down * grid.shape[1] + half_of) * 2 + low) * size, size), size)

    def keep_piece(k, dim, left, combo, piece):
        if aligned[k]:
            parts[k][rows_of(k, at_of(dim, mine[dim], left, combo, every)), :] = piece
        else:
            accs[k][at_of(dim, mine[dim], left, combo, kept)] = piece

    def piece_of(k, dim, index, left, combo):
        if aligned[k]:
            return parts[k][rows_of(k, at_of(dim, index, left, combo, every)), :]
        if dim != core:
            return accs[k][at_of(dim, index, left, combo, kept)]
        size = outs[k].shape[0]
        down, half, low = at_of(dim, index, left, combo, every)
        start = ((down * grid.shape[1] + half) * 2 + low) * size
        low_row = jnp.minimum(lax.div(start, SUB) * SUB, parts[k].shape[0] - 2 * SUB)
        window = parts[k][pl.ds(pl.multiple_of(low_row, SUB), 2 * SUB), :]
        return pltpu.roll(window, lax.rem(2 * SUB - (start - low_row), 2 * SUB), 0)[:size]

    def hops(k, phase):
        dim = plans[k][phase][0]
        base = k * grid.slots + sum(grid.fan(d) for d in orders[k][:phase])
        return [
            (
                remote(
                    stages[k][phase].at[slot], landed[k][phase].at[slot], send.at[base + slot], recv.at[base + slot],
                    device,
                ),
                slot,
                index,
            )
            for slot, device, index in grid.peers(dim)
        ]

    def begin(k, phase):
        dim, _, left = plans[k][phase]
        for copy, slot, index in hops(k, phase):
            for combo in combos(left):
                stages[k][phase][(slot,) + combo] = piece_of(k, dim, index, left, combo).astype(BF16)
            copy.start()

    def finish(k, phase):
        dim, _, left = plans[k][phase]
        copies = hops(k, phase)
        for copy, _, _ in copies:
            copy.wait()
        for combo in combos(left):
            piece = piece_of(k, dim, mine[dim], left, combo)
            for _, slot, _ in copies:
                piece = piece + landed[k][phase][(slot,) + combo].astype(F32)
            keep_piece(k, dim, left, combo, piece)

    def advance(ks, phase):
        for k in ks:
            if phase:
                finish(k, phase - 1)
            if phase < phases:
                begin(k, phase)
            else:
                outs[k][...] = parts[k][rows_of(k, mine), :] if aligned[k] else accs[k][mine[:-1]]

    def vector_across():
        return [
            remote(
                vector_stage, across.at[away - 1], vector_send.at[away - 1], vector_recv.at[away - 1],
                {"fsdp": lax.rem(column + away, members)},
            )
            for away in range(1, members)
        ]

    def vector_along():
        return [
            remote(
                vector_sum, along.at[slot], vector_send.at[members - 1 + slot], vector_recv.at[members - 1 + slot], device
            )
            for slot, device, _ in grid.peers(0)
        ]

    @pl.when(i == 0)
    def _():
        copies = [
            pltpu.make_async_copy(shard, ref.at[tuple(mine)], local.at[k])
            for k, (shard, ref) in enumerate(zip((drive_s, readout_s, mixer_s), wholes))
        ]
        for copy in copies:
            copy.start()
        held = [gain_s, shift_s, through_s, bias_s, real_s, rotation_s, step_s, target_s]
        own = table.at[tuple(mine)]
        own[...] = jnp.zeros_like(own)
        for k, ref in enumerate(held):
            own[k : k + 1, : ref.shape[0]] = ref[...].astype(F32).reshape(1, ref.shape[0])
        sequences = lengths_s.shape[1]
        own[4:5, LANES // 2 : LANES // 2 + sequences] = lengths_s[...].astype(F32)
        announce(grid, True)
        taps = [
            pltpu.make_async_copy(
                cotangent.at[pl.ds(j * tile, tile)], mixed_all.at[pl.ds(j * tile, tile)],
                local.at[len(copies) + tiles + j],
            )
            for j in range(tiles)
        ]
        chunks = [
            pltpu.make_async_copy(
                tokens.at[pl.ds(j * tile, tile)], rows_in.at[pl.ds(j * tile, tile)], local.at[len(copies) + j]
            )
            for j in range(tiles)
        ]
        for copy in chunks + taps:
            copy.start()
        for copy in copies:
            copy.wait()
        meet(grid, True)
        gather_on((0,), 0)
        for copy in table_copies():
            copy.start()
        gather_on((1, 2), 0)

        def turn(ref):
            def one(j, _):
                ref[tile_at(j), :] = permute_tile(perm[...], ref[tile_at(j), :], span).astype(BF16)
                return 0

            return one

        for copy in chunks[: tiles // 2]:
            copy.wait()
        lax.fori_loop(0, tiles // 2, turn(rows_in), 0)
        gather_on((0,), 1)
        gather_on((3,), 0)
        gather_on((1, 2), 1)
        for copy in chunks[tiles // 2 :]:
            copy.wait()
        lax.fori_loop(tiles // 2, tiles, turn(rows_in), 0)
        for copy in table_copies():
            copy.wait()
        rows = table[...].reshape(-1, LANES)
        vectors[...] = jnp.zeros_like(vectors)
        for k, size in enumerate((width, width, width, 2 * width)):
            vectors[k : k + 1, :size] = unpack(rows, k, counts[k], size)
        real, rotation, step_log = [unpack(rows, k, counts[k], states) for k in (4, 5, 6)]
        _, factor_re, factor_im, _, scale_re, scale_im = rates_of(real, rotation, step_log)
        flow_re, flow_im = factor_re, factor_im
        power = 1
        while power < block_rows:
            flow_re, flow_im = flow_re * flow_re - flow_im * flow_im, 2.0 * flow_re * flow_im
            power *= 2
        for k, value in enumerate((factor_re, factor_im, flow_re, flow_im, real, rotation, step_log)):
            rates[k : k + 1, :] = value
        group = table[row].reshape(members * SUB, LANES)
        for m in range(members):
            q = group[m * SUB + 7 : m * SUB + 8, :blocks]
            d = jnp.floor(q * (1.0 / blocks))
            place[:, m * blocks : (m + 1) * blocks] = (q - d * blocks) * members + d
        lengths = jnp.concatenate([group[m * SUB + 4 : m * SUB + 5, :] for m in range(members)], axis=0)
        sequences = lengths_s.shape[1]
        q = table[tuple(mine) + (slice(7, 8), slice(None))]
        diagonal = lax.broadcasted_iota(jnp.int32, (blocks, LANES), 0) == lax.broadcasted_iota(
            jnp.int32, (blocks, LANES), 1
        )
        q = jnp.sum(jnp.where(diagonal, jnp.broadcast_to(q, (blocks, LANES)), 0.0), axis=1, keepdims=True)
        q = jnp.broadcast_to(q, (blocks, LANES))
        d = jnp.floor(q * (1.0 / blocks))
        p = q - d * blocks
        own_place[...] = p * members + d
        start = jnp.zeros((members, LANES), F32)
        marks = jnp.zeros((blocks, LANES), jnp.int32)
        for s in range(sequences):
            broken[s] = jnp.floor(start * (1.0 / block_rows)).astype(jnp.int32)
            mark = jnp.zeros((blocks, LANES), F32)
            for m in range(members):
                mark = jnp.where(d == float(m), jnp.broadcast_to(start[m : m + 1, :], (blocks, LANES)), mark)
            mark = mark - p * block_rows
            inside = (mark >= 0.0) & (mark < block_rows)
            shift = jnp.where(inside, mark, 0.0).astype(jnp.int32)
            marks = marks | jnp.where(inside, lax.shift_left(jnp.ones_like(shift), shift), 0)
            column_of = lengths[:, LANES // 2 + s : LANES // 2 + s + 1]
            start = start + jnp.broadcast_to(column_of, (members, LANES))
        bits[...] = marks
        gain = vectors[0:1, :width]
        shift_by = vectors[1:2, :width]

        def settle(j, _):
            moved, rstd = norm_stats(rows_in[tile_at(j), :].astype(F32))
            normed[tile_at(j), :] = (moved * rstd * gain + shift_by).astype(BF16)
            return 0

        lax.fori_loop(0, tiles // 2, settle, 0)
        gather_on((0,), 2)
        lax.fori_loop(tiles // 2, tiles, settle, 0)
        gather_on((0,), 3)
        gather_on((3,), 1)
        raw = drive_w[...].reshape(width, both).astype(F32)
        drive[:, :states] = (scale_re * raw[:, :states] - scale_im * raw[:, states:]).astype(BF16)
        drive[:, states:] = (scale_re * raw[:, states:] + scale_im * raw[:, :states]).astype(BF16)
        note_norm(4, jnp.sum(jnp.square(drive[...].astype(F32)), axis=0, keepdims=True))
        rate_re = spread(rates[0:1, :], SUB)
        rate_im = spread(rates[1:2, :], SUB)

        def begin_tile(j, _):
            driven = big.at[tile_at(j)]
            driven[...] = dot(normed[tile_at(j), :], drive[...]).astype(big.dtype)
            marks = marks_of(j)
            state = [(jnp.zeros((SUB, states), F32), jnp.zeros((SUB, states), F32)) for _ in range(chains)]
            for t in range(block_rows):
                for c in range(chains):
                    at = c * span + t * SUB
                    mask = mask_of(marks, c, t)
                    re, im = state[c]
                    now_re = mask * (rate_re * re - rate_im * im) + driven[at : at + SUB, :states].astype(F32)
                    now_im = mask * (rate_re * im + rate_im * re) + driven[at : at + SUB, states:].astype(F32)
                    state[c] = (now_re, now_im)
            ends = jnp.concatenate([jnp.concatenate(state[c], axis=1) for c in range(chains)], axis=0)
            at = (column, pl.ds(pl.multiple_of(j * tile_blocks, tile_blocks), tile_blocks))
            pieces_ends[at + (slice(None),)] = encode(ends, vectors[5:6, :both])
            for copy in push_far(at) + [push_near(at, far)]:
                copy.start()
            return 0

        lax.fori_loop(0, tiles, begin_tile, 0)
        for copy in taps:
            copy.wait()
        lax.fori_loop(0, tiles, turn(mixed_all), 0)

        def arrive():
            onward = []
            for k, copy in enumerate(push_far((column,))):
                copy.wait()
                there = 2 * lax.rem(mine[1] + grid.shape[1] - 1 - k, grid.shape[1]) + mine[2]
                onward.append(push_near((there,), far + 1 + k))
                onward[-1].start()
            gather_on((1, 2, 3), 2)
            push_near((column,), far).wait()
            for copy in onward:
                copy.wait()

        cross_blocks(
            members, False, arrive, pieces_ends, vectors[4:5, :both], place, own_place, broken, rates[2:3, :], rates[3:4, :], chosen, dealt_x,
            carry,
        )
        gather_on((1, 2, 3), 3)
        flatten(readout_w, readout)
        flatten(mixer_w, mixer)
        note_norm(6, row_sums(jnp.square(readout[...].astype(F32))))
        for total in (
            weight_grad, bias_grad, through_grad, readout_grad, mixed_sum, drive_grad, decay_cot, driven_sum
        ):
            total[...] = jnp.zeros_like(total)

    rate_re = spread(rates[0:1, :], SUB)
    rate_im = spread(rates[1:2, :], SUB)

    @pl.when(i < tiles)
    def _():
        through = vectors[2:3, :width]
        bias = vectors[3:4, : 2 * width]
        here = tile_at(i)
        joined = joined_all.at[here]
        driven = big.at[here]
        joined_grad = big.at[here]
        marks = marks_of(i)
        entering = of_blocks(carry, i)
        state = [
            (entering[c * SUB : (c + 1) * SUB, :states], entering[c * SUB : (c + 1) * SUB, states:])
            for c in range(chains)
        ]
        for t in range(0, block_rows, 2):
            for c in range(chains):
                held = []
                for step in (t, t + 1):
                    at = c * span + step * SUB
                    mask = mask_of(marks, c, step)
                    re, im = state[c]
                    now_re = mask * (rate_re * re - rate_im * im) + driven[at : at + SUB, :states].astype(F32)
                    now_im = mask * (rate_re * im + rate_im * re) + driven[at : at + SUB, states:].astype(F32)
                    state[c] = (now_re, now_im)
                    held.append(state[c])
                at = c * span + t * SUB
                joined[at : at + 2 * SUB, :states] = jnp.concatenate([held[0][0], held[1][0]], axis=0).astype(BF16)
                joined[at : at + 2 * SUB, states:] = (-jnp.concatenate([held[0][1], held[1][1]], axis=0)).astype(BF16)

        dealt_f32 = normed[here, :].astype(F32)
        mixed = dot(joined[...], readout[...]) + through * dealt_f32
        activated, slope = gelu_parts(mixed)
        features = activated.astype(BF16)
        hidden = dot(features, mixer[...]) + bias
        value = hidden[:, :width]
        sig = 0.5 + 0.5 * jnp.tanh(0.5 * hidden[:, width:])
        gated_low[...] = (value * sig).astype(BF16)
        cot_sig = mixed_all[here, :].astype(F32) * sig
        hidden_low = jnp.concatenate(
            [cot_sig.astype(BF16), (cot_sig * value * (1.0 - sig)).astype(BF16)], axis=1
        )
        weight_grad[...] += contract_rows(features, hidden_low)
        bias_grad[...] += jnp.sum(hidden_low.astype(F32), axis=0, keepdims=True)
        feature_grad = contract_cols(hidden_low, mixer[...]).astype(BF16)
        mixed_grad = (feature_grad.astype(F32) * slope).astype(BF16)
        mixed_all[here, :] = mixed_grad
        mixed_f32 = mixed_grad.astype(F32)
        through_grad[...] += jnp.sum(mixed_f32 * dealt_f32, axis=0, keepdims=True)
        mixed_sum[...] += jnp.sum(mixed_f32, axis=0, keepdims=True)
        readout_grad[...] += contract_rows(joined[...], mixed_grad)
        joined_grad[...] = contract_cols(mixed_grad, readout[...]).astype(big.dtype)

        going = [(jnp.zeros((SUB, states), F32), jnp.zeros((SUB, states), F32)) for _ in range(chains)]
        for t in reversed(range(block_rows)):
            for c in range(chains):
                at = c * span + t * SUB
                mask = mask_of(marks, c, t)
                re = joined_grad[at : at + SUB, :states].astype(F32) + going[c][0]
                im = going[c][1] - joined_grad[at : at + SUB, states:].astype(F32)
                going[c] = (mask * (rate_re * re + rate_im * im), mask * (rate_re * im - rate_im * re))
        heads = jnp.concatenate([jnp.concatenate(going[c], axis=1) for c in range(chains)], axis=0)
        at = (column, pl.ds(pl.multiple_of(i * tile_blocks, tile_blocks), tile_blocks))
        pieces[at + (slice(None),)] = encode(heads, vectors[7:8, :both])

        for copy in push_to(at):
            copy.start()

    @pl.when(i == tiles)
    def _():
        def arrive():
            advance((0, 1), 0)
            for copy in push_to((column,)):
                copy.wait()

        cross_blocks(
            members, True, arrive, pieces, vectors[6:7, :both], place, own_place, broken, rates[2:3, :], rates[3:4, :], chosen, dealt_x,
            coming,
        )
        advance((0, 1), 1)

    @pl.when(i == first_a + tiles // 2)
    def _():
        advance((1,), 2)

    @pl.when(i == first_a + tiles - 2)
    def _():
        advance((0,), 2)

    @pl.when(i == first_b)
    def _():
        advance((1,), 3)

    @pl.when(i == first_b + 2)
    def _():
        advance((0,), 3)

    @pl.when((i >= first_a) & (i < first_b))
    def _():
        j = first_b - 1 - i
        here = tile_at(j)
        joined = joined_all.at[here]
        driven_low = joined
        joined_grad = big.at[here]
        marks = marks_of(j)
        entering = of_blocks(coming, j)
        before = of_blocks(carry, j)
        going = [
            (entering[c * SUB : (c + 1) * SUB, :states], entering[c * SUB : (c + 1) * SUB, states:])
            for c in range(chains)
        ]
        total = [(jnp.zeros((SUB, states), F32), jnp.zeros((SUB, states), F32)) for _ in range(chains)]
        sums = list(total)
        for t in reversed(range(0, block_rows, 2)):
            for c in range(chains):
                pair = c * span + t * SUB
                here_re = joined[pair : pair + SUB, :states].astype(F32)
                here_im = -joined[pair : pair + SUB, states:].astype(F32)
                if t == 0:
                    past_re = before[c * SUB : (c + 1) * SUB, :states]
                    past_im = before[c * SUB : (c + 1) * SUB, states:]
                else:
                    past_re = joined[pair - SUB : pair, :states].astype(F32)
                    past_im = -joined[pair - SUB : pair, states:].astype(F32)
                held = {}
                for step, (prev_re, prev_im) in ((t + 1, (here_re, here_im)), (t, (past_re, past_im))):
                    where = c * span + step * SUB
                    mask = mask_of(marks, c, step)
                    re = joined_grad[where : where + SUB, :states].astype(F32) + going[c][0]
                    im = going[c][1] - joined_grad[where : where + SUB, states:].astype(F32)
                    held[step] = (re, im)
                    sums[c] = (sums[c][0] + re, sums[c][1] + im)
                    on_re = mask * (rate_re * re + rate_im * im)
                    on_im = mask * (rate_re * im - rate_im * re)
                    going[c] = (on_re, on_im)
                    total[c] = (
                        total[c][0] + (on_re * prev_re + on_im * prev_im),
                        total[c][1] + (on_im * prev_re - on_re * prev_im),
                    )
                driven_low[pair : pair + 2 * SUB, :states] = jnp.concatenate(
                    [held[t][0], held[t + 1][0]], axis=0
                ).astype(BF16)
                driven_low[pair : pair + 2 * SUB, states:] = jnp.concatenate(
                    [held[t][1], held[t + 1][1]], axis=0
                ).astype(BF16)
        for c in range(chains):
            decay_cot[...] += jnp.concatenate(total[c], axis=1)
            driven_sum[...] += jnp.concatenate(sums[c], axis=1)
        drive_grad[...] += contract_rows(normed[here, :], driven_low[...])

    @pl.when(i == first_b)
    def _():
        advance((2,), 0)
        cot = jnp.sum(decay_cot[...], axis=0, keepdims=True)
        factor_re, factor_im = rates[0:1, :], rates[1:2, :]
        size = factor_re * factor_re + factor_im * factor_im
        vector_stage[...] = jnp.zeros_like(vector_stage)
        through = vectors[2:3, :width]
        summed = jnp.sum(driven_sum[...], axis=0, keepdims=True)
        shift_sum = through * mixed_sum[...] + row_times(summed, drive[...])
        crossed = row_sums(drive[...].astype(F32) * drive_grad[...]) + through * through_grad[...]
        vector_stage[0:1, :width] = (crossed - vectors[1:2, :width] * shift_sum) / vectors[0:1, :width]
        vector_stage[1:2, :width] = shift_sum
        vector_stage[2:3, :width] = through_grad[...]
        vector_stage[3:4, :] = bias_grad[:, :both]
        vector_stage[4:5, : 2 * width - both] = bias_grad[:, both:]
        vector_stage[5:6, :states] = (cot[:, :states] * factor_re - cot[:, states:] * factor_im) / size
        vector_stage[5:6, states:] = (cot[:, :states] * factor_im + cot[:, states:] * factor_re) / size
        d_re, d_im = drive_grad[:, :states], drive_grad[:, states:]
        raw = drive_w[...].reshape(width, both).astype(F32)
        b_re, b_im = raw[:, :states], raw[:, states:]
        vector_stage[6:7, :states] = jnp.sum(d_re * b_re + d_im * b_im, axis=0, keepdims=True)
        vector_stage[6:7, states:] = jnp.sum(d_im * b_re - d_re * b_im, axis=0, keepdims=True)

        for copy in vector_across():
            copy.start()

    @pl.when(i == first_b + 1)
    def _():
        advance((2,), 1)

    @pl.when(i == first_b + 3)
    def _():
        for copy in vector_across():
            copy.wait()
        total = vector_stage[...]
        for k in range(members - 1):
            total = total + across[k]
        vector_sum[...] = total
        for copy in vector_along():
            copy.start()

    @pl.when(i == first_b + tiles - 2)
    def _():
        advance((2,), 2)

    @pl.when(i == first_b + tiles)
    def _():
        for copy in vector_along():
            copy.wait()
        total = vector_sum[...]
        for k in range(grid.dp - 1):
            total = total + along[k]
        vector_sum[...] = total
        advance((2,), 3)

    @pl.when((i >= first_b) & (i < first_b + tiles))
    def _():
        j = i - first_b
        here = tile_at(j)
        driven_low = joined_all[here, :]
        normed_grad = vectors[2:3, :width] * mixed_all[here, :].astype(F32) + contract_cols(driven_low, drive[...])
        given = normed_grad.astype(BF16).astype(F32)
        moved, rstd = norm_stats(rows_in[here, :].astype(F32))
        xhat = moved * rstd
        scaled = given * vectors[0:1, :width]
        inner = jnp.mean(scaled * xhat, axis=-1, keepdims=True)
        token_part[...] = (
            rstd * (scaled - jnp.mean(scaled, axis=-1, keepdims=True) - xhat * inner)
        ).astype(BF16)


def tail_kernel(
    grid, span, tokens, cotangent, token_part, gated_low, back, rates, drive_sum, readout_sum, weight_sum, vector_sum,
    out, token_grad, gain_grad, shift_grad, real_grad, rotation_grad, timestep_grad, drive_grad, readout_grad,
    through_grad, weight_grad, bias_grad,
):
    width = tokens.shape[1]
    both = vector_sum.shape[1]
    states = both // 2
    out[...] = tokens[...].astype(F32) + permute_tile(back[...], gated_low[...], span)
    token_grad[...] = cotangent[...].astype(F32) + permute_tile(back[...], token_part[...], span)

    @pl.when(pl.program_id(0) == 0)
    def _():
        row, column, _ = grid.here()
        me = row * grid.members + column
        real, rotation, step_log = [rates[k : k + 1, :] for k in (4, 5, 6)]
        timestep, factor_re, factor_im, modulus, scale_re, scale_im = rates_of(real, rotation, step_log)
        d_re, d_im = drive_sum[:, :states], drive_sum[:, states:]
        drive_grad[:, :states] = scale_re * d_re + scale_im * d_im
        drive_grad[:, states:] = scale_re * d_im - scale_im * d_re
        readout_grad[...] = readout_sum[...]
        weight_grad[...] = weight_sum[...]
        s_re, s_im = vector_sum[6:7, :states], vector_sum[6:7, states:]
        total_re = vector_sum[5:6, :states] + (s_re * real - s_im * rotation) / modulus
        total_im = vector_sum[5:6, states:] + (s_re * rotation + s_im * real) / modulus
        ratio_re = (scale_re * real + scale_im * rotation) / modulus
        ratio_im = (scale_im * real - scale_re * rotation) / modulus
        lambda_re = timestep * (total_re * factor_re + total_im * factor_im) - (s_re * ratio_re + s_im * ratio_im)
        lambda_im = timestep * (total_im * factor_re - total_re * factor_im) - (s_im * ratio_re - s_re * ratio_im)
        turn_re = real * factor_re - rotation * factor_im
        turn_im = real * factor_im + rotation * factor_re
        step_grad = timestep * (total_re * turn_re + total_im * turn_im)

        def own(vector, target):
            length, size = vector.shape[1], target.shape[0]
            wide = jnp.broadcast_to(vector, (SUB, length))
            rolled = pltpu.roll(wide, lax.rem(length - me * size, length), 1)
            target[...] = rolled[0:1, :size].reshape(size)

        own(vector_sum[0:1, :width], gain_grad)
        own(vector_sum[1:2, :width], shift_grad)
        own(vector_sum[2:3, :width], through_grad)
        own(jnp.concatenate([vector_sum[3:4, :], vector_sum[4:5, : 2 * width - both]], axis=1), bias_grad)
        own(lambda_re, real_grad)
        own(lambda_im, rotation_grad)
        own(step_grad, timestep_grad)


def whole(shape):
    return pl.BlockSpec(shape, lambda i: (0,) * len(shape), pipeline_mode=pl.Buffered(1))


def total_of(shape):
    return pl.BlockSpec(shape, lambda i: (0,) * len(shape))


def tiled(rows, columns):
    return pl.BlockSpec((rows, columns), lambda i: (i, 0))


def params(cid=None):
    if cid is None:
        return pltpu.CompilerParams(dimension_semantics=("arbitrary",), vmem_limit_bytes=VMEM_LIMIT)
    return pltpu.CompilerParams(
        dimension_semantics=("arbitrary",), vmem_limit_bytes=VMEM_LIMIT, collective_id=cid, has_side_effects=True
    )


def body(
    tokens, cotangent, block_target, sequence_lengths, norm_gain, norm_shift, decay_real, decay_rotation,
    log_timestep, drive_matrix, readout_matrix, feedthrough, mixer_weight, mixer_bias,
):
    members = lax.axis_size("fsdp")
    grid = Grid(lax.axis_size("dp"), members)
    blocks = block_target.shape[0]
    rows, width = tokens.shape
    both = drive_matrix.shape[1]
    states = both // 2
    block_rows = rows // blocks
    span = SUB * block_rows
    tile = 2 * span if members <= SUB else span
    tiles = rows // tile
    tile_blocks = tile // block_rows
    total = blocks * members
    chunk = min(total, 2**29 // total**2)
    sequences = sequence_lengths.shape[1]
    shape = jax.ShapeDtypeStruct
    anywhere = pl.BlockSpec(memory_space=pl.ANY)
    regular = pltpu.SemaphoreType.DMA

    order = np.arange(span)
    source = (order % SUB) * block_rows + order // SUB
    perm = jnp.asarray(source[:, None] == order[None], BF16)
    back = jnp.asarray(order[:, None] == source[None], BF16)

    def flat(size):
        return pl.BlockSpec((size,), lambda i: (0,))

    small = (norm_gain, norm_shift, feedthrough, mixer_bias, decay_real, decay_rotation, log_timestep, block_target)
    counts = tuple(v.shape[0] for v in small)
    shards = (drive_matrix, readout_matrix, mixer_weight)
    slots = grid.slots
    kept_type = F32 if members <= SUB else BF16

    def first(rows_of, columns):
        return pl.BlockSpec((rows_of, columns), lambda i: (jnp.minimum(i, tiles - 1), 0))

    def final(rows_of, columns):
        return pl.BlockSpec((rows_of, columns), lambda i: (jnp.clip(i - 2 * tiles - 1, 0, tiles - 1), 0))

    orders = ((2, 0, 1), (2, 1, 0), (2, 1, 0))
    weights = (readout_matrix, mixer_weight, drive_matrix)
    buffers = []
    for turn, weight in zip(orders, weights):
        for dim, _, left in reduce_plan(grid, turn):
            buffers.append(pltpu.VMEM((grid.fan(dim),) + tuple(grid.shape[d] for d in left) + weight.shape, BF16))
    gated_low, token_part, drive_sum, readout_sum, weight_sum, vector_sum, rates = pl.pallas_call(
        functools.partial(layer_kernel, grid, block_rows, counts, tile, orders),
        grid=(3 * tiles + 2,),
        in_specs=[anywhere, anywhere]
        + [flat(size) for size in counts]
        + [whole((1, sequences)), anywhere, anywhere, anywhere, whole((span, span))],
        out_specs=[
            first(tile, width), final(tile, width), total_of(drive_matrix.shape), total_of(readout_matrix.shape),
            total_of(mixer_weight.shape), total_of((SUB, both)), total_of((SUB, states)),
        ],
        out_shape=[
            shape((rows, width), BF16), shape((rows, width), BF16), shape(drive_matrix.shape, F32),
            shape(readout_matrix.shape, F32), shape(mixer_weight.shape, F32), shape((SUB, both), F32),
            shape((SUB, states), F32),
        ],
        scratch_shapes=[
            pltpu.VMEM((rows, width), BF16), pltpu.VMEM((rows, width), BF16), pltpu.VMEM((rows, width), BF16),
            pltpu.VMEM((rows, both), kept_type), pltpu.VMEM((rows, both), BF16),
            pltpu.VMEM(grid.shape + (SUB, LANES), F32),
        ]
        + [pltpu.VMEM(grid.shape + shard.shape, BF16) for shard in shards]
        + [
            pltpu.VMEM((width, both), BF16), pltpu.VMEM((both, width), BF16),
            pltpu.VMEM((width, 2 * width), BF16), pltpu.VMEM((SUB, 2 * width), F32), pltpu.VMEM((1, total), F32),
            pltpu.VMEM((blocks, LANES), F32), pltpu.VMEM((sequences, members, LANES), jnp.int32),
            pltpu.VMEM((blocks, LANES), jnp.int32), pltpu.VMEM((blocks, both), F32), pltpu.VMEM((blocks, both), F32),
            pltpu.VMEM((members, blocks, both + LANES), jnp.int16),
            pltpu.VMEM((members, blocks, both + LANES), jnp.int16),
            pltpu.VMEM((chunk, total), BF16), pltpu.VMEM((total, both), kept_type),
            pltpu.VMEM((width, 2 * width), F32), pltpu.VMEM((1, 2 * width), F32), pltpu.VMEM((1, width), F32),
            pltpu.VMEM((both, width), F32), pltpu.VMEM((1, width), F32), pltpu.VMEM((width, both), F32),
            pltpu.VMEM((SUB, both), F32), pltpu.VMEM((SUB, both), F32),
            regular((4 * slots,)), regular((4 * slots,)), regular((len(shards) + 2 * tiles,)), regular((members,)),
            regular((members,)), regular((grid.dp * members - 1,)), regular((grid.dp * members - 1,)),
            regular((members - 1,)), regular((members - 1,)),
        ]
        + [pltpu.VMEM(grid.shape[:-1] + weight.shape, F32) for weight in weights if weight.shape[0] % SUB]
        + buffers
        + buffers
        + [
            pltpu.VMEM((SUB, both), F32), pltpu.VMEM((members - 1, SUB, both), F32),
            pltpu.VMEM((grid.dp - 1, SUB, both), F32), regular((3 * slots,)), regular((3 * slots,)),
            regular((members + grid.dp - 2,)), regular((members + grid.dp - 2,)),
        ],
        compiler_params=params(0),
        name="layer",
    )(tokens, cotangent, *small, sequence_lengths, *shards, perm)

    vector_sizes = [v.shape[0] for v in (norm_gain, norm_shift, decay_real, decay_rotation, log_timestep)]
    slab = 2 * tile
    outs = pl.pallas_call(
        functools.partial(tail_kernel, grid, span),
        grid=(rows // slab,),
        in_specs=[tiled(slab, width)] * 4
        + [
            whole((span, span)), whole((SUB, states)), whole(drive_matrix.shape), whole(readout_matrix.shape),
            whole(mixer_weight.shape), whole((SUB, both)),
        ],
        out_specs=[tiled(slab, width)] * 2
        + [flat(size) for size in vector_sizes]
        + [
            total_of(drive_matrix.shape), total_of(readout_matrix.shape), flat(feedthrough.shape[0]),
            total_of(mixer_weight.shape), flat(mixer_bias.shape[0]),
        ],
        out_shape=[shape((rows, width), F32)] * 2
        + [shape((size,), F32) for size in vector_sizes]
        + [
            shape(drive_matrix.shape, F32), shape(readout_matrix.shape, F32), shape(feedthrough.shape, F32),
            shape(mixer_weight.shape, F32), shape(mixer_bias.shape, F32),
        ],
        compiler_params=params(),
        name="tail",
    )(tokens, cotangent, token_part, gated_low, back, rates, drive_sum, readout_sum, weight_sum, vector_sum)
    return tuple(outs)


def solution(mesh):
    rows = P(AXES, None)
    flat = P(AXES)
    return jax.shard_map(
        body,
        mesh=mesh,
        in_specs=(rows, rows, flat, rows, flat, flat, flat, flat, flat, rows, rows, flat, rows, flat),
        out_specs=(rows, rows, flat, flat, flat, flat, flat, rows, rows, flat, rows, flat),
        check_vma=False,
    )
```

```python
import functools
import itertools

import jax
import jax.numpy as jnp
import numpy as np
from jax import lax
from jax.experimental import pallas as pl
from jax.experimental.pallas import tpu as pltpu
from jax.sharding import PartitionSpec as P

EPSILON = 1e-05
AXES = ("dp", "fsdp")
F32 = jnp.float32
BF16 = jnp.bfloat16
LANES = 128
SUB = 8
VMEM_LIMIT = 65400 * 1024


def dot(left, right):
    return jnp.dot(left, right, preferred_element_type=F32)


def contract_rows(left, right):
    return lax.dot_general(left, right, (((0,), (0,)), ((), ())), preferred_element_type=F32)


def contract_cols(left, right):
    return lax.dot_general(left, right, (((1,), (1,)), ((), ())), preferred_element_type=F32)


def lanes_to(mask, width):
    return jnp.concatenate([mask] * (width // LANES), axis=1)


def spread(vector, rows):
    return jnp.broadcast_to(vector, (rows, vector.shape[1]))


def gelu_parts(v):
    cdf = 0.5 + 0.5 * lax.erf(v * 0.7071067811865476)
    density = 0.3989422804014327 * jnp.exp(-0.5 * v * v)
    return v * cdf, cdf + v * density


def permute_tile(perm, tile, span):
    return jnp.concatenate(
        [dot(perm, tile[i * span : (i + 1) * span]) for i in range(tile.shape[0] // span)], axis=0
    )


def norm_stats(rows):
    center = jnp.mean(rows, axis=-1, keepdims=True)
    moved = rows - center
    spread_of = jnp.mean(moved * moved, axis=-1, keepdims=True)
    return moved, lax.rsqrt(spread_of + EPSILON)


MESH = pl.DeviceIdType.MESH


class Grid:
    def __init__(self, dp, members):
        self.dp, self.members = dp, members
        self.shape = (dp, members // 2, 2)
        self.slots = dp - 1 + members // 2 - 1 + 1

    def here(self):
        row, column = lax.axis_index("dp"), lax.axis_index("fsdp")
        return row, column, (row, lax.div(column, 2), lax.rem(column, 2))

    def fan(self, dim):
        return self.shape[dim] - 1

    def peers(self, dim):
        row, column, mine = self.here()
        found = []
        for away in range(1, self.shape[dim]):
            index = lax.rem(mine[dim] + away, self.shape[dim])
            if dim == 0:
                device = {"dp": index}
            elif dim == 1:
                device = {"fsdp": 2 * index + mine[2]}
            else:
                device = {"fsdp": 2 * mine[1] + index}
            found.append((away - 1, device, index))
        return found


def others(grid, everyone):
    row, column, _ = grid.here()
    found = []
    for down in range(grid.dp):
        for away in range(grid.members):
            if (down or away) and (everyone or not (down and away)):
                found.append({"dp": lax.rem(row + down, grid.dp), "fsdp": lax.rem(column + away, grid.members)})
    return found


def announce(grid, everyone=False):
    barrier = pltpu.get_barrier_semaphore()
    for device in others(grid, everyone):
        pl.semaphore_signal(barrier, inc=1, device_id=device, device_id_type=MESH)


def meet(grid, everyone=False):
    count = grid.dp * grid.members - 1 if everyone else grid.dp + grid.members - 2
    pl.semaphore_wait(pltpu.get_barrier_semaphore(), count)


def remote(source, target, send, recv, device):
    return pltpu.make_async_remote_copy(
        src_ref=source, dst_ref=target, send_sem=send, recv_sem=recv, device_id=device, device_id_type=MESH
    )


def gather_phase(grid, ref, cut, axes, dim, done, send, recv, base):
    _, _, mine = grid.here()
    at = tuple(slice(None) if d in done else mine[d] for d in axes)
    if cut is not None:
        at = at + (slice(None), cut)
    return [
        pltpu.make_async_remote_copy(
            src_ref=ref.at[at], dst_ref=ref.at[at], send_sem=send.at[base + slot], recv_sem=recv.at[base + slot],
            device_id=device, device_id_type=MESH,
        )
        for slot, device, _ in grid.peers(dim)
    ]


def reduce_plan(grid, order):
    plan = []
    for phase, dim in enumerate(order):
        done = order[:phase]
        left = tuple(d for d in range(len(grid.shape)) if d not in done and d != dim)
        plan.append((dim, done, left))
    return plan


def lane_index(width):
    return lax.broadcasted_iota(jnp.int32, (1, width), 1).astype(F32)


def unpack(rows, row, count, width):
    lanes = lane_index(width)
    owner = jnp.floor((lanes + 0.5) * (1.0 / count))
    inner = lanes - count * owner
    taken = lax.broadcasted_iota(jnp.int32, (LANES, width), 0).astype(F32) == inner
    spread_out = dot(rows.astype(BF16), jnp.where(taken, 1.0, 0.0).astype(BF16))
    index = lax.broadcasted_iota(jnp.int32, (rows.shape[0], width), 0).astype(F32)
    return jnp.sum(jnp.where(index == owner * SUB + row, spread_out, 0.0), axis=0, keepdims=True)


def rates_of(real, rotation, step_log):
    timestep = jnp.exp(step_log)
    magnitude = jnp.exp(real * timestep)
    turned = rotation * timestep
    factor_re = magnitude * jnp.cos(turned)
    factor_im = magnitude * jnp.sin(turned)
    modulus = real * real + rotation * rotation
    scale_re = ((factor_re - 1.0) * real + factor_im * rotation) / modulus
    scale_im = (factor_im * real - (factor_re - 1.0) * rotation) / modulus
    return timestep, factor_re, factor_im, modulus, scale_re, scale_im


def encode(values, inverse):
    scaled = values * inverse
    most = jnp.maximum(jnp.max(jnp.abs(scaled), axis=1, keepdims=True), 1e-30)
    power = jnp.broadcast_to(jnp.ceil(jnp.log2(most)), (values.shape[0], LANES))
    steps = jnp.round(scaled * lanes_to(32000.0 * jnp.exp2(-power), values.shape[1]))
    return jnp.concatenate([steps, power], axis=1).astype(jnp.int32).astype(jnp.int16)


def cross_blocks(members, reverse, arrive, pieces, norm, place, own_place, broken, flow_re, flow_im, chosen, dealt, carries):
    states = flow_re.shape[1]
    total = place.shape[1]
    steps = total // members
    blocks = steps
    chunk = chosen.shape[0]
    part = blocks // 2

    def choose(group, at):
        rows = lax.broadcasted_iota(jnp.int32, (chunk, total // 2), 0).astype(F32) + float(at)
        wanted = place[:, group * (total // 2) : (group + 1) * (total // 2)]
        chosen[...] = jnp.where(rows == wanted, 1.0, 0.0).astype(BF16)

    for group in range(2):
        choose(group, 0)
        arrive(group)
        for at in range(0, total, chunk):
            if at:
                choose(group, at)
            moved, power = 0.0, 0.0
            for first in range(0, members, 8):
                held = pieces[first : first + 8, group * part : (group + 1) * part].reshape(8 * part, -1)
                held = held.astype(jnp.int32)
                picked = chosen[:, first * part : (first + 8) * part]
                ints = held[:, : 2 * states]
                high = (ints & -256).astype(F32).astype(BF16)
                low = (ints & 255).astype(F32).astype(BF16)
                moved = moved + (dot(picked, high) + dot(picked, low))
                power = power + dot(picked, held[:, 2 * states :].astype(F32).astype(BF16))
            moved = moved * (lanes_to(jnp.exp2(power) * (1.0 / 32000.0), 2 * states) * norm)
            if group:
                moved = moved + dealt[at : at + chunk, :].astype(F32)
            dealt[at : at + chunk, :] = moved.astype(dealt.dtype)
    rate_re = spread(flow_re, members)
    rate_im = spread(-flow_im if reverse else flow_im, members)
    marks = [broken[s] for s in range(broken.shape[0])]

    def step(i, state):
        re, im = state
        p = steps - 1 - i if reverse else i
        at = pl.multiple_of(p * members, members)
        here = dealt[pl.ds(at, members), :].astype(F32)
        met = marks[0] == p
        for mark in marks[1:]:
            met = met | (mark == p)
        mask = lanes_to(jnp.where(met, 0.0, 1.0), states)
        dealt[pl.ds(at, members), :] = jnp.concatenate([re, im], axis=1).astype(dealt.dtype)
        return (
            mask * (rate_re * re - rate_im * im) + here[:, :states],
            mask * (rate_re * im + rate_im * re) + here[:, states:],
        )

    zero = jnp.zeros((members, states), F32)
    lax.fori_loop(0, steps, step, (zero, zero), unroll=4)
    own = own_place.shape[0]
    step_rows = min(total, 1024)
    found = jnp.zeros((own, 2 * states), F32)
    for at in range(0, total, step_rows):
        columns = lax.broadcasted_iota(jnp.int32, (own, step_rows), 1).astype(F32) + float(at)
        taken = jnp.where(columns == lanes_to(own_place[...], step_rows), 1.0, 0.0).astype(BF16)
        entering = dealt[at : at + step_rows, :].astype(F32)
        high = entering.astype(BF16)
        low = (entering - high.astype(F32)).astype(BF16)
        found = found + (dot(taken, high) + dot(taken, low))
    carries[...] = found


def split(values):
    high = values.astype(BF16)
    rest = values - high.astype(F32)
    middle = rest.astype(BF16)
    return high, middle, (rest - middle.astype(F32)).astype(BF16)


def row_times(row, matrix):
    wide = [jnp.broadcast_to(piece.astype(F32), (SUB, row.shape[1])).astype(BF16) for piece in split(row)]
    return sum(contract_cols(piece, matrix) for piece in wide)[0:1]


def row_sums(matrix):
    ones = jnp.ones((SUB, matrix.shape[1]), BF16)
    return sum(contract_cols(ones, piece) for piece in split(matrix))[0:1]


def layer_kernel(
    grid, block_rows, counts, tile, orders, tokens, cotangent, gain_s, shift_s, through_s, bias_s, real_s, rotation_s,
    step_s, target_s, lengths_s, drive_s, readout_s, mixer_s, perm,
    gated_low, token_part, drive_sum, readout_sum, weight_sum, vector_sum, rates,
    rows_in, normed, mixed_all, big, joined_all, table, drive_w, readout_w, mixer_w, drive, readout, mixer,
    vectors, place, own_place, broken, bits, carry, coming, pieces_ends, pieces, chosen, dealt_x, weight_grad,
    bias_grad, through_grad, readout_grad, mixed_sum, drive_grad, decay_cot, driven_sum, send_w, recv_w, local,
    ends_send, ends_recv, table_send, table_recv, push_send, push_recv, *rest,
):
    i = pl.program_id(0)
    tiles = (pl.num_programs(0) - 2) // 3
    row, column, mine = grid.here()
    members = grid.members
    core = 2
    phases = 3
    span = SUB * block_rows
    width = rows_in.shape[1]
    both = joined_all.shape[1]
    states = both // 2
    blocks = target_s.shape[0]
    chains = tile // span
    tile_blocks = tile // block_rows
    axes = (0, 1, 2)
    half = mixer_w.shape[-1] // 2
    wholes = (drive_w, readout_w, mixer_w, mixer_w)
    cuts = (None, None, pl.ds(0, half), pl.ds(half, half))
    ways = ((0, 1, 2), (1, 0, 2), (1, 0, 2), (0, 1, 2))

    def phase_copies(k, phase):
        order = ways[k]
        base = k * grid.slots + sum(grid.fan(d) for d in order[:phase])
        return gather_phase(grid, wholes[k], cuts[k], axes, order[phase], order[:phase], send_w, recv_w, base)

    def table_copies():
        return [
            remote(table.at[mine], table.at[mine], table_send.at[k], table_recv.at[k], device)
            for k, device in enumerate(others(grid, True))
        ]

    def gather_on(ks, phase):
        for k in ks:
            if phase:
                for copy in phase_copies(k, phase - 1):
                    copy.wait()
            if phase < phases:
                for copy in phase_copies(k, phase):
                    copy.start()

    def push_far(at, group):
        return [
            remote(pieces_ends.at[at], pieces_ends.at[at], ends_send.at[group, slot], ends_recv.at[group, slot], device)
            for slot, device, _ in grid.peers(1)
        ]

    def push_near(at, group, slot):
        device = grid.peers(2)[0][1]
        return remote(
            pieces_ends.at[at], pieces_ends.at[at], ends_send.at[group, slot], ends_recv.at[group, slot], device
        )

    def group_rows(group):
        return pl.ds(group * (blocks // 2), blocks // 2)

    far = grid.fan(1)

    def tile_at(j):
        return pl.ds(pl.multiple_of(j * tile, tile), tile)

    def mask_of(marks, c, t):
        single = 1 << t if t < 31 else -(1 << 31)
        return lanes_to(jnp.where((marks[c * SUB : (c + 1) * SUB] & single) == 0, 1.0, 0.0), states)

    def marks_of(j):
        return bits[pl.ds(pl.multiple_of(j * tile_blocks, tile_blocks), tile_blocks), :]

    def of_blocks(ref, j):
        return ref[pl.ds(pl.multiple_of(j * tile_blocks, tile_blocks), tile_blocks), :]

    def note_norm(k, squares):
        norm = jnp.sqrt(squares[:, :states] + squares[:, states:])
        norm = jnp.maximum(jnp.concatenate([norm, norm], axis=1), 1e-20)
        vectors[k : k + 1, :both] = norm
        vectors[k + 1 : k + 2, :both] = 1.0 / norm

    def flatten(source, target):
        size = source.shape[-2]
        for k, where in enumerate(itertools.product(*[range(n) for n in grid.shape])):
            target[k * size : (k + 1) * size, :] = source[where]

    rest = list(rest)
    parts = (readout_grad, weight_grad, drive_grad)
    outs = (readout_sum, weight_sum, drive_sum)
    count = len(parts)
    aligned = [out.shape[0] % SUB == 0 for out in outs]
    accs = [None if whole_rows else rest.pop(0) for whole_rows in aligned]
    stages = [[rest.pop(0) for _ in range(phases)] for _ in range(count)]
    landed = [[rest.pop(0) for _ in range(phases)] for _ in range(count)]
    vector_stage, across, along, send, recv, vector_send, vector_recv = rest
    plans = [reduce_plan(grid, order) for order in orders]
    every = (0, 1, 2)
    kept = every[:-1]
    first_a = tiles + 1
    first_b = 2 * tiles + 1

    def push_to(at, group):
        return [
            remote(
                pieces.at[at], pieces.at[at], push_send.at[group, away - 1], push_recv.at[group, away - 1],
                {"fsdp": lax.rem(column + away, members)},
            )
            for away in range(1, members)
        ]

    def combos(left):
        return list(itertools.product(*[range(grid.shape[d]) for d in left]))

    def at_of(dim, index, left, combo, dims):
        chosen_of = dict(zip(left, combo))
        chosen_of[dim] = index
        return tuple(chosen_of[d] if d in chosen_of else mine[d] for d in dims)

    def rows_of(k, where):
        size = outs[k].shape[0]
        down, half_of, low = where
        return pl.ds(pl.multiple_of(((down * grid.shape[1] + half_of) * 2 + low) * size, size), size)

    def keep_piece(k, dim, left, combo, piece):
        if aligned[k]:
            parts[k][rows_of(k, at_of(dim, mine[dim], left, combo, every)), :] = piece
        else:
            accs[k][at_of(dim, mine[dim], left, combo, kept)] = piece

    def piece_of(k, dim, index, left, combo):
        if aligned[k]:
            return parts[k][rows_of(k, at_of(dim, index, left, combo, every)), :]
        if dim != core:
            return accs[k][at_of(dim, index, left, combo, kept)]
        size = outs[k].shape[0]
        down, half, low = at_of(dim, index, left, combo, every)
        start = ((down * grid.shape[1] + half) * 2 + low) * size
        low_row = jnp.minimum(lax.div(start, SUB) * SUB, parts[k].shape[0] - 2 * SUB)
        window = parts[k][pl.ds(pl.multiple_of(low_row, SUB), 2 * SUB), :]
        return pltpu.roll(window, lax.rem(2 * SUB - (start - low_row), 2 * SUB), 0)[:size]

    def hops(k, phase):
        dim = plans[k][phase][0]
        base = k * grid.slots + sum(grid.fan(d) for d in orders[k][:phase])
        return [
            (
                remote(
                    stages[k][phase].at[slot], landed[k][phase].at[slot], send.at[base + slot], recv.at[base + slot],
                    device,
                ),
                slot,
                index,
            )
            for slot, device, index in grid.peers(dim)
        ]

    def begin(k, phase):
        dim, _, left = plans[k][phase]
        for copy, slot, index in hops(k, phase):
            for combo in combos(left):
                stages[k][phase][(slot,) + combo] = piece_of(k, dim, index, left, combo).astype(BF16)
            copy.start()

    def finish(k, phase):
        dim, _, left = plans[k][phase]
        copies = hops(k, phase)
        for copy, _, _ in copies:
            copy.wait()
        for combo in combos(left):
            piece = piece_of(k, dim, mine[dim], left, combo)
            for _, slot, _ in copies:
                piece = piece + landed[k][phase][(slot,) + combo].astype(F32)
            keep_piece(k, dim, left, combo, piece)

    def advance(ks, phase):
        for k in ks:
            if phase:
                finish(k, phase - 1)
            if phase < phases:
                begin(k, phase)
            else:
                outs[k][...] = parts[k][rows_of(k, mine), :] if aligned[k] else accs[k][mine[:-1]]

    def vector_across():
        return [
            remote(
                vector_stage, across.at[away - 1], vector_send.at[away - 1], vector_recv.at[away - 1],
                {"fsdp": lax.rem(column + away, members)},
            )
            for away in range(1, members)
        ]

    def vector_along():
        return [
            remote(
                vector_sum, along.at[slot], vector_send.at[members - 1 + slot], vector_recv.at[members - 1 + slot], device
            )
            for slot, device, _ in grid.peers(0)
        ]

    @pl.when(i == 0)
    def _():
        copies = [
            pltpu.make_async_copy(shard, ref.at[tuple(mine)], local.at[k])
            for k, (shard, ref) in enumerate(zip((drive_s, readout_s, mixer_s), wholes))
        ]
        for copy in copies:
            copy.start()
        held = [gain_s, shift_s, through_s, bias_s, real_s, rotation_s, step_s, target_s]
        own = table.at[tuple(mine)]
        own[...] = jnp.zeros_like(own)
        for k, ref in enumerate(held):
            own[k : k + 1, : ref.shape[0]] = ref[...].astype(F32).reshape(1, ref.shape[0])
        sequences = lengths_s.shape[1]
        own[4:5, LANES // 2 : LANES // 2 + sequences] = lengths_s[...].astype(F32)
        announce(grid, True)
        taps = [
            pltpu.make_async_copy(
                cotangent.at[pl.ds(j * tile, tile)], mixed_all.at[pl.ds(j * tile, tile)],
                local.at[len(copies) + tiles + j],
            )
            for j in range(tiles)
        ]
        chunks = [
            pltpu.make_async_copy(
                tokens.at[pl.ds(j * tile, tile)], rows_in.at[pl.ds(j * tile, tile)], local.at[len(copies) + j]
            )
            for j in range(tiles)
        ]
        for copy in chunks + taps:
            copy.start()
        for copy in copies:
            copy.wait()
        meet(grid, True)
        gather_on((0,), 0)
        for copy in table_copies():
            copy.start()
        gather_on((1, 2), 0)

        def turn(ref):
            def one(j, _):
                ref[tile_at(j), :] = permute_tile(perm[...], ref[tile_at(j), :], span).astype(BF16)
                return 0

            return one

        for copy in chunks[: tiles // 2]:
            copy.wait()
        lax.fori_loop(0, tiles // 2, turn(rows_in), 0)
        gather_on((0,), 1)
        gather_on((3,), 0)
        gather_on((1, 2), 1)
        for copy in chunks[tiles // 2 :]:
            copy.wait()
        lax.fori_loop(tiles // 2, tiles, turn(rows_in), 0)
        for total in (
            weight_grad, bias_grad, through_grad, readout_grad, mixed_sum, drive_grad, decay_cot, driven_sum
        ):
            total[...] = jnp.zeros_like(total)
        for copy in table_copies():
            copy.wait()
        rows = table[...].reshape(-1, LANES)
        vectors[...] = jnp.zeros_like(vectors)
        for k, size in enumerate((width, width, width, 2 * width)):
            vectors[k : k + 1, :size] = unpack(rows, k, counts[k], size)
        real, rotation, step_log = [unpack(rows, k, counts[k], states) for k in (4, 5, 6)]
        _, factor_re, factor_im, _, scale_re, scale_im = rates_of(real, rotation, step_log)
        flow_re, flow_im = factor_re, factor_im
        power = 1
        while power < block_rows:
            flow_re, flow_im = flow_re * flow_re - flow_im * flow_im, 2.0 * flow_re * flow_im
            power *= 2
        for k, value in enumerate((factor_re, factor_im, flow_re, flow_im, real, rotation, step_log)):
            rates[k : k + 1, :] = value
        group = table[row].reshape(members * SUB, LANES)
        for m in range(members):
            q = group[m * SUB + 7 : m * SUB + 8, :blocks]
            d = jnp.floor(q * (1.0 / blocks))
            q = (q - d * blocks) * members + d
            for side in range(2):
                start = (side * members + m) * (blocks // 2)
                place[:, start : start + blocks // 2] = q[:, side * (blocks // 2) : (side + 1) * (blocks // 2)]
        lengths = jnp.concatenate([group[m * SUB + 4 : m * SUB + 5, :] for m in range(members)], axis=0)
        sequences = lengths_s.shape[1]
        q = table[tuple(mine) + (slice(7, 8), slice(None))]
        diagonal = lax.broadcasted_iota(jnp.int32, (blocks, LANES), 0) == lax.broadcasted_iota(
            jnp.int32, (blocks, LANES), 1
        )
        q = jnp.sum(jnp.where(diagonal, jnp.broadcast_to(q, (blocks, LANES)), 0.0), axis=1, keepdims=True)
        q = jnp.broadcast_to(q, (blocks, LANES))
        d = jnp.floor(q * (1.0 / blocks))
        p = q - d * blocks
        own_place[...] = p * members + d
        start = jnp.zeros((members, LANES), F32)
        marks = jnp.zeros((blocks, LANES), jnp.int32)
        for s in range(sequences):
            broken[s] = jnp.floor(start * (1.0 / block_rows)).astype(jnp.int32)
            mark = jnp.zeros((blocks, LANES), F32)
            for m in range(members):
                mark = jnp.where(d == float(m), jnp.broadcast_to(start[m : m + 1, :], (blocks, LANES)), mark)
            mark = mark - p * block_rows
            inside = (mark >= 0.0) & (mark < block_rows)
            shift = jnp.where(inside, mark, 0.0).astype(jnp.int32)
            marks = marks | jnp.where(inside, lax.shift_left(jnp.ones_like(shift), shift), 0)
            column_of = lengths[:, LANES // 2 + s : LANES // 2 + s + 1]
            start = start + jnp.broadcast_to(column_of, (members, LANES))
        bits[...] = marks
        gain = vectors[0:1, :width]
        shift_by = vectors[1:2, :width]

        def settle(j, _):
            moved, rstd = norm_stats(rows_in[tile_at(j), :].astype(F32))
            normed[tile_at(j), :] = (moved * rstd * gain + shift_by).astype(BF16)
            return 0

        lax.fori_loop(0, tiles // 2, settle, 0)
        gather_on((0,), 2)
        lax.fori_loop(tiles // 2, tiles, settle, 0)
        gather_on((0,), 3)
        gather_on((3,), 1)
        raw = drive_w[...].reshape(width, both).astype(F32)
        drive[:, :states] = (scale_re * raw[:, :states] - scale_im * raw[:, states:]).astype(BF16)
        drive[:, states:] = (scale_re * raw[:, states:] + scale_im * raw[:, :states]).astype(BF16)
        note_norm(4, jnp.sum(jnp.square(drive[...].astype(F32)), axis=0, keepdims=True))
        rate_re = spread(rates[0:1, :], SUB)
        rate_im = spread(rates[1:2, :], SUB)

        def begin_tile(j, _):
            driven = big.at[tile_at(j)]
            driven[...] = dot(normed[tile_at(j), :], drive[...]).astype(big.dtype)
            marks = marks_of(j)
            state = [(jnp.zeros((SUB, states), F32), jnp.zeros((SUB, states), F32)) for _ in range(chains)]
            for t in range(block_rows):
                for c in range(chains):
                    at = c * span + t * SUB
                    mask = mask_of(marks, c, t)
                    re, im = state[c]
                    now_re = mask * (rate_re * re - rate_im * im) + driven[at : at + SUB, :states].astype(F32)
                    now_im = mask * (rate_re * im + rate_im * re) + driven[at : at + SUB, states:].astype(F32)
                    state[c] = (now_re, now_im)
            ends = jnp.concatenate([jnp.concatenate(state[c], axis=1) for c in range(chains)], axis=0)
            at = (column, pl.ds(pl.multiple_of(j * tile_blocks, tile_blocks), tile_blocks))
            pieces_ends[at + (slice(None),)] = encode(ends, vectors[5:6, :both])
            group = lax.div(j, tiles // 2)
            for copy in push_far(at, group) + [push_near(at, group, far)]:
                copy.start()
            return 0

        lax.fori_loop(0, tiles, begin_tile, 0)
        for copy in taps:
            copy.wait()
        lax.fori_loop(0, tiles, turn(mixed_all), 0)
        gather_on((1, 2, 3), 2)
        gather_on((1, 2, 3), 3)
        flatten(readout_w, readout)
        flatten(mixer_w, mixer)
        note_norm(6, row_sums(jnp.square(readout[...].astype(F32))))

        def arrive(group):
            onward = []
            for k, copy in enumerate(push_far((column, group_rows(group)), group)):
                copy.wait()
                there = 2 * lax.rem(mine[1] + grid.shape[1] - 1 - k, grid.shape[1]) + mine[2]
                onward.append(push_near((there, group_rows(group)), group, far + 1 + k))
                onward[-1].start()
            push_near((column, group_rows(group)), group, far).wait()
            for copy in onward:
                copy.wait()

        cross_blocks(
            members, False, arrive, pieces_ends, vectors[4:5, :both], place, own_place, broken, rates[2:3, :], rates[3:4, :], chosen, dealt_x,
            carry,
        )

    rate_re = spread(rates[0:1, :], SUB)
    rate_im = spread(rates[1:2, :], SUB)

    @pl.when(i < tiles)
    def _():
        through = vectors[2:3, :width]
        bias = vectors[3:4, : 2 * width]
        here = tile_at(i)
        joined = joined_all.at[here]
        driven = big.at[here]
        joined_grad = big.at[here]
        marks = marks_of(i)
        entering = of_blocks(carry, i)
        state = [
            (entering[c * SUB : (c + 1) * SUB, :states], entering[c * SUB : (c + 1) * SUB, states:])
            for c in range(chains)
        ]
        for t in range(0, block_rows, 2):
            for c in range(chains):
                held = []
                for step in (t, t + 1):
                    at = c * span + step * SUB
                    mask = mask_of(marks, c, step)
                    re, im = state[c]
                    now_re = mask * (rate_re * re - rate_im * im) + driven[at : at + SUB, :states].astype(F32)
                    now_im = mask * (rate_re * im + rate_im * re) + driven[at : at + SUB, states:].astype(F32)
                    state[c] = (now_re, now_im)
                    held.append(state[c])
                at = c * span + t * SUB
                joined[at : at + 2 * SUB, :states] = jnp.concatenate([held[0][0], held[1][0]], axis=0).astype(BF16)
                joined[at : at + 2 * SUB, states:] = (-jnp.concatenate([held[0][1], held[1][1]], axis=0)).astype(BF16)

        dealt_f32 = normed[here, :].astype(F32)
        mixed = dot(joined[...], readout[...]) + through * dealt_f32
        activated, slope = gelu_parts(mixed)
        features = activated.astype(BF16)
        hidden = dot(features, mixer[...]) + bias
        value = hidden[:, :width]
        sig = 0.5 + 0.5 * jnp.tanh(0.5 * hidden[:, width:])
        gated_low[...] = (value * sig).astype(BF16)
        cot_sig = mixed_all[here, :].astype(F32) * sig
        hidden_low = jnp.concatenate(
            [cot_sig.astype(BF16), (cot_sig * value * (1.0 - sig)).astype(BF16)], axis=1
        )
        weight_grad[...] += contract_rows(features, hidden_low)
        bias_grad[...] += jnp.sum(hidden_low.astype(F32), axis=0, keepdims=True)
        feature_grad = contract_cols(hidden_low, mixer[...]).astype(BF16)
        mixed_grad = (feature_grad.astype(F32) * slope).astype(BF16)
        mixed_all[here, :] = mixed_grad
        mixed_f32 = mixed_grad.astype(F32)
        through_grad[...] += jnp.sum(mixed_f32 * dealt_f32, axis=0, keepdims=True)
        mixed_sum[...] += jnp.sum(mixed_f32, axis=0, keepdims=True)
        readout_grad[...] += contract_rows(joined[...], mixed_grad)
        joined_grad[...] = contract_cols(mixed_grad, readout[...]).astype(big.dtype)

        going = [(jnp.zeros((SUB, states), F32), jnp.zeros((SUB, states), F32)) for _ in range(chains)]
        for t in reversed(range(block_rows)):
            for c in range(chains):
                at = c * span + t * SUB
                mask = mask_of(marks, c, t)
                re = joined_grad[at : at + SUB, :states].astype(F32) + going[c][0]
                im = going[c][1] - joined_grad[at : at + SUB, states:].astype(F32)
                going[c] = (mask * (rate_re * re + rate_im * im), mask * (rate_re * im - rate_im * re))
        heads = jnp.concatenate([jnp.concatenate(going[c], axis=1) for c in range(chains)], axis=0)
        at = (column, pl.ds(pl.multiple_of(i * tile_blocks, tile_blocks), tile_blocks))
        pieces[at + (slice(None),)] = encode(heads, vectors[7:8, :both])

        for copy in push_to(at, lax.div(i, tiles // 2)):
            copy.start()

    @pl.when(i == tiles)
    def _():
        def arrive(group):
            advance((0, 1), group)
            for copy in push_to((column, group_rows(group)), group):
                copy.wait()

        cross_blocks(
            members, True, arrive, pieces, vectors[6:7, :both], place, own_place, broken, rates[2:3, :], rates[3:4, :], chosen, dealt_x,
            coming,
        )

    @pl.when(i == first_b - 1)
    def _():
        advance((1,), 2)

    @pl.when((i >= first_a) & (i < first_b))
    def _():
        j = first_b - 1 - i
        here = tile_at(j)
        joined = joined_all.at[here]
        driven_low = joined
        joined_grad = big.at[here]
        marks = marks_of(j)
        entering = of_blocks(coming, j)
        before = of_blocks(carry, j)
        going = [
            (entering[c * SUB : (c + 1) * SUB, :states], entering[c * SUB : (c + 1) * SUB, states:])
            for c in range(chains)
        ]
        total = [(jnp.zeros((SUB, states), F32), jnp.zeros((SUB, states), F32)) for _ in range(chains)]
        sums = list(total)
        for t in reversed(range(0, block_rows, 2)):
            for c in range(chains):
                pair = c * span + t * SUB
                here_re = joined[pair : pair + SUB, :states].astype(F32)
                here_im = -joined[pair : pair + SUB, states:].astype(F32)
                if t == 0:
                    past_re = before[c * SUB : (c + 1) * SUB, :states]
                    past_im = before[c * SUB : (c + 1) * SUB, states:]
                else:
                    past_re = joined[pair - SUB : pair, :states].astype(F32)
                    past_im = -joined[pair - SUB : pair, states:].astype(F32)
                held = {}
                for step, (prev_re, prev_im) in ((t + 1, (here_re, here_im)), (t, (past_re, past_im))):
                    where = c * span + step * SUB
                    mask = mask_of(marks, c, step)
                    re = joined_grad[where : where + SUB, :states].astype(F32) + going[c][0]
                    im = going[c][1] - joined_grad[where : where + SUB, states:].astype(F32)
                    held[step] = (re, im)
                    sums[c] = (sums[c][0] + re, sums[c][1] + im)
                    on_re = mask * (rate_re * re + rate_im * im)
                    on_im = mask * (rate_re * im - rate_im * re)
                    going[c] = (on_re, on_im)
                    total[c] = (
                        total[c][0] + (on_re * prev_re + on_im * prev_im),
                        total[c][1] + (on_im * prev_re - on_re * prev_im),
                    )
                driven_low[pair : pair + 2 * SUB, :states] = jnp.concatenate(
                    [held[t][0], held[t + 1][0]], axis=0
                ).astype(BF16)
                driven_low[pair : pair + 2 * SUB, states:] = jnp.concatenate(
                    [held[t][1], held[t + 1][1]], axis=0
                ).astype(BF16)
        for c in range(chains):
            decay_cot[...] += jnp.concatenate(total[c], axis=1)
            driven_sum[...] += jnp.concatenate(sums[c], axis=1)
        drive_grad[...] += contract_rows(normed[here, :], driven_low[...])

    @pl.when(i == first_b)
    def _():
        advance((2,), 0)
        cot = jnp.sum(decay_cot[...], axis=0, keepdims=True)
        factor_re, factor_im = rates[0:1, :], rates[1:2, :]
        size = factor_re * factor_re + factor_im * factor_im
        vector_stage[...] = jnp.zeros_like(vector_stage)
        through = vectors[2:3, :width]
        summed = jnp.sum(driven_sum[...], axis=0, keepdims=True)
        shift_sum = through * mixed_sum[...] + row_times(summed, drive[...])
        crossed = row_sums(drive[...].astype(F32) * drive_grad[...]) + through * through_grad[...]
        vector_stage[0:1, :width] = (crossed - vectors[1:2, :width] * shift_sum) / vectors[0:1, :width]
        vector_stage[1:2, :width] = shift_sum
        vector_stage[2:3, :width] = through_grad[...]
        vector_stage[3:4, :] = bias_grad[:, :both]
        vector_stage[4:5, : 2 * width - both] = bias_grad[:, both:]
        vector_stage[5:6, :states] = (cot[:, :states] * factor_re - cot[:, states:] * factor_im) / size
        vector_stage[5:6, states:] = (cot[:, :states] * factor_im + cot[:, states:] * factor_re) / size
        d_re, d_im = drive_grad[:, :states], drive_grad[:, states:]
        raw = drive_w[...].reshape(width, both).astype(F32)
        b_re, b_im = raw[:, :states], raw[:, states:]
        vector_stage[6:7, :states] = jnp.sum(d_re * b_re + d_im * b_im, axis=0, keepdims=True)
        vector_stage[6:7, states:] = jnp.sum(d_im * b_re - d_re * b_im, axis=0, keepdims=True)

        for copy in vector_across():
            copy.start()

    @pl.when(i == first_b + 1)
    def _():
        advance((2,), 1)

    @pl.when(i == first_b + 2)
    def _():
        advance((0,), 2)

    @pl.when(i == first_b + 3)
    def _():
        for copy in vector_across():
            copy.wait()
        total = vector_stage[...]
        for k in range(members - 1):
            total = total + across[k]
        vector_sum[...] = total
        for copy in vector_along():
            copy.start()

    @pl.when(i == first_b + tiles - 2)
    def _():
        advance((2,), 2)

    @pl.when(i == first_b + tiles)
    def _():
        for copy in vector_along():
            copy.wait()
        total = vector_sum[...]
        for k in range(grid.dp - 1):
            total = total + along[k]
        vector_sum[...] = total
        advance((0, 1, 2), 3)

    @pl.when((i >= first_b) & (i < first_b + tiles))
    def _():
        j = i - first_b
        here = tile_at(j)
        driven_low = joined_all[here, :]
        normed_grad = vectors[2:3, :width] * mixed_all[here, :].astype(F32) + contract_cols(driven_low, drive[...])
        given = normed_grad.astype(BF16).astype(F32)
        moved, rstd = norm_stats(rows_in[here, :].astype(F32))
        xhat = moved * rstd
        scaled = given * vectors[0:1, :width]
        inner = jnp.mean(scaled * xhat, axis=-1, keepdims=True)
        token_part[...] = (
            rstd * (scaled - jnp.mean(scaled, axis=-1, keepdims=True) - xhat * inner)
        ).astype(BF16)


def tail_kernel(
    grid, span, tokens, cotangent, token_part, gated_low, back, rates, drive_sum, readout_sum, weight_sum, vector_sum,
    out, token_grad, gain_grad, shift_grad, real_grad, rotation_grad, timestep_grad, drive_grad, readout_grad,
    through_grad, weight_grad, bias_grad,
):
    width = tokens.shape[1]
    both = vector_sum.shape[1]
    states = both // 2
    out[...] = tokens[...].astype(F32) + permute_tile(back[...], gated_low[...], span)
    token_grad[...] = cotangent[...].astype(F32) + permute_tile(back[...], token_part[...], span)

    @pl.when(pl.program_id(0) == 0)
    def _():
        row, column, _ = grid.here()
        me = row * grid.members + column
        real, rotation, step_log = [rates[k : k + 1, :] for k in (4, 5, 6)]
        timestep, factor_re, factor_im, modulus, scale_re, scale_im = rates_of(real, rotation, step_log)
        d_re, d_im = drive_sum[:, :states], drive_sum[:, states:]
        drive_grad[:, :states] = scale_re * d_re + scale_im * d_im
        drive_grad[:, states:] = scale_re * d_im - scale_im * d_re
        readout_grad[...] = readout_sum[...]
        weight_grad[...] = weight_sum[...]
        s_re, s_im = vector_sum[6:7, :states], vector_sum[6:7, states:]
        total_re = vector_sum[5:6, :states] + (s_re * real - s_im * rotation) / modulus
        total_im = vector_sum[5:6, states:] + (s_re * rotation + s_im * real) / modulus
        ratio_re = (scale_re * real + scale_im * rotation) / modulus
        ratio_im = (scale_im * real - scale_re * rotation) / modulus
        lambda_re = timestep * (total_re * factor_re + total_im * factor_im) - (s_re * ratio_re + s_im * ratio_im)
        lambda_im = timestep * (total_im * factor_re - total_re * factor_im) - (s_im * ratio_re - s_re * ratio_im)
        turn_re = real * factor_re - rotation * factor_im
        turn_im = real * factor_im + rotation * factor_re
        step_grad = timestep * (total_re * turn_re + total_im * turn_im)

        def own(vector, target):
            length, size = vector.shape[1], target.shape[0]
            wide = jnp.broadcast_to(vector, (SUB, length))
            rolled = pltpu.roll(wide, lax.rem(length - me * size, length), 1)
            target[...] = rolled[0:1, :size].reshape(size)

        own(vector_sum[0:1, :width], gain_grad)
        own(vector_sum[1:2, :width], shift_grad)
        own(vector_sum[2:3, :width], through_grad)
        own(jnp.concatenate([vector_sum[3:4, :], vector_sum[4:5, : 2 * width - both]], axis=1), bias_grad)
        own(lambda_re, real_grad)
        own(lambda_im, rotation_grad)
        own(step_grad, timestep_grad)


def whole(shape):
    return pl.BlockSpec(shape, lambda i: (0,) * len(shape), pipeline_mode=pl.Buffered(1))


def total_of(shape):
    return pl.BlockSpec(shape, lambda i: (0,) * len(shape))


def tiled(rows, columns):
    return pl.BlockSpec((rows, columns), lambda i: (i, 0))


def params(cid=None):
    if cid is None:
        return pltpu.CompilerParams(dimension_semantics=("arbitrary",), vmem_limit_bytes=VMEM_LIMIT)
    return pltpu.CompilerParams(
        dimension_semantics=("arbitrary",), vmem_limit_bytes=VMEM_LIMIT, collective_id=cid, has_side_effects=True
    )


def body(
    tokens, cotangent, block_target, sequence_lengths, norm_gain, norm_shift, decay_real, decay_rotation,
    log_timestep, drive_matrix, readout_matrix, feedthrough, mixer_weight, mixer_bias,
):
    members = lax.axis_size("fsdp")
    grid = Grid(lax.axis_size("dp"), members)
    blocks = block_target.shape[0]
    rows, width = tokens.shape
    both = drive_matrix.shape[1]
    states = both // 2
    block_rows = rows // blocks
    span = SUB * block_rows
    tile = 2 * span if members <= SUB else span
    tiles = rows // tile
    tile_blocks = tile // block_rows
    total = blocks * members
    chunk = min(total, 2**40 // total**3)
    sequences = sequence_lengths.shape[1]
    shape = jax.ShapeDtypeStruct
    anywhere = pl.BlockSpec(memory_space=pl.ANY)
    regular = pltpu.SemaphoreType.DMA

    order = np.arange(span)
    source = (order % SUB) * block_rows + order // SUB
    perm = jnp.asarray(source[:, None] == order[None], BF16)
    back = jnp.asarray(order[:, None] == source[None], BF16)

    def flat(size):
        return pl.BlockSpec((size,), lambda i: (0,))

    small = (norm_gain, norm_shift, feedthrough, mixer_bias, decay_real, decay_rotation, log_timestep, block_target)
    counts = tuple(v.shape[0] for v in small)
    shards = (drive_matrix, readout_matrix, mixer_weight)
    slots = grid.slots
    kept_type = F32 if members <= SUB else BF16

    def first(rows_of, columns):
        return pl.BlockSpec((rows_of, columns), lambda i: (jnp.minimum(i, tiles - 1), 0))

    def final(rows_of, columns):
        return pl.BlockSpec((rows_of, columns), lambda i: (jnp.clip(i - 2 * tiles - 1, 0, tiles - 1), 0))

    orders = ((2, 0, 1), (2, 1, 0), (2, 1, 0))
    weights = (readout_matrix, mixer_weight, drive_matrix)
    buffers = []
    for turn, weight in zip(orders, weights):
        for dim, _, left in reduce_plan(grid, turn):
            buffers.append(pltpu.VMEM((grid.fan(dim),) + tuple(grid.shape[d] for d in left) + weight.shape, BF16))
    gated_low, token_part, drive_sum, readout_sum, weight_sum, vector_sum, rates = pl.pallas_call(
        functools.partial(layer_kernel, grid, block_rows, counts, tile, orders),
        grid=(3 * tiles + 2,),
        in_specs=[anywhere, anywhere]
        + [flat(size) for size in counts]
        + [whole((1, sequences)), anywhere, anywhere, anywhere, whole((span, span))],
        out_specs=[
            first(tile, width), final(tile, width), total_of(drive_matrix.shape), total_of(readout_matrix.shape),
            total_of(mixer_weight.shape), total_of((SUB, both)), total_of((SUB, states)),
        ],
        out_shape=[
            shape((rows, width), BF16), shape((rows, width), BF16), shape(drive_matrix.shape, F32),
            shape(readout_matrix.shape, F32), shape(mixer_weight.shape, F32), shape((SUB, both), F32),
            shape((SUB, states), F32),
        ],
        scratch_shapes=[
            pltpu.VMEM((rows, width), BF16), pltpu.VMEM((rows, width), BF16), pltpu.VMEM((rows, width), BF16),
            pltpu.VMEM((rows, both), kept_type), pltpu.VMEM((rows, both), BF16),
            pltpu.VMEM(grid.shape + (SUB, LANES), F32),
        ]
        + [pltpu.VMEM(grid.shape + shard.shape, BF16) for shard in shards]
        + [
            pltpu.VMEM((width, both), BF16), pltpu.VMEM((both, width), BF16),
            pltpu.VMEM((width, 2 * width), BF16), pltpu.VMEM((SUB, 2 * width), F32), pltpu.VMEM((1, total), F32),
            pltpu.VMEM((blocks, LANES), F32), pltpu.VMEM((sequences, members, LANES), jnp.int32),
            pltpu.VMEM((blocks, LANES), jnp.int32), pltpu.VMEM((blocks, both), F32), pltpu.VMEM((blocks, both), F32),
            pltpu.VMEM((members, blocks, both + LANES), jnp.int16),
            pltpu.VMEM((members, blocks, both + LANES), jnp.int16),
            pltpu.VMEM((chunk, total // 2), BF16), pltpu.VMEM((total, both), kept_type),
            pltpu.VMEM((width, 2 * width), F32), pltpu.VMEM((1, 2 * width), F32), pltpu.VMEM((1, width), F32),
            pltpu.VMEM((both, width), F32), pltpu.VMEM((1, width), F32), pltpu.VMEM((width, both), F32),
            pltpu.VMEM((SUB, both), F32), pltpu.VMEM((SUB, both), F32),
            regular((4 * slots,)), regular((4 * slots,)), regular((len(shards) + 2 * tiles,)), regular((2, members)),
            regular((2, members)), regular((grid.dp * members - 1,)), regular((grid.dp * members - 1,)),
            regular((2, members - 1)), regular((2, members - 1)),
        ]
        + [pltpu.VMEM(grid.shape[:-1] + weight.shape, F32) for weight in weights if weight.shape[0] % SUB]
        + buffers
        + buffers
        + [
            pltpu.VMEM((SUB, both), F32), pltpu.VMEM((members - 1, SUB, both), F32),
            pltpu.VMEM((grid.dp - 1, SUB, both), F32), regular((3 * slots,)), regular((3 * slots,)),
            regular((members + grid.dp - 2,)), regular((members + grid.dp - 2,)),
        ],
        compiler_params=params(0),
        name="layer",
    )(tokens, cotangent, *small, sequence_lengths, *shards, perm)

    vector_sizes = [v.shape[0] for v in (norm_gain, norm_shift, decay_real, decay_rotation, log_timestep)]
    slab = 4 * tile
    outs = pl.pallas_call(
        functools.partial(tail_kernel, grid, span),
        grid=(rows // slab,),
        in_specs=[tiled(slab, width)] * 4
        + [
            whole((span, span)), whole((SUB, states)), whole(drive_matrix.shape), whole(readout_matrix.shape),
            whole(mixer_weight.shape), whole((SUB, both)),
        ],
        out_specs=[tiled(slab, width)] * 2
        + [flat(size) for size in vector_sizes]
        + [
            total_of(drive_matrix.shape), total_of(readout_matrix.shape), flat(feedthrough.shape[0]),
            total_of(mixer_weight.shape), flat(mixer_bias.shape[0]),
        ],
        out_shape=[shape((rows, width), F32)] * 2
        + [shape((size,), F32) for size in vector_sizes]
        + [
            shape(drive_matrix.shape, F32), shape(readout_matrix.shape, F32), shape(feedthrough.shape, F32),
            shape(mixer_weight.shape, F32), shape(mixer_bias.shape, F32),
        ],
        compiler_params=params(),
        name="tail",
    )(tokens, cotangent, token_part, gated_low, back, rates, drive_sum, readout_sum, weight_sum, vector_sum)
    return tuple(outs)


def solution(mesh):
    rows = P(AXES, None)
    flat = P(AXES)
    return jax.shard_map(
        body,
        mesh=mesh,
        in_specs=(rows, rows, flat, rows, flat, flat, flat, flat, flat, rows, rows, flat, rows, flat),
        out_specs=(rows, rows, flat, flat, flat, flat, flat, rows, rows, flat, rows, flat),
        check_vma=False,
    )
```
